32 devices in a mesh: dp: 4 (over y, core), expert: 8 (over z, x).
Axes of the slice: x: 2, y: 2, z: 4, core: 2. Of those that a mesh axis runs over, the one named last changes fastest.
Arguments:
- tokens: bfloat16 [8192, 2048], P(('dp', 'expert')), may hold values from -6 to 6
- grad_out: bfloat16 [8192, 2048], P(('dp', 'expert')), may hold values from -6 to 6
- routes: int32 [8192, 3], P(('dp', 'expert')), may hold values from 0 to 7, all different within a row; in each aligned block of 256 rows (0 to 255, 256 to 511, ...) at most 108 rows name the same one
- gate_values: float32 [8192, 3], P(('dp', 'expert')), may hold values from 0.1 to 0.5
- parents: int32 [4, 8], P('dp'), may hold values from 0 to 6, as said below
- attn_gain: bfloat16 [2048], P(('dp', 'expert')), may hold values from 0.5 to 1.5
- w_query: bfloat16 [2048, 3072], P(('dp', 'expert')), may hold values from -0.125 to 0.125
- w_latent: bfloat16 [2048, 576], P(('dp', 'expert')), may hold values from -0.125 to 0.125
- latent_gain: bfloat16 [512], P(('dp', 'expert')), may hold values from 0.5 to 1.5
- w_expand: bfloat16 [512, 4096], P(('dp', 'expert')), may hold values from -0.25 to 0.25
- w_output: bfloat16 [2048, 2048], P(('dp', 'expert')), may hold values from -0.75 to 0.75
- ffn_gain: bfloat16 [2048], P(('dp', 'expert')), may hold values from 0.5 to 1.5
- shared_gate: bfloat16 [2048, 2816], P(('dp', 'expert')), may hold values from -0.125 to 0.125
- shared_up: bfloat16 [2048, 2816], P(('dp', 'expert')), may hold values from -0.125 to 0.125
- shared_down: bfloat16 [2816, 2048], P(('dp', 'expert')), may hold values from -0.21875 to 0.21875
- expert_gate: bfloat16 [8, 2048, 1408], P('expert'), may hold values from -0.125 to 0.125
- expert_up: bfloat16 [8, 2048, 1408], P('expert'), may hold values from -0.125 to 0.125
- expert_down: bfloat16 [8, 1408, 2048], P('expert'), may hold values from -0.3125 to 0.3125
Outputs:
- block_out: bfloat16 [8192, 2048], P(('dp', 'expert'))
- grad_tokens: float32 [8192, 2048], P(('dp', 'expert'))
- grad_attn_gain: float32 [2048], P(('dp', 'expert'))
- grad_w_query: float32 [2048, 3072], P(('dp', 'expert'))
- grad_w_latent: float32 [2048, 576], P(('dp', 'expert'))
- grad_latent_gain: float32 [512], P(('dp', 'expert'))
- grad_w_expand: float32 [512, 4096], P(('dp', 'expert'))
- grad_w_output: float32 [2048, 2048], P(('dp', 'expert'))
- grad_ffn_gain: float32 [2048], P(('dp', 'expert'))
- grad_shared_gate: float32 [2048, 2816], P(('dp', 'expert'))
- grad_shared_up: float32 [2048, 2816], P(('dp', 'expert'))
- grad_shared_down: float32 [2816, 2048], P(('dp', 'expert'))
- grad_expert_gate: float32 [8, 2048, 1408], P('expert', 'dp')
- grad_expert_up: float32 [8, 2048, 1408], P('expert', 'dp')
- grad_expert_down: float32 [8, 1408, 2048], P('expert', None, 'dp')
The draws below stay inside these ranges and needn't reach their ends.
Inputs may be any that keep to these rules, and one draw needn't show every extreme that they name: `routes`: each token's 3 entries are different experts; among the tokens of one device no expert is named more than 108 times, a bound that some block reaches. parents[t, 0] = 0 (segment 0 is the root), 0 <= parents[t, s] < s for s >= 1, and the last segment's parent is the segment before it.
All inputs are finite; a program needn't handle non-finite values.
Results may differ from the reference program's by a relative error of at most 0.02.
Values may be sent and summed in bfloat16 or wider, within the bound.
A program may use at most 384 MiB of HBM per device.

```python
import math
import jax
import jax.numpy as jnp
import numpy as np
from jax import lax

D = 2048
HEADS = 16
NOPE = 128
ROPE = 64
KV = 512
VD = 128
FF = 1408
SFF = 2816
TOP = 3
SEG = 256
TOK_DEV = 256
TREE_LEN = 2048
NSEG = 8
TREES = 4
TOKENS = 8192
EXPERTS = 8
CAP = 108


def draw_parents(key, part):
    raw = jax.random.randint(key, (TREES, NSEG), 0, 1 << 20)
    seg_ids = jnp.arange(NSEG, dtype=jnp.int32)
    limit = jnp.maximum(seg_ids, 1)
    drawn = (raw % limit[None, :]).astype(jnp.int32)
    last_parent = jnp.maximum(seg_ids - 1, 0)
    return jnp.where((seg_ids == NSEG - 1)[None, :], last_parent[None, :], drawn).astype(jnp.int32)


def steps_of(stream_key, dims, shards, least, high):
    def one(axis_at, parts):
        steps = jax.random.uniform(jax.random.fold_in(jax.random.fold_in(stream_key, 6), axis_at), (parts,), jnp.float32, least / len(shards), high / len(shards))
        return jnp.repeat(jnp.exp(steps), dims[axis_at] // parts).reshape((-1,) + (1,) * (len(dims) - axis_at - 1))

    loudness = one(*shards[0])
    for cut in shards[1:]:
        loudness = loudness * one(*cut)
    return loudness


def routed_block(own_key, own, number, rows, amount, top, most, lean):
    order = jax.random.permutation(own_key, amount)
    packed, ordinary = load_shares(amount, rows * top, most, lean, True), load_shares(amount, rows * top, most, lean, False)
    places = jnp.arange(amount)

    def named(lengths, offset_by):
        used = int((lengths > 0).sum())
        fixed = max(1, used // 4)
        passed = fixed + (places - fixed + offset_by * (used - fixed)) % max(1, amount - fixed)
        return jnp.zeros((amount,), jnp.int32).at[order[jnp.where(places < fixed, places, passed)]].set(jnp.asarray(lengths, jnp.int32))

    lengths = jnp.where(number % 4 == 0, named(packed, number // 4), named(ordinary, number - number // 4 - 1))
    mixed = jax.random.permutation(jax.random.fold_in(own, 3), amount)
    giver, taker = mixed[0:amount // 2 * 2:2], mixed[1:amount // 2 * 2:2]
    room = jnp.minimum(lengths[giver] - 1, most - lengths[taker]) // 2
    room = jnp.where((giver == order[0]) | (taker == order[0]) | (lengths[taker] == 0), 0, jnp.maximum(room, 0))
    passed = jax.random.randint(jax.random.fold_in(own, 4), (amount // 2,), 0, 1 << 20) % (room + 1)
    lengths = lengths.at[giver].add(-passed).at[taker].add(passed)
    labels = jnp.searchsorted(jnp.cumsum(lengths), jnp.arange(rows * top), side="right").astype(jnp.int32)
    table = labels.reshape(top, rows).T
    table = table[jax.random.permutation(jax.random.fold_in(own, 1), rows)]
    offset_by = jax.random.randint(jax.random.fold_in(own, 2), (rows, 1), 0, top)
    return jnp.take_along_axis(table, (jnp.arange(top)[None, :] + offset_by) % top, axis=1)


def load_shares(number_of, total, bound, slope, full):
    portions = [(1 << 20) // math.isqrt(standing ** slope) + 1 for standing in range(1, number_of + 1)]
    largest = bound if full else min(bound, max(-(-total // number_of), total * portions[0] // sum(portions)))
    least = 1 if total - largest >= number_of - 1 else 0
    counts, surplus = [largest] + [least] * (number_of - 1), total - largest - least * (number_of - 1)
    while surplus > 0:
        free = [i for i in range(1, number_of) if counts[i] < largest] or [i for i in range(1, number_of) if counts[i] < bound]
        pool, budget = sum([portions[i] for i in free]), surplus
        for i in free:
            extra = min(bound - counts[i], max(1, budget * portions[i] // pool), surplus)
            counts[i] = counts[i] + extra
            surplus = surplus - extra
    return np.array(counts)


def centred(key, shape, width, bound, cuts=(), kind=jnp.bfloat16):
    values = jax.random.normal(key, shape, jnp.float32) * width
    if len(cuts) > 0:
        values = steps_of(key, shape, cuts, -0.22, 0.18) * values
    return jnp.clip(values, min=-bound, max=bound).astype(kind)


def setup_inputs(seed: int = 0) -> dict:
    key_of = jax.random.split(jax.random.key(seed), 19)
    tokens = centred(key_of[0], (TOKENS, D), 1.0, 6.0, ((0, 32),))
    grad_out = centred(key_of[1], (TOKENS, D), 1.0, 6.0, ((0, 32),))
    routes_keys = jax.random.split(jax.random.fold_in(key_of[2], 1), TOKENS // TOK_DEV)
    routes_turns = jax.random.permutation(jax.random.fold_in(key_of[2], 3), TOKENS // TOK_DEV)
    routes = jax.vmap(lambda own, number: routed_block(jax.random.fold_in(key_of[2], 2), own, number, TOK_DEV, EXPERTS, TOP, CAP, 1))(routes_keys, routes_turns).reshape((TOKENS, TOP))
    gate_values = jnp.clip(0.1 + 0.4 * jax.random.uniform(key_of[3], (TOKENS, TOP), jnp.float32) ** steps_of(key_of[3], (TOKENS, TOP), ((0, 32),), -0.2, 0.2), 0.1, 0.5)
    parents = draw_parents(jax.random.fold_in(key_of[18], 71), 0)
    attn_gain = jnp.clip(1.0 + 0.1 * jax.random.normal(key_of[5], (D,), jnp.float32), 0.5, 1.5).astype(jnp.bfloat16)
    w_query = centred(key_of[6], (D, HEADS * (NOPE + ROPE)), D ** -0.5, 0.125, ((0, 32),))
    w_latent = centred(key_of[7], (D, KV + ROPE), D ** -0.5, 0.125, ((0, 32),))
    latent_gain = jnp.clip(1.0 + 0.1 * jax.random.normal(key_of[8], (KV,), jnp.float32), 0.5, 1.5).astype(jnp.bfloat16)
    w_expand = centred(key_of[9], (KV, HEADS * (NOPE + VD)), KV ** -0.5, 0.25, ((0, 32),))
    w_output = centred(key_of[10], (HEADS * VD, D), (HEADS * VD // 32) ** -0.5, 0.75, ((0, 32),))
    ffn_gain = jnp.clip(1.0 + 0.1 * jax.random.normal(key_of[11], (D,), jnp.float32), 0.5, 1.5).astype(jnp.bfloat16)
    shared_gate = centred(key_of[12], (D, SFF), D ** -0.5, 0.125, ((0, 32),))
    shared_up = centred(key_of[13], (D, SFF), D ** -0.5, 0.125, ((0, 32),))
    shared_down = centred(key_of[14], (SFF, D), (SFF // 4) ** -0.5, 0.21875, ((0, 32),))
    expert_gate = centred(key_of[15], (EXPERTS, D, FF), D ** -0.5, 0.125, ((0, 8),))
    expert_up = centred(key_of[16], (EXPERTS, D, FF), D ** -0.5, 0.125, ((0, 8),))
    expert_down = centred(key_of[17], (EXPERTS, FF, D), (FF // 4) ** -0.5, 0.3125, ((0, 8),))
    return dict(tokens=tokens, grad_out=grad_out, routes=routes, gate_values=gate_values, parents=parents, attn_gain=attn_gain, w_query=w_query, w_latent=w_latent, latent_gain=latent_gain, w_expand=w_expand, w_output=w_output, ffn_gain=ffn_gain, shared_gate=shared_gate, shared_up=shared_up, shared_down=shared_down, expert_gate=expert_gate, expert_up=expert_up, expert_down=expert_down)


@jax.custom_vjp
def low(v):
    return lax.optimization_barrier(v.astype(jnp.bfloat16)).astype(jnp.float32)

@jax.custom_vjp
def low_back(v):
    return v

def low_keep(v):
    return (low(v), None)

def low_pass(kept, grad):
    return (grad,)

def back_keep(v):
    return (v, None)

def back_low(kept, grad):
    return (low(grad),)
low.defvjp(low_keep, low_pass)
low_back.defvjp(back_keep, back_low)
epsilon = 1e-06
highest = lax.Precision.HIGHEST

def matmul(left, right):
    return jnp.dot(left, right, precision=highest)

def norm_rows(values, gain_vec):
    return values * lax.rsqrt(lax.optimization_barrier(jnp.mean(values * values, axis=-1, keepdims=True)) + epsilon) * gain_vec

def rotate(values, cos_table, sin_table):
    half_width = values.shape[-1] // 2
    first_half = values[..., :half_width]
    second_half = values[..., half_width:]
    return jnp.concatenate([first_half * cos_table - second_half * sin_table, second_half * cos_table + first_half * sin_table], axis=-1)

def ancestry(parent_row, seg_count):
    identity = jnp.eye(seg_count, dtype=jnp.float32)
    parent_hot = (parent_row[:, None] == jnp.arange(seg_count, dtype=jnp.int32)[None, :]).astype(jnp.float32)

    def grow(turn_index, reachable):
        return jnp.maximum(identity, jnp.dot(parent_hot, reachable))
    return lax.fori_loop(0, seg_count, grow, identity)

def tree_layout(parent_row):
    reachable = ancestry(parent_row, NSEG)
    index = jnp.arange(TREE_LEN, dtype=jnp.int32)
    seg_of = index // SEG
    offset = index % SEG
    seg_depth = lax.optimization_barrier(jnp.sum(reachable, axis=1)) - 1.0
    positions = seg_depth[seg_of] * SEG + offset.astype(reachable.dtype)
    reach_tok = reachable[seg_of][:, seg_of] > 0.5
    same_seg = seg_of[:, None] == seg_of[None, :]
    allowed = reach_tok & ~same_seg | same_seg & (offset[None, :] <= offset[:, None])
    return (positions, allowed)

def reference(tokens, grad_out, routes, gate_values, parents, attn_gain, w_query, w_latent, latent_gain, w_expand, w_output, ffn_gain, shared_gate, shared_up, shared_down, expert_gate, expert_up, expert_down):
    positions, allowed = jax.vmap(tree_layout)(parents)
    positions = positions.reshape(TOKENS)
    half_width = ROPE // 2
    freq = 10000.0 ** (-2.0 * jnp.arange(half_width, dtype=jnp.float32) / ROPE)
    angle = positions[:, None] * freq[None, :]
    cos_table = jnp.cos(angle)
    sin_table = jnp.sin(angle)
    expert_ids = jnp.arange(EXPERTS, dtype=jnp.int32)
    combine_weights = lax.optimization_barrier(jnp.sum(gate_values[:, :, None] * (routes[:, :, None] == expert_ids[None, None, :]).astype(jnp.float32), axis=1))
    score_scale = (NOPE + ROPE) ** (-0.5)

    def tree_attention(pieces):
        query_t, keys_t, rope_t, allow_t = pieces
        score = (jnp.einsum('qhd,khd->hqk', query_t[..., :NOPE], keys_t[..., :NOPE], precision=highest) + jnp.einsum('qhr,kr->hqk', query_t[..., NOPE:], rope_t, precision=highest)) * score_scale
        score = low_back(score)
        score = jnp.where(allow_t[None], score, -1e+30)
        probability = low(jax.nn.softmax(score, axis=-1))
        values = jnp.einsum('hqk,khd->qhd', probability, keys_t[..., NOPE:], precision=highest)
        return values.reshape(TREE_LEN, HEADS * VD)

    def forward(tokens_f, attn_gain, w_query, w_latent, latent_gain, w_expand, w_output, ffn_gain, shared_gate, shared_up, shared_down, expert_gate, expert_up, expert_down):
        first_normed = low(norm_rows(tokens_f, attn_gain))
        query = low_back(matmul(first_normed, w_query)).reshape(TOKENS, HEADS, NOPE + ROPE)
        query = low(jnp.concatenate([query[..., :NOPE], rotate(query[..., NOPE:], cos_table[:, None, :], sin_table[:, None, :])], axis=-1))
        latent = low_back(matmul(first_normed, w_latent))
        latent_normed = low(norm_rows(latent[:, :KV], latent_gain))
        rope_key = low(rotate(latent[:, KV:], cos_table, sin_table))
        key_value = low(matmul(latent_normed, w_expand)).reshape(TOKENS, HEADS, NOPE + VD)
        attended = lax.map(jax.checkpoint(tree_attention), (query.reshape(TREES, TREE_LEN, HEADS, NOPE + ROPE), key_value.reshape(TREES, TREE_LEN, HEADS, NOPE + VD), rope_key.reshape(TREES, TREE_LEN, ROPE), allowed))
        attended = low(low_back(attended.reshape(TOKENS, HEADS * VD)))
        resid = tokens_f + low_back(matmul(attended, w_output))
        second_normed = low(norm_rows(resid, ffn_gain))
        gate_part = low_back(matmul(second_normed, shared_gate))
        up_part = low_back(matmul(second_normed, shared_up))
        shared_act = low(low_back(jax.nn.silu(gate_part) * up_part))
        shared_result = low_back(matmul(shared_act, shared_down))

        def one_expert(total, pieces):
            gate_w, up_w, down_w, column = pieces
            expert_rows = low_back(second_normed)
            expert_gate_part = low_back(matmul(expert_rows, gate_w))
            expert_up_part = low_back(matmul(expert_rows, up_w))
            activated = low(low_back(jax.nn.silu(expert_gate_part) * expert_up_part))
            expert_result = low(low_back(matmul(activated, down_w)))
            return (total + column[:, None] * expert_result, None)
        routed, unused = lax.scan(jax.checkpoint(one_expert), jnp.zeros_like(resid), (expert_gate, expert_up, expert_down, combine_weights.T))
        return resid + shared_result + routed
    primals = [tokens.astype(jnp.float32)] + [weight.astype(jnp.float32) for weight in (attn_gain, w_query, w_latent, latent_gain, w_expand, w_output, ffn_gain, shared_gate, shared_up, shared_down, expert_gate, expert_up, expert_down)]
    result, pullback = jax.vjp(forward, *primals)
    grads = pullback(grad_out.astype(jnp.float32))
    return (result.astype(jnp.bfloat16), grads[0], grads[1], grads[2], grads[3], grads[4], grads[5], grads[6], grads[7], grads[8], grads[9], grads[10], grads[11], grads[12], grads[13])
```

```python
import functools

import jax
import jax.numpy as jnp
from jax import lax
from jax.experimental import pallas as pl
from jax.experimental.pallas import tpu as pltpu
from jax.sharding import PartitionSpec as P

HEADS = 16
NOPE = 128
ROPE = 64
KV = 512
VD = 128
SEG = 256
KEY = 256

epsilon = 1e-06
bf16 = jnp.bfloat16
f32 = jnp.float32
EVERY = ("dp", "expert")
MESH = pl.DeviceIdType.MESH
VMEM_LIMIT = 60 << 20
WIRE = pl.CostEstimate(flops=0, bytes_accessed=300_000_000, transcendentals=0)


def norm_rows(values, gain_vec):
    return (
        values * lax.rsqrt(jnp.mean(values * values, axis=-1, keepdims=True) + epsilon) * gain_vec
    )


def rotate(values, cos_table, sin_table):
    half_width = values.shape[-1] // 2
    first_half = values[..., :half_width]
    second_half = values[..., half_width:]
    return jnp.concatenate(
        [
            first_half * cos_table - second_half * sin_table,
            second_half * cos_table + first_half * sin_table,
        ],
        axis=-1,
    )


def gating(gate_part, up_part):
    return jax.nn.silu(gate_part) * up_part


def ancestry(parent_row, seg_count):
    identity = jnp.eye(seg_count, dtype=f32)
    parent_hot = (parent_row[:, None] == jnp.arange(seg_count, dtype=jnp.int32)[None, :]).astype(
        f32
    )
    reachable = identity
    for _ in range(seg_count - 1):
        reachable = jnp.maximum(identity, jnp.dot(parent_hot, reachable))
    return reachable


def matmul(left, right):
    return jnp.dot(left, right, preferred_element_type=f32)


def dot_last(left, right):
    return lax.dot_general(left, right, (((1,), (1,)), ((), ())), preferred_element_type=f32)


def dot_first(left, right):
    return lax.dot_general(left, right, (((0,), (0,)), ((), ())), preferred_element_type=f32)


def greet(rank, last):
    barrier = pltpu.get_barrier_semaphore()
    a = rank // 2

    def hail(other):
        pl.semaphore_signal(barrier, inc=1, device_id={"expert": other}, device_id_type=MESH)

    hail(rank + 1 - 2 * (rank % 2))

    @pl.when(a < last)
    def _():
        hail(rank + 2)

    @pl.when(a > 0)
    def _():
        hail(rank - 2)

    pl.semaphore_wait(barrier, 1 + (a + last - 1) // last + (2 * last - 1 - a) // last)


def gather_kernel(chunks, x_ref, o_ref, sx, rx, su, ru, sd, rd):
    rank = lax.axis_index("expert")
    last = o_ref.shape[0] // 2 - 1
    a = rank // 2
    side = rank + 1 - 2 * (rank % 2)
    rows = x_ref.shape[0] // chunks
    greet(rank, last)

    def piece(ref, c):
        return ref.at[pl.ds(c * rows, rows)]

    def to(src, block, c, send, recv, target):
        return pltpu.make_async_remote_copy(
            src_ref=src,
            dst_ref=piece(o_ref.at[block], c),
            send_sem=send,
            recv_sem=recv,
            device_id={"expert": target},
            device_id_type=MESH,
        )

    for c in range(chunks):
        own = piece(x_ref, c)
        to(own, rank, c, sx.at[0, c], rx.at[0, c], side).start()

        @pl.when(a < last)
        def _():
            to(own, rank, c, su.at[0, c], ru.at[0, c], rank + 2).start()

        @pl.when(a > 0)
        def _():
            to(own, rank, c, sd.at[0, c], rd.at[0, c], rank - 2).start()

    for s in range(1, last + 1):
        for c in range(chunks):

            @pl.when(a >= s)
            def _():
                block = rank - 2 * s
                src = piece(o_ref.at[block], c)
                to(src, block, c, su.at[s - 1, c], ru.at[s - 1, c], rank + 2).wait_recv()
                to(src, block, c, sx.at[s, c], rx.at[s, c], side).start()

                @pl.when(a < last)
                def _():
                    to(src, block, c, su.at[s, c], ru.at[s, c], rank + 2).start()

            @pl.when(a + s <= last)
            def _():
                block = rank + 2 * s
                src = piece(o_ref.at[block], c)
                to(src, block, c, sd.at[s - 1, c], rd.at[s - 1, c], rank - 2).wait_recv()
                to(src, block, c, sx.at[last + s, c], rx.at[last + s, c], side).start()

                @pl.when(a > 0)
                def _():
                    to(src, block, c, sd.at[s, c], rd.at[s, c], rank - 2).start()

    o_ref[rank] = x_ref[...]
    for c in range(chunks):
        own = piece(x_ref, c)
        to(own, side, c, sx.at[0, c], rx.at[0, c], side).wait()

        @pl.when(a < last)
        def _():
            to(own, rank, c, su.at[0, c], ru.at[0, c], rank + 2).wait_send()

        @pl.when(a > 0)
        def _():
            to(own, rank, c, sd.at[0, c], rd.at[0, c], rank - 2).wait_send()

    for s in range(1, last + 1):
        for c in range(chunks):

            @pl.when(a >= s)
            def _():
                block = rank - 2 * s
                src = piece(o_ref.at[block], c)
                to(src, side - 2 * s, c, sx.at[s, c], rx.at[s, c], side).wait()

                @pl.when(a < last)
                def _():
                    to(src, block, c, su.at[s, c], ru.at[s, c], rank + 2).wait_send()

            @pl.when(a + s <= last)
            def _():
                block = rank + 2 * s
                src = piece(o_ref.at[block], c)
                to(src, side + 2 * s, c, sx.at[last + s, c], rx.at[last + s, c], side).wait()

                @pl.when(a > 0)
                def _():
                    to(src, block, c, sd.at[s, c], rd.at[s, c], rank - 2).wait_send()


def gather_rows(x, count, call_id, chunks=2):
    half = count // 2
    dma = pltpu.SemaphoreType.DMA
    return pl.pallas_call(
        functools.partial(gather_kernel, chunks),
        out_shape=jax.ShapeDtypeStruct((count,) + x.shape, x.dtype),
        in_specs=[pl.BlockSpec(memory_space=pltpu.VMEM)],
        out_specs=pl.BlockSpec(memory_space=pltpu.VMEM),
        scratch_shapes=[dma((2 * half, chunks))] * 2 + [dma((half, chunks))] * 4,
        compiler_params=pltpu.CompilerParams(
            collective_id=call_id, has_side_effects=True, vmem_limit_bytes=VMEM_LIMIT
        ),
        cost_estimate=WIRE,
        name="gather_rows",
    )(x)


def reduce_kernel(chunks, p_ref, o_ref, rx, st, ru, rd, acc, sxs, rxs, sus, rus, sds, rds):
    rank = lax.axis_index("expert")
    last = p_ref.shape[0] // 2 - 1
    a = rank // 2
    b = rank % 2
    rows = p_ref.shape[1] // chunks
    greet(rank, last)
    h = a // 2
    order = [3 - 3 * h, 2 - h, 4 * h + 1 - a, a]

    def cut(ref, c):
        return ref.at[pl.ds(c * rows, rows)]

    def copy(src, dst, send, recv, target):
        return pltpu.make_async_remote_copy(
            src_ref=src,
            dst_ref=dst,
            send_sem=send,
            recv_sem=recv,
            device_id={"expert": target},
            device_id_type=MESH,
        )

    def across(t, c):
        return copy(
            cut(p_ref.at[2 * t + 1 - b], c),
            cut(rx.at[t], c),
            sxs.at[t, c],
            rxs.at[t, c],
            rank + 1 - 2 * b,
        )

    def upward(t, c):
        return copy(cut(st.at[t], c), cut(ru.at[t], c), sus.at[t, c], rus.at[t, c], rank + 2)

    def downward(t, c):
        return copy(cut(st.at[t], c), cut(rd.at[t], c), sds.at[t, c], rds.at[t, c], rank - 2)

    for t in order:
        for c in range(chunks):
            across(t, c).start()
    for t in order:
        for c in range(chunks):
            across(t, c).wait_recv()
            acc[...] = cut(p_ref.at[2 * t + b], c)[...].astype(f32) + cut(rx.at[t], c)[...].astype(
                f32
            )

            @pl.when((t >= a) & (a > 0))
            def _():
                upward(t, c).wait_recv()
                acc[...] += cut(ru.at[t], c)[...].astype(f32)

            @pl.when((t <= a) & (a < last))
            def _():
                downward(t, c).wait_recv()
                acc[...] += cut(rd.at[t], c)[...].astype(f32)

            @pl.when(t == a)
            def _():
                cut(o_ref, c)[...] = acc[...]

            @pl.when(t > a)
            def _():
                cut(st.at[t], c)[...] = acc[...].astype(st.dtype)
                upward(t, c).start()

            @pl.when(t < a)
            def _():
                cut(st.at[t], c)[...] = acc[...].astype(st.dtype)
                downward(t, c).start()

    for t in order:
        for c in range(chunks):
            across(t, c).wait_send()

            @pl.when(t > a)
            def _():
                upward(t, c).wait_send()

            @pl.when(t < a)
            def _():
                downward(t, c).wait_send()


def reduce_rows(p, call_id, chunks=4):
    count, rows, width = p.shape
    half = count // 2
    buf = pltpu.VMEM((half, rows, width), p.dtype)
    sem = pltpu.SemaphoreType.DMA((half, chunks))
    return pl.pallas_call(
        functools.partial(reduce_kernel, chunks),
        out_shape=jax.ShapeDtypeStruct((rows, width), f32),
        in_specs=[pl.BlockSpec(memory_space=pltpu.VMEM)],
        out_specs=pl.BlockSpec(memory_space=pltpu.VMEM),
        scratch_shapes=[buf] * 4 + [pltpu.VMEM((rows // chunks, width), f32)] + [sem] * 6,
        compiler_params=pltpu.CompilerParams(
            collective_id=call_id, has_side_effects=True, vmem_limit_bytes=VMEM_LIMIT
        ),
        cost_estimate=WIRE,
        name="reduce_rows",
    )(p)


def triangle():
    keys = lax.broadcasted_iota(jnp.int32, (SEG, SEG), 0)
    queries = lax.broadcasted_iota(jnp.int32, (SEG, SEG), 1)
    return keys <= queries


def attend_kernel(
    heads, segs, scale, reach_ref, q_ref, k_ref, v_ref, out_ref, full_ref, log_ref, m_s, l_s, acc_s
):
    i = pl.program_id(0)
    diag = triangle()

    def score(h, j):
        keys = k_ref[pl.ds(j * SEG, SEG), h * KEY : (h + 1) * KEY]
        return dot_last(keys, q_ref[:, h * KEY : (h + 1) * KEY]) * scale

    def weigh(h, j, weights):
        vals = v_ref[pl.ds(j * SEG, SEG), h * VD : (h + 1) * VD]
        return dot_first(vals, weights.astype(bf16))

    for h in range(heads):
        s = jnp.where(diag, score(h, i), -1e30)
        top = jnp.max(s, axis=0, keepdims=True)
        w = jnp.where(diag, jnp.exp(s - top), 0.0)
        m_s[h : h + 1] = top
        l_s[h : h + 1] = jnp.sum(w, axis=0, keepdims=True)
        acc_s[h] = weigh(h, i, w)

    def step(j, carry):
        @pl.when(reach_ref[i * segs + j] > 0)
        def _():
            for h in range(heads):
                s = score(h, j)
                old = m_s[h : h + 1]
                top = jnp.maximum(old, jnp.max(s, axis=0, keepdims=True))
                w = jnp.exp(s - top)
                fade = jnp.exp(old - top)
                m_s[h : h + 1] = top
                l_s[h : h + 1] = l_s[h : h + 1] * fade + jnp.sum(w, axis=0, keepdims=True)
                acc_s[h] = acc_s[h] * fade + weigh(h, j, w)

        return carry

    lax.fori_loop(0, i, step, 0)
    for h in range(heads):
        total = l_s[h : h + 1]
        rows = (acc_s[h] * (1.0 / total)).T
        full_ref[:, h * VD : (h + 1) * VD] = rows
        out_ref[:, h * VD : (h + 1) * VD] = rows.astype(bf16)
        log_ref[h : h + 1] = m_s[h : h + 1] + jnp.log(total)


def attend(reach, q, k, v, scale):
    tree = q.shape[0]
    segs = tree // SEG
    heads = q.shape[1] // KEY
    whole = lambda width: pl.BlockSpec((tree, width), lambda i, r: (0, 0))
    part = lambda width: pl.BlockSpec((SEG, width), lambda i, r: (i, 0))
    return pl.pallas_call(
        functools.partial(attend_kernel, heads, segs, scale),
        grid_spec=pltpu.PrefetchScalarGridSpec(
            num_scalar_prefetch=1,
            grid=(segs,),
            in_specs=[part(heads * KEY), whole(heads * KEY), whole(heads * VD)],
            out_specs=[
                part(heads * VD),
                part(heads * VD),
                pl.BlockSpec((heads, SEG), lambda i, r: (0, i)),
            ],
            scratch_shapes=[
                pltpu.VMEM((heads, SEG), f32),
                pltpu.VMEM((heads, SEG), f32),
                pltpu.VMEM((heads, VD, SEG), f32),
            ],
        ),
        out_shape=[
            jax.ShapeDtypeStruct((tree, heads * VD), bf16),
            jax.ShapeDtypeStruct((tree, heads * VD), f32),
            jax.ShapeDtypeStruct((heads, tree), f32),
        ],
        compiler_params=pltpu.CompilerParams(vmem_limit_bytes=VMEM_LIMIT),
        name="attend",
    )(reach, q, k, v)


def attend_back_kernel(
    heads,
    segs,
    scale,
    reach_ref,
    q_ref,
    k_ref,
    v_ref,
    g_ref,
    log_ref,
    delta_ref,
    dq_ref,
    dkv_ref,
    dr_ref,
    dk_s,
    dv_s,
):
    j = pl.program_id(0)
    diag = triangle()

    @pl.when(j == 0)
    def _():
        dq_ref[...] = jnp.zeros_like(dq_ref)

    dk_s[...] = jnp.zeros_like(dk_s)
    dv_s[...] = jnp.zeros_like(dv_s)

    def block(i, masked):
        rows = pl.ds(i * SEG, SEG)
        for h in range(heads):
            kcols = slice(h * KEY, (h + 1) * KEY)
            vcols = slice(h * VD, (h + 1) * VD)
            q = q_ref[rows, kcols]
            k = k_ref[:, kcols]
            g = g_ref[rows, vcols]
            s = dot_last(k, q) * scale
            w = jnp.exp(s - log_ref[h : h + 1, rows])
            if masked:
                w = jnp.where(diag, w, 0.0)
            dw = dot_last(v_ref[:, vcols], g)
            ds = (w * (dw - delta_ref[h : h + 1, rows])).astype(bf16)
            dv_s[h] += matmul(w.astype(bf16), g)
            dk_s[h] += matmul(ds, q)
            dq_ref[rows, kcols] += dot_first(ds, k)

    block(j, True)

    def step(i, carry):
        @pl.when(reach_ref[i * segs + j] > 0)
        def _():
            block(i, False)

        return carry

    lax.fori_loop(j + 1, segs, step, 0)
    rope = jnp.zeros((SEG, KEY - NOPE), f32)
    for h in range(heads):
        dkv_ref[:, h * KEY : h * KEY + NOPE] = (dk_s[h, :, :NOPE] * scale).astype(bf16)
        dkv_ref[:, h * KEY + NOPE : (h + 1) * KEY] = dv_s[h].astype(bf16)
        rope = rope + dk_s[h, :, NOPE:]
    dr_ref[...] = rope * scale


def attend_back(reach, q, k, v, g, log_total, delta, scale):
    tree = q.shape[0]
    segs = tree // SEG
    heads = q.shape[1] // KEY
    whole = lambda width: pl.BlockSpec((tree, width), lambda j, r: (0, 0))
    part = lambda width: pl.BlockSpec((SEG, width), lambda j, r: (j, 0))
    lane = pl.BlockSpec((heads, tree), lambda j, r: (0, 0))
    return pl.pallas_call(
        functools.partial(attend_back_kernel, heads, segs, scale),
        grid_spec=pltpu.PrefetchScalarGridSpec(
            num_scalar_prefetch=1,
            grid=(segs,),
            in_specs=[
                whole(heads * KEY),
                part(heads * KEY),
                part(heads * VD),
                whole(heads * VD),
                lane,
                lane,
            ],
            out_specs=[whole(heads * KEY), part(heads * KEY), part(KEY - NOPE)],
            scratch_shapes=[
                pltpu.VMEM((heads, SEG, KEY), f32),
                pltpu.VMEM((heads, SEG, VD), f32),
            ],
        ),
        out_shape=[
            jax.ShapeDtypeStruct((tree, heads * KEY), f32),
            jax.ShapeDtypeStruct((tree, heads * KEY), bf16),
            jax.ShapeDtypeStruct((tree, KEY - NOPE), f32),
        ],
        compiler_params=pltpu.CompilerParams(vmem_limit_bytes=VMEM_LIMIT),
        name="attend_back",
    )(reach, q, k, v, g, log_total, delta)


def per_device(
    tokens,
    grad_out,
    routes,
    gate_values,
    parents,
    attn_gain,
    w_query,
    w_latent,
    latent_gain,
    w_expand,
    w_output,
    ffn_gain,
    shared_gate,
    shared_up,
    shared_down,
    expert_gate,
    expert_up,
    expert_down,
):
    group = lax.axis_size("expert")
    spread = lax.axis_size("dp")
    rank = lax.axis_index("expert")
    tok_dev, width = tokens.shape
    tree = tok_dev * group
    segs = parents.shape[1]
    per_token = routes.shape[1]
    capacity = tok_dev * per_token * 9 // (8 * group)
    slots = -(-capacity // 16) * 16
    scale = (NOPE + ROPE) ** (-0.5)
    mine = HEADS // group
    rows_w = w_query.shape[0]
    rows_l = w_expand.shape[0]
    ff_cut = shared_down.shape[0]
    ff_own = ff_cut * spread
    ff_pad = -(-ff_own // 128) * 128
    q_own = mine * KEY
    e_own = mine * (NOPE + VD)
    e_fold = rows_l * e_own // rows_w

    x_all = gather_rows(tokens, group, 0).reshape(tree, width)
    g_all = lax.all_gather(grad_out, "expert", axis=0, tiled=True)

    wq_cut = jnp.pad(
        w_query.reshape(rows_w, group, mine, NOPE + ROPE),
        ((0, 0), (0, 0), (0, 0), (0, KEY - NOPE - ROPE)),
    ).reshape(rows_w, group, q_own)

    def ff_columns(weight):
        cut = weight.reshape(rows_w, spread, group, ff_cut).transpose(0, 2, 1, 3)
        return jnp.pad(
            cut.reshape(rows_w, group, ff_own), ((0, 0), (0, 0), (0, ff_pad - ff_own))
        )

    we_cut = (
        w_expand.reshape(rows_l, group, e_own).transpose(1, 0, 2).reshape(group, rows_w, e_fold)
    )
    packed = jnp.concatenate(
        [
            wq_cut.transpose(1, 0, 2),
            we_cut,
            ff_columns(shared_gate).transpose(1, 0, 2),
            ff_columns(shared_up).transpose(1, 0, 2),
        ],
        axis=2,
    )
    packed = lax.all_to_all(packed, "expert", split_axis=0, concat_axis=0, tiled=True)
    packed = lax.all_gather(packed, "dp", axis=0, tiled=True).reshape(width, -1)
    wq = packed[:, :q_own]
    we = packed[:, q_own : q_own + e_fold].reshape(KV, e_own)
    sg = packed[:, q_own + e_fold : q_own + e_fold + ff_pad]
    su = packed[:, q_own + e_fold + ff_pad :]
    sd = lax.all_gather(shared_down, "dp", axis=0, tiled=True)
    sd = jnp.pad(sd, ((0, ff_pad - ff_own), (0, 0)))

    lat_w = KV + ROPE
    gains = jnp.stack(
        [attn_gain, ffn_gain, jnp.pad(latent_gain, (0, rows_w - rows_l))], axis=1
    )
    gains = jnp.pad(gains, ((0, 0), (0, ROPE - 3)))
    lat_pack = lax.all_gather(
        jnp.concatenate([w_latent, gains], axis=1), EVERY, axis=0, tiled=True
    )
    wl = lat_pack[:, :lat_w]
    a_gain = lat_pack[:, lat_w].astype(f32)
    f_gain = lat_pack[:, lat_w + 1].astype(f32)
    l_gain = lat_pack[:, lat_w + 2].reshape(-1, rows_w)[:, :rows_l].reshape(KV).astype(f32)
    wo = lax.all_gather(w_output, EVERY, axis=0, tiled=True)

    reachable = ancestry(parents[0], segs)
    depth = jnp.sum(reachable, axis=1) - 1.0
    reach = reachable.astype(jnp.int32).reshape(segs * segs)
    positions = (depth[:, None] * SEG + jnp.arange(SEG, dtype=f32)[None, :]).reshape(tree)
    half_width = ROPE // 2
    freq = 10000.0 ** (-2.0 * jnp.arange(half_width, dtype=f32) / ROPE)
    angle = positions[:, None] * freq[None, :]
    cos_table = jnp.cos(angle)
    sin_table = jnp.sin(angle)

    def own(values):
        return lax.dynamic_slice_in_dim(values, rank * tok_dev, tok_dev, 0)

    h1 = norm_rows(x_all.astype(f32), a_gain).astype(bf16)
    query = matmul(h1, wq).reshape(tree, mine, KEY)

    def query_rope(query_in):
        return jnp.concatenate(
            [
                query_in[..., :NOPE],
                rotate(
                    query_in[..., NOPE : NOPE + ROPE], cos_table[:, None, :], sin_table[:, None, :]
                ),
                jnp.zeros(query_in.shape[:-1] + (KEY - NOPE - ROPE,), f32),
            ],
            axis=-1,
        )

    def query_rope_back(grad):
        return jnp.concatenate(
            [
                grad[..., :NOPE],
                rotate(
                    grad[..., NOPE : NOPE + ROPE], cos_table[:, None, :], -sin_table[:, None, :]
                ),
                jnp.zeros(grad.shape[:-1] + (KEY - NOPE - ROPE,), f32),
            ],
            axis=-1,
        )

    q_att = query_rope(query).astype(bf16).reshape(tree, q_own)
    latent = matmul(h1, wl)
    ckv = norm_rows(latent[:, :KV], l_gain).astype(bf16)
    krope = rotate(latent[:, KV:], cos_table, sin_table).astype(bf16)
    kv = matmul(ckv, we).astype(bf16).reshape(tree, mine, NOPE + VD)
    k_att = jnp.concatenate(
        [
            kv[..., :NOPE],
            jnp.broadcast_to(krope[:, None, :], (tree, mine, ROPE)),
            jnp.zeros((tree, mine, KEY - NOPE - ROPE), bf16),
        ],
        axis=-1,
    ).reshape(tree, q_own)
    v_att = kv[..., NOPE:].reshape(tree, mine * VD)
    attn_heads, attended, log_total = attend(reach, q_att, k_att, v_att, scale)
    attn_own = lax.all_to_all(attn_heads, "expert", split_axis=0, concat_axis=1, tiled=True)
    tokens_f = tokens.astype(f32)
    resid = tokens_f + matmul(attn_own, wo)
    second_normed, second_norm_back = jax.vjp(norm_rows, resid, f_gain)

    h2 = gather_rows(second_normed.astype(bf16), group, 2)
    expert_ids = jnp.arange(group, dtype=jnp.int32)
    gate_of = jnp.sum(
        jnp.where(routes[:, :, None] == expert_ids[None, None, :], gate_values[:, :, None], 0.0),
        axis=1,
    )
    gate_of = lax.all_to_all(gate_of.T, "expert", split_axis=0, concat_axis=0, tiled=True)
    routed = gate_of > 0.0
    upto = (
        jnp.arange(tok_dev, dtype=jnp.int32)[:, None]
        <= jnp.arange(tok_dev, dtype=jnp.int32)[None, :]
    )
    place = matmul(routed.astype(bf16), upto.astype(bf16)).astype(jnp.int32) - 1
    chosen = (
        place[:, None, :] == jnp.arange(slots, dtype=jnp.int32)[None, :, None]
    ) & routed[:, None, :]
    pick = chosen.astype(bf16)
    slot_gate = jnp.sum(jnp.where(chosen, gate_of[:, None, :], 0.0), axis=2).reshape(-1, 1)

    def take(rows):
        return jnp.einsum("bst,btd->bsd", pick, rows, preferred_element_type=f32).reshape(
            group * slots, width
        )

    def give(rows):
        return jnp.einsum(
            "bst,bsd->btd", pick, rows.reshape(group, slots, width), preferred_element_type=f32
        ).reshape(tree, width)

    h2_flat = h2.reshape(tree, width)
    e_rows = take(h2).astype(bf16)
    activated, e_gating_back = jax.vjp(
        gating, matmul(e_rows, expert_gate[0]), matmul(e_rows, expert_up[0])
    )
    activated = activated.astype(bf16)
    e_result = (matmul(activated, expert_down[0]).astype(bf16).astype(f32) * slot_gate).astype(
        bf16
    )
    s_act, s_gating_back = jax.vjp(gating, matmul(h2_flat, sg), matmul(h2_flat, su))
    s_act = s_act.astype(bf16)
    out_part = (matmul(s_act, sd) + give(e_result)).astype(bf16).reshape(group, tok_dev, width)

    e_grad = (take(g_all.reshape(group, tok_dev, width)) * slot_gate).astype(bf16)
    grad_e_act = dot_last(e_grad, expert_down[0]).astype(bf16)
    grad_e_down = dot_first(activated, e_grad).astype(bf16)
    grad_e_gate_part, grad_e_up_part = e_gating_back(grad_e_act.astype(f32))
    grad_e_gate_part = grad_e_gate_part.astype(bf16)
    grad_e_up_part = grad_e_up_part.astype(bf16)
    grad_e_gate = dot_first(e_rows, grad_e_gate_part).astype(bf16)
    grad_e_up = dot_first(e_rows, grad_e_up_part).astype(bf16)
    grad_rows = (
        dot_last(grad_e_gate_part, expert_gate[0]) + dot_last(grad_e_up_part, expert_up[0])
    ).astype(bf16)
    grad_s_act = dot_last(g_all, sd).astype(bf16)
    grad_s_down = dot_first(s_act, g_all).astype(bf16)
    grad_s_gate_part, grad_s_up_part = s_gating_back(grad_s_act.astype(f32))
    grad_s_gate_part = grad_s_gate_part.astype(bf16)
    grad_s_up_part = grad_s_up_part.astype(bf16)
    grad_s_cols = jnp.concatenate(
        [dot_first(h2_flat, grad_s_gate_part), dot_first(h2_flat, grad_s_up_part)], axis=1
    ).astype(bf16)
    second_part = (
        (give(grad_rows) + dot_last(grad_s_gate_part, sg) + dot_last(grad_s_up_part, su))
        .astype(bf16)
        .reshape(group, tok_dev, width)
    )
    out_sum = lax.psum_scatter(
        out_part.reshape(tree, width), "expert", scatter_dimension=0, tiled=True
    )
    block_out = (resid + out_sum.astype(f32)).astype(bf16)
    (second_part, grad_e_gate, grad_e_up, grad_e_down, grad_s_down, grad_s_cols) = (
        lax.optimization_barrier(
            (second_part, grad_e_gate, grad_e_up, grad_e_down, grad_s_down, grad_s_cols)
        )
    )
    grad_second = reduce_rows(second_part, 3)

    grad_e_gate = lax.psum_scatter(grad_e_gate, "dp", scatter_dimension=0, tiled=True)
    grad_e_up = lax.psum_scatter(grad_e_up, "dp", scatter_dimension=0, tiled=True)
    grad_e_down = lax.psum_scatter(grad_e_down, "dp", scatter_dimension=1, tiled=True)
    grad_s_down = lax.psum_scatter(grad_s_down[:ff_own], "dp", scatter_dimension=0, tiled=True)

    def spread_columns(grads):
        summed = lax.psum_scatter(grads, "dp", scatter_dimension=0, tiled=True)
        return lax.all_to_all(
            summed.reshape(group, rows_w, -1), "expert", split_axis=0, concat_axis=0, tiled=True
        )

    grad_s_cols = spread_columns(grad_s_cols)

    def ff_restore(cut):
        return (
            cut[:, :, :ff_own]
            .reshape(group, rows_w, spread, ff_cut)
            .transpose(1, 2, 0, 3)
            .reshape(rows_w, -1)
            .astype(f32)
        )

    grad_s_gate = ff_restore(grad_s_cols[:, :, :ff_pad])
    grad_s_up = ff_restore(grad_s_cols[:, :, ff_pad:])

    grad_f = grad_out.astype(f32)
    grad_resid_norm, grad_f_gain = second_norm_back(grad_second)
    grad_resid = grad_f + grad_resid_norm
    grad_attn_out = grad_resid.astype(bf16)
    grad_w_out = lax.psum_scatter(
        dot_first(attn_own, grad_attn_out).astype(bf16), "dp", scatter_dimension=0, tiled=True
    )
    grad_w_out = lax.psum_scatter(
        grad_w_out, "expert", scatter_dimension=0, tiled=True
    ).astype(f32)
    grad_attended = dot_last(grad_attn_out, wo).astype(bf16)
    grad_heads = lax.all_to_all(grad_attended, "expert", split_axis=1, concat_axis=0, tiled=True)
    delta = jnp.sum(
        (grad_heads.astype(f32) * attended).reshape(tree, mine, VD), axis=-1
    ).T
    grad_q, grad_kv, grad_krope = attend_back(
        reach, q_att, k_att, v_att, grad_heads, log_total, delta, scale
    )
    grad_w_exp = dot_first(ckv, grad_kv)
    lat_part = (
        jnp.concatenate([dot_last(grad_kv, we), grad_krope], axis=1)
        .astype(bf16)
        .reshape(group, tok_dev, -1)
    )
    grad_lat_sum = reduce_rows(lat_part, 5)

    def latent_parts(latent_in, gain_vec):
        return (
            norm_rows(latent_in[:, :KV], gain_vec),
            rotate(latent_in[:, KV:], own(cos_table), own(sin_table)),
        )

    unused, latent_back = jax.vjp(latent_parts, own(latent), l_gain)
    grad_latent, grad_l_gain = latent_back(
        (grad_lat_sum[:, :KV], grad_lat_sum[:, KV : KV + ROPE])
    )
    grad_latent = grad_latent.astype(bf16)
    grad_w_lat = dot_first(own(h1), grad_latent)
    grad_gains = jnp.stack(
        [
            grad_f_gain,
            jnp.pad(grad_l_gain.reshape(-1, rows_l), ((0, 0), (0, rows_w - rows_l))).reshape(width),
        ],
        axis=1,
    )
    lat_grads = lax.psum_scatter(
        jnp.concatenate(
            [grad_w_lat, jnp.pad(grad_gains, ((0, 0), (0, ROPE - 2)))], axis=1
        ).astype(bf16),
        EVERY,
        scatter_dimension=0,
        tiled=True,
    ).astype(f32)
    grad_w_lat = lat_grads[:, :lat_w]
    grad_f_gain = lat_grads[:, lat_w]
    grad_l_gain = lat_grads[:rows_l, lat_w + 1]

    grad_q_lin = (
        query_rope_back((grad_q * scale).reshape(tree, mine, KEY)).astype(bf16).reshape(tree, q_own)
    )
    grad_a_cols = jnp.concatenate(
        [dot_first(h1, grad_q_lin), grad_w_exp.reshape(width, e_fold)], axis=1
    ).astype(bf16)
    grad_a_cols = spread_columns(grad_a_cols)
    grad_w_q = (
        grad_a_cols[:, :, :q_own]
        .reshape(group, rows_w, mine, KEY)[..., : NOPE + ROPE]
        .transpose(1, 0, 2, 3)
        .reshape(rows_w, -1)
        .astype(f32)
    )
    grad_w_exp = (
        grad_a_cols[:, :, q_own:]
        .reshape(group, rows_l, e_own)
        .transpose(1, 0, 2)
        .reshape(rows_l, -1)
        .astype(f32)
    )
    grad_a_gain = (
        jnp.sum(grad_w_q * w_query.astype(f32), axis=1)
        + jnp.sum(grad_w_lat * w_latent.astype(f32), axis=1)
    ) / attn_gain.astype(f32)

    first_part = dot_last(grad_q_lin, wq).astype(bf16).reshape(group, tok_dev, width)
    grad_first = reduce_rows(first_part, 6) + dot_last(grad_latent, wl)
    unused, first_norm_back = jax.vjp(
        lambda v: norm_rows(v, a_gain), tokens_f
    )
    (grad_tokens_norm,) = first_norm_back(grad_first)
    grad_tokens = grad_resid + grad_tokens_norm
    return (
        block_out,
        grad_tokens,
        grad_a_gain,
        grad_w_q,
        grad_w_lat,
        grad_l_gain,
        grad_w_exp,
        grad_w_out,
        grad_f_gain,
        grad_s_gate,
        grad_s_up,
        grad_s_down.astype(f32),
        grad_e_gate.astype(f32)[None],
        grad_e_up.astype(f32)[None],
        grad_e_down.astype(f32)[None],
    )


def solution(mesh):
    placed = (
        P(EVERY, None),
        P(EVERY, None),
        P(EVERY, None),
        P(EVERY, None),
        P("dp", None),
        P(EVERY),
        P(EVERY, None),
        P(EVERY, None),
        P(EVERY),
        P(EVERY, None),
        P(EVERY, None),
        P(EVERY),
        P(EVERY, None),
        P(EVERY, None),
        P(EVERY, None),
        P("expert", None, None),
        P("expert", None, None),
        P("expert", None, None),
    )
    return jax.shard_map(
        per_device,
        mesh=mesh,
        in_specs=placed,
        out_specs=(
            P(EVERY, None),
            P(EVERY, None),
            P(EVERY),
            P(EVERY, None),
            P(EVERY, None),
            P(EVERY),
            P(EVERY, None),
            P(EVERY, None),
            P(EVERY),
            P(EVERY, None),
            P(EVERY, None),
            P(EVERY, None),
            P("expert", "dp", None),
            P("expert", "dp", None),
            P("expert", None, "dp"),
        ),
        check_vma=False,
    )
```

```python
import functools

import jax
import jax.numpy as jnp
from jax import lax
from jax.experimental import pallas as pl
from jax.experimental.pallas import tpu as pltpu
from jax.sharding import PartitionSpec as P

HEADS = 16
NOPE = 128
ROPE = 64
KV = 512
VD = 128
SEG = 256
KEY = 256

epsilon = 1e-06
bf16 = jnp.bfloat16
f32 = jnp.float32
EVERY = ("dp", "expert")
MESH = pl.DeviceIdType.MESH
VMEM_LIMIT = 60 << 20
WIRE = pl.CostEstimate(flops=0, bytes_accessed=300_000_000, transcendentals=0)


def norm_rows(values, gain_vec):
    return (
        values * lax.rsqrt(jnp.mean(values * values, axis=-1, keepdims=True) + epsilon) * gain_vec
    )


def rotate(values, cos_table, sin_table):
    half_width = values.shape[-1] // 2
    first_half = values[..., :half_width]
    second_half = values[..., half_width:]
    return jnp.concatenate(
        [
            first_half * cos_table - second_half * sin_table,
            second_half * cos_table + first_half * sin_table,
        ],
        axis=-1,
    )


def gating(gate_part, up_part):
    return jax.nn.silu(gate_part) * up_part


def ancestry(parent_row, seg_count):
    identity = jnp.eye(seg_count, dtype=f32)
    parent_hot = (parent_row[:, None] == jnp.arange(seg_count, dtype=jnp.int32)[None, :]).astype(
        f32
    )
    reachable = identity
    for _ in range(seg_count - 1):
        reachable = jnp.maximum(identity, jnp.dot(parent_hot, reachable))
    return reachable


def matmul(left, right):
    return jnp.dot(left, right, preferred_element_type=f32)


def dot_last(left, right):
    return lax.dot_general(left, right, (((1,), (1,)), ((), ())), preferred_element_type=f32)


def dot_first(left, right):
    return lax.dot_general(left, right, (((0,), (0,)), ((), ())), preferred_element_type=f32)


def greet(rank, last):
    barrier = pltpu.get_barrier_semaphore()
    a = rank // 2

    def hail(other):
        pl.semaphore_signal(barrier, inc=1, device_id={"expert": other}, device_id_type=MESH)

    hail(rank + 1 - 2 * (rank % 2))

    @pl.when(a < last)
    def _():
        hail(rank + 2)

    @pl.when(a > 0)
    def _():
        hail(rank - 2)

    pl.semaphore_wait(barrier, 1 + (a + last - 1) // last + (2 * last - 1 - a) // last)


class Chain:
    def __init__(self, chunks, x_ref, o_ref, sx, rx, su, ru, sd, rd):
        self.chunks, self.x, self.o = chunks, x_ref, o_ref
        self.sems = (sx, rx, su, ru, sd, rd)
        self.rank = lax.axis_index("expert")
        self.last = o_ref.shape[0] // 2 - 1
        self.a = self.rank // 2
        self.side = self.rank + 1 - 2 * (self.rank % 2)
        self.rows = x_ref.shape[0] // chunks

    def piece(self, ref, c):
        return ref.at[pl.ds(c * self.rows, self.rows)]

    def to(self, src, block, c, send, recv, target):
        return pltpu.make_async_remote_copy(
            src_ref=src,
            dst_ref=self.piece(self.o.at[block], c),
            send_sem=send,
            recv_sem=recv,
            device_id={"expert": target},
            device_id_type=MESH,
        )

    def start(self):
        sx, rx, su, ru, sd, rd = self.sems
        rank, a, last, to = self.rank, self.a, self.last, self.to
        for c in range(self.chunks):
            own = self.piece(self.x, c)
            to(own, rank, c, sx.at[0, c], rx.at[0, c], self.side).start()

            @pl.when(a < last)
            def _():
                to(own, rank, c, su.at[0, c], ru.at[0, c], rank + 2).start()

            @pl.when(a > 0)
            def _():
                to(own, rank, c, sd.at[0, c], rd.at[0, c], rank - 2).start()

    def step(self, s):
        sx, rx, su, ru, sd, rd = self.sems
        rank, a, last, to = self.rank, self.a, self.last, self.to
        for c in range(self.chunks):

            @pl.when(a >= s)
            def _():
                block = rank - 2 * s
                src = self.piece(self.o.at[block], c)
                to(src, block, c, su.at[s - 1, c], ru.at[s - 1, c], rank + 2).wait_recv()
                to(src, block, c, sx.at[s, c], rx.at[s, c], self.side).start()

                @pl.when(a < last)
                def _():
                    to(src, block, c, su.at[s, c], ru.at[s, c], rank + 2).start()

            @pl.when(a + s <= last)
            def _():
                block = rank + 2 * s
                src = self.piece(self.o.at[block], c)
                to(src, block, c, sd.at[s - 1, c], rd.at[s - 1, c], rank - 2).wait_recv()
                to(src, block, c, sx.at[last + s, c], rx.at[last + s, c], self.side).start()

                @pl.when(a > 0)
                def _():
                    to(src, block, c, sd.at[s, c], rd.at[s, c], rank - 2).start()

    def finish(self):
        sx, rx, su, ru, sd, rd = self.sems
        rank, a, last, to, side = self.rank, self.a, self.last, self.to, self.side
        for c in range(self.chunks):
            own = self.piece(self.x, c)
            to(own, side, c, sx.at[0, c], rx.at[0, c], side).wait()

            @pl.when(a < last)
            def _():
                to(own, rank, c, su.at[0, c], ru.at[0, c], rank + 2).wait_send()

            @pl.when(a > 0)
            def _():
                to(own, rank, c, sd.at[0, c], rd.at[0, c], rank - 2).wait_send()

        for s in range(1, last + 1):
            for c in range(self.chunks):

                @pl.when(a >= s)
                def _():
                    block = rank - 2 * s
                    src = self.piece(self.o.at[block], c)
                    to(src, side - 2 * s, c, sx.at[s, c], rx.at[s, c], side).wait()

                    @pl.when(a < last)
                    def _():
                        to(src, block, c, su.at[s, c], ru.at[s, c], rank + 2).wait_send()

                @pl.when(a + s <= last)
                def _():
                    block = rank + 2 * s
                    src = self.piece(self.o.at[block], c)
                    to(src, side + 2 * s, c, sx.at[last + s, c], rx.at[last + s, c], side).wait()

                    @pl.when(a > 0)
                    def _():
                        to(src, block, c, sd.at[s, c], rd.at[s, c], rank - 2).wait_send()


def chain_sems(count, chunks):
    half = count // 2
    dma = pltpu.SemaphoreType.DMA
    return [dma((2 * half, chunks))] * 2 + [dma((half, chunks))] * 4


def gather_kernel(chunks, x_ref, o_ref, *sems):
    chain = Chain(chunks, x_ref, o_ref, *sems)
    greet(chain.rank, chain.last)
    chain.start()
    o_ref[chain.rank] = x_ref[...]
    for s in range(1, chain.last + 1):
        chain.step(s)
    chain.finish()


def prologue_kernel(
    chunks,
    x_ref,
    w_ref,
    d_ref,
    t_ref,
    o_ref,
    pk_ref,
    do_ref,
    to_ref,
    wa_s,
    wa_r,
    ta_s,
    ta_r,
    wp_s,
    wp_r,
    dp_s,
    dp_r,
    *sems,
):
    group, spread = o_ref.shape[0], pk_ref.shape[0]
    chain = Chain(chunks, x_ref, o_ref, *sems)
    rank, line = chain.rank, lax.axis_index("dp")
    barrier = pltpu.get_barrier_semaphore()
    for k in range(1, group):
        pl.semaphore_signal(
            barrier,
            inc=1,
            device_id={"expert": lax.rem(rank + k, group)},
            device_id_type=MESH,
        )
    for k in range(1, spread):
        pl.semaphore_signal(
            barrier, inc=1, device_id={"dp": lax.rem(line + k, spread)}, device_id_type=MESH
        )
    pl.semaphore_wait(barrier, group + spread - 2)

    def cut(k):
        peer = lax.rem(rank + k, group)
        return pltpu.make_async_remote_copy(
            src_ref=w_ref.at[peer],
            dst_ref=pk_ref.at[line, rank],
            send_sem=wa_s.at[k - 1],
            recv_sem=wa_r.at[k - 1],
            device_id={"expert": peer},
            device_id_type=MESH,
        )

    def gates(k):
        peer = lax.rem(rank + k, group)
        return pltpu.make_async_remote_copy(
            src_ref=t_ref.at[peer],
            dst_ref=to_ref.at[rank],
            send_sem=ta_s.at[k - 1],
            recv_sem=ta_r.at[k - 1],
            device_id={"expert": peer},
            device_id_type=MESH,
        )

    def along(src, dst, send, recv, k):
        return pltpu.make_async_remote_copy(
            src_ref=src,
            dst_ref=dst,
            send_sem=send.at[k - 1],
            recv_sem=recv.at[k - 1],
            device_id={"dp": lax.rem(line + k, spread)},
            device_id_type=MESH,
        )

    for k in range(1, group):
        cut(k).start()
        gates(k).start()
    chain.start()
    for k in range(1, spread):
        along(d_ref, do_ref.at[line], dp_s, dp_r, k).start()
    pk_ref[line, rank] = w_ref[rank]
    do_ref[line] = d_ref[...]
    to_ref[rank] = t_ref[rank]
    o_ref[rank] = x_ref[...]
    for k in range(1, group):
        cut(k).wait_recv()
    for k in range(1, spread):
        along(pk_ref.at[line], pk_ref.at[line], wp_s, wp_r, k).start()
    for s in range(1, chain.last + 1):
        chain.step(s)
    chain.finish()
    for k in range(1, group):
        cut(k).wait_send()
        gates(k).wait()
    for k in range(1, spread):
        along(d_ref, do_ref.at[line], dp_s, dp_r, k).wait()
        along(pk_ref.at[line], pk_ref.at[line], wp_s, wp_r, k).wait()


def prologue(x, cuts, down, gates, spread, call_id, chunks=2):
    group = cuts.shape[0]
    dma = pltpu.SemaphoreType.DMA
    vmem = pl.BlockSpec(memory_space=pltpu.VMEM)
    return pl.pallas_call(
        functools.partial(prologue_kernel, chunks),
        out_shape=[
            jax.ShapeDtypeStruct((group,) + x.shape, x.dtype),
            jax.ShapeDtypeStruct((spread,) + cuts.shape, cuts.dtype),
            jax.ShapeDtypeStruct((spread,) + down.shape, down.dtype),
            jax.ShapeDtypeStruct(gates.shape, gates.dtype),
        ],
        in_specs=[vmem] * 4,
        out_specs=[vmem] * 4,
        scratch_shapes=[dma((group - 1,))] * 4
        + [dma((spread - 1,))] * 4
        + chain_sems(group, chunks),
        compiler_params=pltpu.CompilerParams(
            collective_id=call_id, has_side_effects=True, vmem_limit_bytes=VMEM_LIMIT
        ),
        cost_estimate=WIRE,
        name="prologue",
    )(x, cuts, down, gates)


def gather_rows(x, count, call_id, chunks=2):
    return pl.pallas_call(
        functools.partial(gather_kernel, chunks),
        out_shape=jax.ShapeDtypeStruct((count,) + x.shape, x.dtype),
        in_specs=[pl.BlockSpec(memory_space=pltpu.VMEM)],
        out_specs=pl.BlockSpec(memory_space=pltpu.VMEM),
        scratch_shapes=chain_sems(count, chunks),
        compiler_params=pltpu.CompilerParams(
            collective_id=call_id, has_side_effects=True, vmem_limit_bytes=VMEM_LIMIT
        ),
        cost_estimate=WIRE,
        name="gather_rows",
    )(x)


def ring_pairs(group):
    half = group // 2
    side = [(r, r + 1 - 2 * (r % 2)) for r in range(group)]
    onward = [(2 * a + b, 2 * ((a + 1) % half) + b) for a in range(half) for b in range(2)]
    return side, onward


def tie(*values):
    return lax.optimization_barrier(values)


def reduce_kernel(chunks, p_ref, o_ref, rx, st, ru, rd, acc, sxs, rxs, sus, rus, sds, rds):
    rank = lax.axis_index("expert")
    last = p_ref.shape[0] // 2 - 1
    a = rank // 2
    b = rank % 2
    rows = p_ref.shape[1] // chunks
    greet(rank, last)
    h = a // 2
    order = [3 - 3 * h, 2 - h, 4 * h + 1 - a, a]

    def cut(ref, c):
        return ref.at[pl.ds(c * rows, rows)]

    def copy(src, dst, send, recv, target):
        return pltpu.make_async_remote_copy(
            src_ref=src,
            dst_ref=dst,
            send_sem=send,
            recv_sem=recv,
            device_id={"expert": target},
            device_id_type=MESH,
        )

    def across(t, c):
        return copy(
            cut(p_ref.at[2 * t + 1 - b], c),
            cut(rx.at[t], c),
            sxs.at[t, c],
            rxs.at[t, c],
            rank + 1 - 2 * b,
        )

    def upward(t, c):
        return copy(cut(st.at[t], c), cut(ru.at[t], c), sus.at[t, c], rus.at[t, c], rank + 2)

    def downward(t, c):
        return copy(cut(st.at[t], c), cut(rd.at[t], c), sds.at[t, c], rds.at[t, c], rank - 2)

    for t in order:
        for c in range(chunks):
            across(t, c).start()
    for t in order:
        for c in range(chunks):
            across(t, c).wait_recv()
            acc[...] = cut(p_ref.at[2 * t + b], c)[...].astype(f32) + cut(rx.at[t], c)[...].astype(
                f32
            )

            @pl.when((t >= a) & (a > 0))
            def _():
                upward(t, c).wait_recv()
                acc[...] += cut(ru.at[t], c)[...].astype(f32)

            @pl.when((t <= a) & (a < last))
            def _():
                downward(t, c).wait_recv()
                acc[...] += cut(rd.at[t], c)[...].astype(f32)

            @pl.when(t == a)
            def _():
                cut(o_ref, c)[...] = acc[...]

            @pl.when(t > a)
            def _():
                cut(st.at[t], c)[...] = acc[...].astype(st.dtype)
                upward(t, c).start()

            @pl.when(t < a)
            def _():
                cut(st.at[t], c)[...] = acc[...].astype(st.dtype)
                downward(t, c).start()

    for t in order:
        for c in range(chunks):
            across(t, c).wait_send()

            @pl.when(t > a)
            def _():
                upward(t, c).wait_send()

            @pl.when(t < a)
            def _():
                downward(t, c).wait_send()


def reduce_rows(p, call_id, chunks=4):
    count, rows, width = p.shape
    half = count // 2
    buf = pltpu.VMEM((half, rows, width), p.dtype)
    sem = pltpu.SemaphoreType.DMA((half, chunks))
    return pl.pallas_call(
        functools.partial(reduce_kernel, chunks),
        out_shape=jax.ShapeDtypeStruct((rows, width), f32),
        in_specs=[pl.BlockSpec(memory_space=pltpu.VMEM)],
        out_specs=pl.BlockSpec(memory_space=pltpu.VMEM),
        scratch_shapes=[buf] * 4 + [pltpu.VMEM((rows // chunks, width), f32)] + [sem] * 6,
        compiler_params=pltpu.CompilerParams(
            collective_id=call_id, has_side_effects=True, vmem_limit_bytes=VMEM_LIMIT
        ),
        cost_estimate=WIRE,
        name="reduce_rows",
    )(p)


def swap_halves(values):
    lane = lax.broadcasted_iota(jnp.int32, values.shape, 1)
    half = ROPE // 2
    return jnp.where(lane < half, pltpu.roll(values, KEY - NOPE - half, 1), pltpu.roll(values, half, 1))


def turns(seg_cos, seg_sin, off_cos, off_sin):
    lane = lax.broadcasted_iota(jnp.int32, off_cos.shape, 1)
    sine = seg_sin * off_cos + seg_cos * off_sin
    return seg_cos * off_cos - seg_sin * off_sin, jnp.where(lane < ROPE // 2, -sine, sine)


def project_kernel(
    heads,
    x_ref,
    wq_ref,
    wl_ref,
    we_ref,
    ag_ref,
    lg_ref,
    sc_ref,
    ss_ref,
    oc_ref,
    os_ref,
    h1_ref,
    q_ref,
    k_ref,
    v_ref,
    lat_ref,
    ckv_ref,
):
    i = pl.program_id(0)
    x = x_ref[...].astype(f32)
    power = jnp.mean(x * x, axis=-1, keepdims=True)
    h1 = (x * lax.rsqrt(power + epsilon) * ag_ref[...]).astype(bf16)
    h1_ref[...] = h1
    cosine, sine = turns(sc_ref[pl.ds(i, 1)], ss_ref[pl.ds(i, 1)], oc_ref[...], os_ref[...])

    def turn(values):
        return (values * cosine + swap_halves(values) * sine).astype(bf16)

    query = matmul(h1, wq_ref[...])
    for h in range(heads):
        at = h * KEY
        q_ref[:, at : at + NOPE] = query[:, at : at + NOPE].astype(bf16)
        q_ref[:, at + NOPE : at + KEY] = turn(query[:, at + NOPE : at + KEY])
    latent = matmul(h1, wl_ref[...])
    lat_ref[...] = latent
    low = latent[:, :KV]
    power = jnp.mean(low * low, axis=-1, keepdims=True)
    ckv = (low * lax.rsqrt(power + epsilon) * lg_ref[...]).astype(bf16)
    ckv_ref[...] = ckv
    krope = turn(latent[:, KV:])
    kv = matmul(ckv, we_ref[...]).astype(bf16)
    for h in range(heads):
        at = h * KEY
        k_ref[:, at : at + NOPE] = kv[:, at : at + NOPE]
        k_ref[:, at + NOPE : at + KEY] = krope
        v_ref[:, h * VD : (h + 1) * VD] = kv[:, at + NOPE : at + KEY]


def project(x, packed, lat_pack, we, a_gain, l_gain, tables, heads):
    tree, width = x.shape
    segs = tree // SEG
    lat_width = lat_pack.shape[1]
    fixed = lambda arr: pl.BlockSpec(arr.shape, lambda i: (0, 0))
    part = lambda cols: pl.BlockSpec((SEG, cols), lambda i: (i, 0))
    return pl.pallas_call(
        functools.partial(project_kernel, heads),
        grid=(segs,),
        in_specs=[
            part(width),
            pl.BlockSpec((width, heads * KEY), lambda i: (0, 0)),
            fixed(lat_pack),
            fixed(we),
            fixed(a_gain),
            fixed(l_gain),
        ]
        + [fixed(table) for table in tables],
        out_specs=[
            part(width),
            part(heads * KEY),
            part(heads * KEY),
            part(heads * VD),
            part(lat_width),
            part(KV),
        ],
        out_shape=[
            jax.ShapeDtypeStruct((tree, width), bf16),
            jax.ShapeDtypeStruct((tree, heads * KEY), bf16),
            jax.ShapeDtypeStruct((tree, heads * KEY), bf16),
            jax.ShapeDtypeStruct((tree, heads * VD), bf16),
            jax.ShapeDtypeStruct((tree, lat_width), f32),
            jax.ShapeDtypeStruct((tree, KV), bf16),
        ],
        compiler_params=pltpu.CompilerParams(vmem_limit_bytes=VMEM_LIMIT),
        cost_estimate=pl.CostEstimate(flops=0, bytes_accessed=60_000_000, transcendentals=0),
        name="project",
    )(x, packed, lat_pack, we, a_gain, l_gain, *tables)


def triangle():
    keys = lax.broadcasted_iota(jnp.int32, (SEG, SEG), 0)
    queries = lax.broadcasted_iota(jnp.int32, (SEG, SEG), 1)
    return keys <= queries


def attend_kernel(
    heads, segs, scale, reach_ref, q_ref, k_ref, v_ref, out_ref, full_ref, log_ref, m_s, l_s, acc_s
):
    i = pl.program_id(0)
    diag = triangle()

    def score(h, j):
        keys = k_ref[pl.ds(j * SEG, SEG), h * KEY : (h + 1) * KEY]
        return dot_last(keys, q_ref[:, h * KEY : (h + 1) * KEY]) * scale

    def weigh(h, j, weights):
        vals = v_ref[pl.ds(j * SEG, SEG), h * VD : (h + 1) * VD]
        return dot_first(vals, weights.astype(bf16))

    for h in range(heads):
        s = jnp.where(diag, score(h, i), -1e30)
        top = jnp.max(s, axis=0, keepdims=True)
        w = jnp.where(diag, jnp.exp(s - top), 0.0)
        m_s[h : h + 1] = top
        l_s[h : h + 1] = jnp.sum(w, axis=0, keepdims=True)
        acc_s[h] = weigh(h, i, w)

    def step(j, carry):
        @pl.when(reach_ref[i * segs + j] > 0)
        def _():
            for h in range(heads):
                s = score(h, j)
                old = m_s[h : h + 1]
                top = jnp.maximum(old, jnp.max(s, axis=0, keepdims=True))
                w = jnp.exp(s - top)
                fade = jnp.exp(old - top)
                m_s[h : h + 1] = top
                l_s[h : h + 1] = l_s[h : h + 1] * fade + jnp.sum(w, axis=0, keepdims=True)
                acc_s[h] = acc_s[h] * fade + weigh(h, j, w)

        return carry

    lax.fori_loop(0, i, step, 0)
    for h in range(heads):
        total = l_s[h : h + 1]
        rows = (acc_s[h] * (1.0 / total)).T
        full_ref[:, h * VD : (h + 1) * VD] = rows
        out_ref[:, h * VD : (h + 1) * VD] = rows.astype(bf16)
        log_ref[h : h + 1] = m_s[h : h + 1] + jnp.log(total)


def attend(reach, q, k, v, scale):
    tree = q.shape[0]
    segs = tree // SEG
    heads = q.shape[1] // KEY
    whole = lambda width: pl.BlockSpec((tree, width), lambda i, r: (0, 0))
    part = lambda width: pl.BlockSpec((SEG, width), lambda i, r: (i, 0))
    return pl.pallas_call(
        functools.partial(attend_kernel, heads, segs, scale),
        grid_spec=pltpu.PrefetchScalarGridSpec(
            num_scalar_prefetch=1,
            grid=(segs,),
            in_specs=[part(heads * KEY), whole(heads * KEY), whole(heads * VD)],
            out_specs=[
                part(heads * VD),
                part(heads * VD),
                pl.BlockSpec((heads, SEG), lambda i, r: (0, i)),
            ],
            scratch_shapes=[
                pltpu.VMEM((heads, SEG), f32),
                pltpu.VMEM((heads, SEG), f32),
                pltpu.VMEM((heads, VD, SEG), f32),
            ],
        ),
        out_shape=[
            jax.ShapeDtypeStruct((tree, heads * VD), bf16),
            jax.ShapeDtypeStruct((tree, heads * VD), f32),
            jax.ShapeDtypeStruct((heads, tree), f32),
        ],
        compiler_params=pltpu.CompilerParams(vmem_limit_bytes=VMEM_LIMIT),
        cost_estimate=pl.CostEstimate(flops=0, bytes_accessed=70_000_000, transcendentals=0),
        name="attend",
    )(reach, q, k, v)


def attend_back_kernel(
    heads,
    segs,
    scale,
    reach_ref,
    q_ref,
    k_ref,
    v_ref,
    g_ref,
    att_ref,
    log_ref,
    we_ref,
    sc_ref,
    ss_ref,
    oc_ref,
    os_ref,
    gq_ref,
    dkv_ref,
    lat_ref,
    dq_s,
    dk_s,
    dv_s,
    delta_s,
):
    j = pl.program_id(0)
    diag = triangle()

    @pl.when(j == 0)
    def _():
        def prepare(i, carry):
            rows = pl.ds(i * SEG, SEG)
            for h in range(heads):
                vcols = slice(h * VD, (h + 1) * VD)
                both = g_ref[rows, vcols].astype(f32) * att_ref[rows, vcols]
                delta_s[h : h + 1, rows] = jnp.sum(both.T, axis=0, keepdims=True)
            dq_s[rows] = jnp.zeros((SEG, heads * KEY), f32)
            return carry

        lax.fori_loop(0, segs, prepare, 0)

    dk_s[...] = jnp.zeros_like(dk_s)
    dv_s[...] = jnp.zeros_like(dv_s)

    def block(i, masked):
        rows = pl.ds(i * SEG, SEG)
        for h in range(heads):
            kcols = slice(h * KEY, (h + 1) * KEY)
            vcols = slice(h * VD, (h + 1) * VD)
            q = q_ref[rows, kcols]
            k = k_ref[:, kcols]
            g = g_ref[rows, vcols]
            s = dot_last(k, q) * scale
            w = jnp.exp(s - log_ref[h : h + 1, rows])
            if masked:
                w = jnp.where(diag, w, 0.0)
            dw = dot_last(v_ref[:, vcols], g)
            ds = (w * (dw - delta_s[h : h + 1, rows])).astype(bf16)
            dv_s[h] += matmul(w.astype(bf16), g)
            dk_s[h] += matmul(ds, q)
            dq_s[rows, kcols] += dot_first(ds, k)

    block(j, True)

    def step(i, carry):
        @pl.when(reach_ref[i * segs + j] > 0)
        def _():
            block(i, False)

        return carry

    lax.fori_loop(j + 1, segs, step, 0)
    rope = jnp.zeros((SEG, KEY - NOPE), f32)
    for h in range(heads):
        dkv_ref[:, h * KEY : h * KEY + NOPE] = (dk_s[h, :, :NOPE] * scale).astype(bf16)
        dkv_ref[:, h * KEY + NOPE : (h + 1) * KEY] = dv_s[h].astype(bf16)
        rope = rope + dk_s[h, :, NOPE:]
    lat_ref[:, :KV] = dot_last(dkv_ref[...], we_ref[...]).astype(bf16)
    lat_ref[:, KV:] = (rope * scale).astype(bf16)

    @pl.when(j == segs - 1)
    def _():
        def finish(i, carry):
            rows = pl.ds(i * SEG, SEG)
            cosine, sine = turns(
                sc_ref[pl.ds(i, 1)], ss_ref[pl.ds(i, 1)], oc_ref[...], os_ref[...]
            )
            for h in range(heads):
                at = h * KEY
                gq_ref[rows, at : at + NOPE] = (dq_s[rows, at : at + NOPE] * scale).astype(bf16)
                turned = dq_s[rows, at + NOPE : at + KEY] * scale
                gq_ref[rows, at + NOPE : at + KEY] = (
                    turned * cosine - swap_halves(turned) * sine
                ).astype(bf16)
            return carry

        lax.fori_loop(0, segs, finish, 0)


def attend_back(reach, q, k, v, g, attended, log_total, we, tables, scale):
    tree = q.shape[0]
    segs = tree // SEG
    heads = q.shape[1] // KEY
    whole = lambda width: pl.BlockSpec((tree, width), lambda j, r: (0, 0))
    part = lambda width: pl.BlockSpec((SEG, width), lambda j, r: (j, 0))
    fixed = lambda arr: pl.BlockSpec(arr.shape, lambda j, r: (0, 0))
    lat_width = KV + KEY - NOPE
    return pl.pallas_call(
        functools.partial(attend_back_kernel, heads, segs, scale),
        grid_spec=pltpu.PrefetchScalarGridSpec(
            num_scalar_prefetch=1,
            grid=(segs,),
            in_specs=[
                whole(heads * KEY),
                part(heads * KEY),
                part(heads * VD),
                whole(heads * VD),
                whole(heads * VD),
                fixed(log_total),
                fixed(we),
            ]
            + [fixed(table) for table in tables],
            out_specs=[whole(heads * KEY), part(heads * KEY), part(lat_width)],
            scratch_shapes=[
                pltpu.VMEM((tree, heads * KEY), f32),
                pltpu.VMEM((heads, SEG, KEY), f32),
                pltpu.VMEM((heads, SEG, VD), f32),
                pltpu.VMEM((heads, tree), f32),
            ],
        ),
        out_shape=[
            jax.ShapeDtypeStruct((tree, heads * KEY), bf16),
            jax.ShapeDtypeStruct((tree, heads * KEY), bf16),
            jax.ShapeDtypeStruct((tree, lat_width), bf16),
        ],
        compiler_params=pltpu.CompilerParams(vmem_limit_bytes=VMEM_LIMIT),
        cost_estimate=pl.CostEstimate(flops=0, bytes_accessed=90_000_000, transcendentals=0),
        name="attend_back",
    )(reach, q, k, v, g, attended, log_total, we, *tables)


def per_device(
    tokens,
    grad_out,
    routes,
    gate_values,
    parents,
    attn_gain,
    w_query,
    w_latent,
    latent_gain,
    w_expand,
    w_output,
    ffn_gain,
    shared_gate,
    shared_up,
    shared_down,
    expert_gate,
    expert_up,
    expert_down,
):
    group = lax.axis_size("expert")
    spread = lax.axis_size("dp")
    rank = lax.axis_index("expert")
    tok_dev, width = tokens.shape
    tree = tok_dev * group
    segs = parents.shape[1]
    per_token = routes.shape[1]
    capacity = tok_dev * per_token * 9 // (8 * group)
    slots = -(-capacity // 16) * 16
    scale = (NOPE + ROPE) ** (-0.5)
    mine = HEADS // group
    rows_w = w_query.shape[0]
    rows_l = w_expand.shape[0]
    ff_cut = shared_down.shape[0]
    ff_own = ff_cut * spread
    ff_pad = -(-ff_own // 128) * 128
    q_own = mine * KEY
    e_own = mine * (NOPE + VD)
    e_fold = rows_l * e_own // rows_w

    wq_cut = jnp.pad(
        w_query.reshape(rows_w, group, mine, NOPE + ROPE),
        ((0, 0), (0, 0), (0, 0), (0, KEY - NOPE - ROPE)),
    ).reshape(rows_w, group, q_own)

    def ff_columns(weight):
        cut = weight.reshape(rows_w, spread, group, ff_cut).transpose(0, 2, 1, 3)
        return jnp.pad(
            cut.reshape(rows_w, group, ff_own), ((0, 0), (0, 0), (0, ff_pad - ff_own))
        )

    we_cut = (
        w_expand.reshape(rows_l, group, e_own).transpose(1, 0, 2).reshape(group, rows_w, e_fold)
    )
    packed = jnp.concatenate(
        [
            wq_cut.transpose(1, 0, 2),
            we_cut,
            ff_columns(shared_gate).transpose(1, 0, 2),
            ff_columns(shared_up).transpose(1, 0, 2),
        ],
        axis=2,
    )
    expert_ids = jnp.arange(group, dtype=jnp.int32)
    gate_of = jnp.sum(
        jnp.where(routes[:, :, None] == expert_ids[None, None, :], gate_values[:, :, None], 0.0),
        axis=1,
    ).T
    gate_of = jnp.broadcast_to(gate_of[:, None, :], (group, 8, tok_dev))
    x_all, packed, sd, gate_of = prologue(tokens, packed, shared_down, gate_of, spread, 0)
    x_all, parents, gate_of = lax.optimization_barrier(
        (x_all.reshape(tree, width), parents, gate_of[:, 0])
    )
    packed = packed.reshape(width, -1)
    wq = packed[:, :q_own]
    we = packed[:, q_own : q_own + e_fold].reshape(KV, e_own)
    sg = packed[:, q_own + e_fold : q_own + e_fold + ff_pad]
    su = packed[:, q_own + e_fold + ff_pad :]
    sd = jnp.pad(sd.reshape(ff_own, width), ((0, ff_pad - ff_own), (0, 0)))

    lat_w = KV + ROPE
    gains = jnp.stack(
        [attn_gain, ffn_gain, jnp.pad(latent_gain, (0, rows_w - rows_l))], axis=1
    )
    gains = jnp.pad(gains, ((0, 0), (0, ROPE - 3)))
    lat_pack = lax.all_gather(
        jnp.concatenate([w_latent, gains], axis=1), EVERY, axis=0, tiled=True
    )
    wl = lat_pack[:, :lat_w]
    a_gain = lat_pack[:, lat_w].astype(f32)
    f_gain = lat_pack[:, lat_w + 1].astype(f32)
    l_gain = lat_pack[:, lat_w + 2].reshape(-1, rows_w)[:, :rows_l].reshape(KV).astype(f32)
    wo = lax.all_gather(w_output, EVERY, axis=0, tiled=True)
    reachable = ancestry(parents[0], segs)
    depth = jnp.sum(reachable, axis=1) - 1.0
    reach = reachable.astype(jnp.int32).reshape(segs * segs)
    half_width = ROPE // 2
    freq = 10000.0 ** (-2.0 * jnp.arange(half_width, dtype=f32) / ROPE)
    seg_angle = (depth * SEG)[:, None] * freq[None, :]
    off_angle = jnp.arange(SEG, dtype=f32)[:, None] * freq[None, :]

    def lanes(values):
        return jnp.pad(
            jnp.concatenate([values, values], axis=1), ((0, 0), (0, KEY - NOPE - ROPE))
        )

    tables = [
        lanes(jnp.cos(seg_angle)),
        lanes(jnp.sin(seg_angle)),
        lanes(jnp.cos(off_angle)),
        lanes(jnp.sin(off_angle)),
    ]
    seg_cos = lax.dynamic_slice_in_dim(tables[0], rank, 1, 0)[:, :half_width]
    seg_sin = lax.dynamic_slice_in_dim(tables[1], rank, 1, 0)[:, :half_width]
    off_cos = tables[2][:, :half_width]
    off_sin = tables[3][:, :half_width]
    own_cos = seg_cos * off_cos - seg_sin * off_sin
    own_sin = seg_sin * off_cos + seg_cos * off_sin

    def own(values):
        return lax.dynamic_slice_in_dim(values, rank * tok_dev, tok_dev, 0)

    h1, q_att, k_att, v_att, latent, ckv = project(
        x_all, packed, lat_pack, we, a_gain[None], l_gain[None], tables, mine
    )
    side, ring = ring_pairs(group)

    def across(values):
        return lax.ppermute(values, "expert", side)

    def onward(values):
        return lax.ppermute(values, "expert", ring)

    def sum_with(mine, *others):
        total = mine.astype(f32)
        for other in others:
            total = total + other.astype(f32)
        return total

    q_att, g0 = tie(q_att, grad_out)
    g1, g0_side = onward(g0), across(g0)
    attn_heads, attended, log_total = attend(reach, q_att, k_att, v_att, scale)
    attn_heads, g1, g0_side = tie(attn_heads, g1, g0_side)
    g2, g1_side = onward(g1), across(g1)
    attn_own = lax.all_to_all(attn_heads, "expert", split_axis=0, concat_axis=1, tiled=True)
    attn_own, g2, g1_side = tie(attn_own, g2, g1_side)
    g3, g2_side = onward(g2), across(g2)
    tokens_f = tokens.astype(f32)
    resid = tokens_f + matmul(attn_own, wo)
    second_normed, second_norm_back = jax.vjp(norm_rows, resid, f_gain)
    h0, g3, g2_side = tie(second_normed.astype(bf16), g3, g2_side)

    half = group // 2
    h1_back, h0_side = tie(onward(h0), across(h0))
    h2_back, h1_side, g3_side = onward(h1_back), across(h1_back), across(g3)
    gate_of = jnp.concatenate(
        [
            lax.dynamic_slice_in_dim(
                gate_of, 2 * lax.rem(rank // 2 - s + half, half) + lax.rem(rank + k, 2), 1, 0
            )
            for s in range(half)
            for k in range(2)
        ],
        axis=0,
    )
    routed = gate_of > 0.0
    upto = (
        jnp.arange(tok_dev, dtype=jnp.int32)[:, None]
        <= jnp.arange(tok_dev, dtype=jnp.int32)[None, :]
    )
    place = matmul(routed.astype(bf16), upto.astype(bf16)).astype(jnp.int32) - 1
    chosen = (
        place[:, None, :] == jnp.arange(slots, dtype=jnp.int32)[None, :, None]
    ) & routed[:, None, :]
    pick_all = chosen.astype(bf16)
    gates_all = jnp.sum(jnp.where(chosen, gate_of[:, None, :], 0.0), axis=2)

    def experts(s, h2, g_rows):
        pick = pick_all[2 * s : 2 * s + 2]
        slot_gate = gates_all[2 * s : 2 * s + 2].reshape(2 * slots, 1)

        def take(rows):
            return jnp.einsum("bst,btd->bsd", pick, rows, preferred_element_type=f32).reshape(
                2 * slots, width
            )

        def give(rows):
            return jnp.einsum(
                "bst,bsd->btd", pick, rows.reshape(2, slots, width), preferred_element_type=f32
            ).reshape(2 * tok_dev, width)

        h2 = jnp.stack(h2)
        e_rows = take(h2).astype(bf16)
        activated, e_gating_back = jax.vjp(
            gating, matmul(e_rows, expert_gate[0]), matmul(e_rows, expert_up[0])
        )
        activated = activated.astype(bf16)
        e_result = (
            matmul(activated, expert_down[0]).astype(bf16).astype(f32) * slot_gate
        ).astype(bf16)
        h2 = h2.reshape(2 * tok_dev, width)
        s_act, s_gating_back = jax.vjp(gating, matmul(h2, sg), matmul(h2, su))
        s_act = s_act.astype(bf16)
        out_part = (matmul(s_act, sd) + give(e_result)).astype(bf16)

        g_rows = jnp.stack(g_rows)
        e_grad = (take(g_rows) * slot_gate).astype(bf16)
        g_rows = g_rows.reshape(2 * tok_dev, width)
        grad_e_act = dot_last(e_grad, expert_down[0]).astype(bf16)
        grad_gate_part, grad_up_part = e_gating_back(grad_e_act.astype(f32))
        grad_gate_part = grad_gate_part.astype(bf16)
        grad_up_part = grad_up_part.astype(bf16)
        grad_rows = (
            dot_last(grad_gate_part, expert_gate[0]) + dot_last(grad_up_part, expert_up[0])
        ).astype(bf16)
        grad_s_act = dot_last(g_rows, sd).astype(bf16)
        grad_s_gate_part, grad_s_up_part = s_gating_back(grad_s_act.astype(f32))
        grad_s_gate_part = grad_s_gate_part.astype(bf16)
        grad_s_up_part = grad_s_up_part.astype(bf16)
        second_part = (
            give(grad_rows) + dot_last(grad_s_gate_part, sg) + dot_last(grad_s_up_part, su)
        ).astype(bf16)
        return (
            out_part[:tok_dev],
            out_part[tok_dev:],
            second_part[:tok_dev],
            second_part[tok_dev:],
            (
                e_rows,
                activated,
                e_grad,
                grad_gate_part,
                grad_up_part,
                h2,
                s_act,
                g_rows,
                jnp.concatenate([grad_s_gate_part, grad_s_up_part], axis=1),
            ),
        )

    o0, o0_far, n0, n0_far, kept0 = experts(0, (h0, h0_side), (g0, g0_side))
    n0, h2_back, h1_side, g3_side = tie(n0, h2_back, h1_side, g3_side)
    h3_back, h2_side = onward(h2_back), across(h2_back)
    o1, o1_far, n1, n1_far, kept1 = experts(1, (h1_back, h1_side), (g1, g1_side))
    n1, n1_far, h3_back, h2_side = tie(n1, n1_far, h3_back, h2_side)
    h3_side, n1_in = across(h3_back), across(n1_far)
    o2, o2_far, n2, n2_far, kept2 = experts(2, (h2_back, h2_side), (g2, g2_side))
    n2, n2_far, h3_side, n1_in = tie(n2, n2_far, h3_side, n1_in)
    ring1, n2_in = onward(sum_with(n1, n1_in).astype(bf16)), across(n2_far)
    o3, o3_far, n3, n3_far, kept3 = experts(3, (h3_back, h3_side), (g3, g3_side))
    kept = [kept0, kept1, kept2, kept3]
    n3, n3_far, ring1, n2_in = tie(n3, n3_far, ring1, n2_in)
    ring2, n3_in = onward(sum_with(n2, n2_in, ring1).astype(bf16)), across(n3_far)
    e_rows, activated, e_grad, grad_gate_part, grad_up_part = (
        jnp.concatenate([pieces[k] for pieces in kept], axis=0) for k in range(5)
    )
    grad_e_gate = dot_first(e_rows, grad_gate_part).astype(bf16)
    grad_e_up = dot_first(e_rows, grad_up_part).astype(bf16)
    grad_e_gate, grad_e_up, ring2, n3_in, activated = tie(
        grad_e_gate, grad_e_up, ring2, n3_in, activated
    )
    ring3, n0_in = onward(sum_with(n3, n3_in, ring2).astype(bf16)), across(n0_far)
    grad_e_down = dot_first(activated, e_grad).astype(bf16)
    grad_s_down = sum(dot_first(pieces[6], pieces[7]) for pieces in kept).astype(bf16)
    grad_s_cols = sum(dot_first(pieces[5], pieces[8]) for pieces in kept).astype(bf16)
    grad_e_down, grad_s_down, grad_s_cols, ring3, n0_in, o1_far, o2_far, o3_far, o0_far = tie(
        grad_e_down, grad_s_down, grad_s_cols, ring3, n0_in, o1_far, o2_far, o3_far, o0_far
    )
    grad_second = sum_with(n0, n0_in, ring3)
    o1_in = across(o1_far)

    grad_e_gate = lax.psum_scatter(grad_e_gate, "dp", scatter_dimension=0, tiled=True)
    grad_e_up = lax.psum_scatter(grad_e_up, "dp", scatter_dimension=0, tiled=True)
    grad_e_down = lax.psum_scatter(grad_e_down, "dp", scatter_dimension=1, tiled=True)
    grad_s_down = lax.psum_scatter(grad_s_down[:ff_own], "dp", scatter_dimension=0, tiled=True)

    def sum_columns(grads):
        return lax.psum_scatter(grads, "dp", scatter_dimension=0, tiled=True)

    grad_s_cols = sum_columns(grad_s_cols)

    def ff_restore(cut):
        return (
            cut[:, :, :ff_own]
            .reshape(group, rows_w, spread, ff_cut)
            .transpose(1, 2, 0, 3)
            .reshape(rows_w, -1)
            .astype(f32)
        )

    grad_f = grad_out.astype(f32)
    grad_resid_norm, grad_f_gain = second_norm_back(grad_second)
    grad_resid = grad_f + grad_resid_norm
    grad_attn_out = grad_resid.astype(bf16)
    grad_w_out = dot_first(attn_own, grad_attn_out).astype(bf16)
    grad_attended = dot_last(grad_attn_out, wo).astype(bf16)
    grad_attended, grad_w_out, o1_in = tie(grad_attended, grad_w_out, o1_in)
    ring1, o2_in = onward(sum_with(o1, o1_in).astype(bf16)), across(o2_far)
    grad_heads = lax.all_to_all(grad_attended, "expert", split_axis=1, concat_axis=0, tiled=True)
    grad_heads, grad_e_gate, ring1, o2_in = tie(grad_heads, grad_e_gate, ring1, o2_in)
    ring2, o3_in = onward(sum_with(o2, o2_in, ring1).astype(bf16)), across(o3_far)
    grad_w_out = lax.psum_scatter(grad_w_out, "dp", scatter_dimension=0, tiled=True)
    grad_q_lin, grad_kv, lat_part = attend_back(
        reach, q_att, k_att, v_att, grad_heads, attended, log_total, we, tables, scale
    )
    lat_part, grad_e_up, ring2, o3_in = tie(lat_part, grad_e_up, ring2, o3_in)
    ring3, o0_in = onward(sum_with(o3, o3_in, ring2).astype(bf16)), across(o0_far)
    grad_w_exp = dot_first(ckv, grad_kv)
    lat_part = lat_part.reshape(group, tok_dev, -1)
    grad_lat_sum = reduce_rows(lat_part, 5, 2)
    grad_lat_sum, ring3, o0_in = tie(grad_lat_sum, ring3, o0_in)
    block_out = (resid + sum_with(o0, o0_in, ring3)).astype(bf16)

    def latent_parts(latent_in, gain_vec):
        return (
            norm_rows(latent_in[:, :KV], gain_vec),
            rotate(latent_in[:, KV : KV + ROPE], own_cos, own_sin),
        )

    unused, latent_back = jax.vjp(latent_parts, own(latent), l_gain)
    grad_latent, grad_l_gain = latent_back(
        (grad_lat_sum[:, :KV], grad_lat_sum[:, KV : KV + ROPE])
    )
    grad_latent = grad_latent.astype(bf16)
    grad_w_lat = dot_first(own(h1), grad_latent)[:, :KV + ROPE]
    grad_gains = jnp.stack(
        [
            grad_f_gain,
            jnp.pad(grad_l_gain.reshape(-1, rows_l), ((0, 0), (0, rows_w - rows_l))).reshape(width),
        ],
        axis=1,
    )
    lat_grads = lax.psum_scatter(
        jnp.concatenate(
            [grad_w_lat, jnp.pad(grad_gains, ((0, 0), (0, ROPE - 2)))], axis=1
        ).astype(bf16),
        "dp",
        scatter_dimension=0,
        tiled=True,
    )

    grad_a_cols = jnp.concatenate(
        [dot_first(h1, grad_q_lin), grad_w_exp.reshape(width, e_fold)], axis=1
    ).astype(bf16)
    grad_a_cols = sum_columns(grad_a_cols)
    first_part = dot_last(grad_q_lin, wq).astype(bf16).reshape(group, tok_dev, width)
    first_part, grad_e_down, grad_s_down, grad_s_cols = lax.optimization_barrier(
        (first_part, grad_e_down, grad_s_down, grad_s_cols)
    )
    first_sum = reduce_rows(first_part, 6)
    first_sum, rest, cols = lax.optimization_barrier(
        (
            first_sum,
            jnp.concatenate([grad_w_out, lat_grads], axis=1),
            jnp.concatenate([grad_s_cols, grad_a_cols], axis=1),
        )
    )
    cols = lax.all_to_all(
        cols.reshape(group, rows_w, -1), "expert", split_axis=0, concat_axis=0, tiled=True
    )
    rest = reduce_rows(rest.reshape(group, rows_w, -1), 7, max(1, rows_w // 32))
    grad_w_out = rest[:, :width]
    grad_w_lat = rest[:, width : width + lat_w]
    grad_f_gain = rest[:, width + lat_w]
    grad_l_gain = rest[:rows_l, width + lat_w + 1]
    grad_s_gate = ff_restore(cols[:, :, :ff_pad])
    grad_s_up = ff_restore(cols[:, :, ff_pad : 2 * ff_pad])
    grad_a_cols = cols[:, :, 2 * ff_pad :]
    grad_w_q = (
        grad_a_cols[:, :, :q_own]
        .reshape(group, rows_w, mine, KEY)[..., : NOPE + ROPE]
        .transpose(1, 0, 2, 3)
        .reshape(rows_w, -1)
        .astype(f32)
    )
    grad_w_exp = (
        grad_a_cols[:, :, q_own:]
        .reshape(group, rows_l, e_own)
        .transpose(1, 0, 2)
        .reshape(rows_l, -1)
        .astype(f32)
    )
    grad_a_gain = (
        jnp.sum(grad_w_q * w_query.astype(f32), axis=1)
        + jnp.sum(grad_w_lat * w_latent.astype(f32), axis=1)
    ) / attn_gain.astype(f32)

    grad_first = first_sum + dot_last(grad_latent[:, :lat_w], wl)
    unused, first_norm_back = jax.vjp(
        lambda v: norm_rows(v, a_gain), tokens_f
    )
    (grad_tokens_norm,) = first_norm_back(grad_first)
    grad_tokens = grad_resid + grad_tokens_norm
    return (
        block_out,
        grad_tokens,
        grad_a_gain,
        grad_w_q,
        grad_w_lat,
        grad_l_gain,
        grad_w_exp,
        grad_w_out,
        grad_f_gain,
        grad_s_gate,
        grad_s_up,
        grad_s_down.astype(f32),
        grad_e_gate.astype(f32)[None],
        grad_e_up.astype(f32)[None],
        grad_e_down.astype(f32)[None],
    )


def solution(mesh):
    placed = (
        P(EVERY, None),
        P(EVERY, None),
        P(EVERY, None),
        P(EVERY, None),
        P("dp", None),
        P(EVERY),
        P(EVERY, None),
        P(EVERY, None),
        P(EVERY),
        P(EVERY, None),
        P(EVERY, None),
        P(EVERY),
        P(EVERY, None),
        P(EVERY, None),
        P(EVERY, None),
        P("expert", None, None),
        P("expert", None, None),
        P("expert", None, None),
    )
    return jax.shard_map(
        per_device,
        mesh=mesh,
        in_specs=placed,
        out_specs=(
            P(EVERY, None),
            P(EVERY, None),
            P(EVERY),
            P(EVERY, None),
            P(EVERY, None),
            P(EVERY),
            P(EVERY, None),
            P(EVERY, None),
            P(EVERY),
            P(EVERY, None),
            P(EVERY, None),
            P(EVERY, None),
            P("expert", "dp", None),
            P("expert", "dp", None),
            P("expert", None, "dp"),
        ),
        check_vma=False,
    )
```

```python
import functools

import jax
import jax.numpy as jnp
from jax import lax
from jax.experimental import pallas as pl
from jax.experimental.pallas import tpu as pltpu
from jax.sharding import PartitionSpec as P

HEADS = 16
NOPE = 128
ROPE = 64
KV = 512
VD = 128
SEG = 256
KEY = 256

epsilon = 1e-06
bf16 = jnp.bfloat16
f32 = jnp.float32
EVERY = ("dp", "expert")
MESH = pl.DeviceIdType.MESH
VMEM_LIMIT = 60 << 20
WIRE = pl.CostEstimate(flops=0, bytes_accessed=300_000_000, transcendentals=0)


def norm_rows(values, gain_vec):
    return (
        values * lax.rsqrt(jnp.mean(values * values, axis=-1, keepdims=True) + epsilon) * gain_vec
    )


def rotate(values, cos_table, sin_table):
    half_width = values.shape[-1] // 2
    first_half = values[..., :half_width]
    second_half = values[..., half_width:]
    return jnp.concatenate(
        [
            first_half * cos_table - second_half * sin_table,
            second_half * cos_table + first_half * sin_table,
        ],
        axis=-1,
    )


def gating(gate_part, up_part):
    return jax.nn.silu(gate_part) * up_part


def ancestry(parent_row, seg_count):
    identity = jnp.eye(seg_count, dtype=f32)
    parent_hot = (parent_row[:, None] == jnp.arange(seg_count, dtype=jnp.int32)[None, :]).astype(
        f32
    )
    reachable = identity
    for _ in range(seg_count - 1):
        reachable = jnp.maximum(identity, jnp.dot(parent_hot, reachable))
    return reachable


def matmul(left, right):
    return jnp.dot(left, right, preferred_element_type=f32)


def dot_last(left, right):
    return lax.dot_general(left, right, (((1,), (1,)), ((), ())), preferred_element_type=f32)


def dot_first(left, right):
    return lax.dot_general(left, right, (((0,), (0,)), ((), ())), preferred_element_type=f32)


def greet(rank, last):
    barrier = pltpu.get_barrier_semaphore()
    a = rank // 2

    def hail(other):
        pl.semaphore_signal(barrier, inc=1, device_id={"expert": other}, device_id_type=MESH)

    hail(rank + 1 - 2 * (rank % 2))

    @pl.when(a < last)
    def _():
        hail(rank + 2)

    @pl.when(a > 0)
    def _():
        hail(rank - 2)

    pl.semaphore_wait(barrier, 1 + (a + last - 1) // last + (2 * last - 1 - a) // last)


class Chain:
    def __init__(self, chunks, x_ref, o_ref, sx, rx, su, ru, sd, rd):
        self.chunks, self.x, self.o = chunks, x_ref, o_ref
        self.sems = (sx, rx, su, ru, sd, rd)
        self.rank = lax.axis_index("expert")
        self.last = o_ref.shape[0] // 2 - 1
        self.a = self.rank // 2
        self.side = self.rank + 1 - 2 * (self.rank % 2)
        self.rows = x_ref.shape[0] // chunks

    def piece(self, ref, c):
        return ref.at[pl.ds(c * self.rows, self.rows)]

    def to(self, src, block, c, send, recv, target):
        return pltpu.make_async_remote_copy(
            src_ref=src,
            dst_ref=self.piece(self.o.at[block], c),
            send_sem=send,
            recv_sem=recv,
            device_id={"expert": target},
            device_id_type=MESH,
        )

    def start(self):
        sx, rx, su, ru, sd, rd = self.sems
        rank, a, last, to = self.rank, self.a, self.last, self.to
        for c in range(self.chunks):
            own = self.piece(self.x, c)
            to(own, rank, c, sx.at[0, c], rx.at[0, c], self.side).start()

            @pl.when(a < last)
            def _():
                to(own, rank, c, su.at[0, c], ru.at[0, c], rank + 2).start()

            @pl.when(a > 0)
            def _():
                to(own, rank, c, sd.at[0, c], rd.at[0, c], rank - 2).start()

    def step(self, s):
        sx, rx, su, ru, sd, rd = self.sems
        rank, a, last, to = self.rank, self.a, self.last, self.to
        for c in range(self.chunks):

            @pl.when(a >= s)
            def _():
                block = rank - 2 * s
                src = self.piece(self.o.at[block], c)
                to(src, block, c, su.at[s - 1, c], ru.at[s - 1, c], rank + 2).wait_recv()
                to(src, block, c, sx.at[s, c], rx.at[s, c], self.side).start()

                @pl.when(a < last)
                def _():
                    to(src, block, c, su.at[s, c], ru.at[s, c], rank + 2).start()

            @pl.when(a + s <= last)
            def _():
                block = rank + 2 * s
                src = self.piece(self.o.at[block], c)
                to(src, block, c, sd.at[s - 1, c], rd.at[s - 1, c], rank - 2).wait_recv()
                to(src, block, c, sx.at[last + s, c], rx.at[last + s, c], self.side).start()

                @pl.when(a > 0)
                def _():
                    to(src, block, c, sd.at[s, c], rd.at[s, c], rank - 2).start()

    def finish(self):
        sx, rx, su, ru, sd, rd = self.sems
        rank, a, last, to, side = self.rank, self.a, self.last, self.to, self.side
        for c in range(self.chunks):
            own = self.piece(self.x, c)
            to(own, side, c, sx.at[0, c], rx.at[0, c], side).wait()

            @pl.when(a < last)
            def _():
                to(own, rank, c, su.at[0, c], ru.at[0, c], rank + 2).wait_send()

            @pl.when(a > 0)
            def _():
                to(own, rank, c, sd.at[0, c], rd.at[0, c], rank - 2).wait_send()

        for s in range(1, last + 1):
            for c in range(self.chunks):

                @pl.when(a >= s)
                def _():
                    block = rank - 2 * s
                    src = self.piece(self.o.at[block], c)
                    to(src, side - 2 * s, c, sx.at[s, c], rx.at[s, c], side).wait()

                    @pl.when(a < last)
                    def _():
                        to(src, block, c, su.at[s, c], ru.at[s, c], rank + 2).wait_send()

                @pl.when(a + s <= last)
                def _():
                    block = rank + 2 * s
                    src = self.piece(self.o.at[block], c)
                    to(src, side + 2 * s, c, sx.at[last + s, c], rx.at[last + s, c], side).wait()

                    @pl.when(a > 0)
                    def _():
                        to(src, block, c, sd.at[s, c], rd.at[s, c], rank - 2).wait_send()


def chain_sems(count, chunks):
    half = count // 2
    dma = pltpu.SemaphoreType.DMA
    return [dma((2 * half, chunks))] * 2 + [dma((half, chunks))] * 4


class Share:
    def __init__(self, ref, send_out, recv_out, send_pass, recv_pass):
        self.ref = ref
        self.sems = (send_out, recv_out, send_pass, recv_pass)
        self.line = lax.axis_index("dp")
        self.count = ref.shape[0] // 2

    def out(self, k):
        peer = 2 * lax.rem(self.line // 2 + k, self.count) + self.line % 2
        return pltpu.make_async_remote_copy(
            src_ref=self.ref.at[self.line],
            dst_ref=self.ref.at[self.line],
            send_sem=self.sems[0].at[k],
            recv_sem=self.sems[1].at[k],
            device_id={"dp": peer},
            device_id_type=MESH,
        )

    def hand(self, k):
        slab = 2 * lax.rem(self.line // 2 + self.count - k, self.count) + self.line % 2
        return pltpu.make_async_remote_copy(
            src_ref=self.ref.at[slab],
            dst_ref=self.ref.at[slab],
            send_sem=self.sems[2].at[k],
            recv_sem=self.sems[3].at[k],
            device_id={"dp": self.line + 1 - 2 * (self.line % 2)},
            device_id_type=MESH,
        )

    def start(self):
        for k in range(1, self.count):
            self.out(k).start()
        self.hand(0).start()

    def middle(self):
        for k in range(1, self.count):
            self.out(k).wait_recv()
            self.hand(k).start()

    def finish(self):
        for k in range(1, self.count):
            self.out(k).wait_send()
        for k in range(self.count):
            self.hand(k).wait()


def prologue_kernel(
    chunks,
    x_ref,
    w_ref,
    d_ref,
    t_ref,
    o_ref,
    pk_ref,
    do_ref,
    to_ref,
    wa_s,
    wa_r,
    ta_s,
    ta_r,
    da_s,
    da_r,
    *sems,
):
    group, spread = o_ref.shape[0], pk_ref.shape[0]
    packs, downs = Share(pk_ref, *sems[:4]), Share(do_ref, *sems[4:8])
    chain = Chain(chunks, x_ref, o_ref, *sems[8:])
    rank, line = chain.rank, packs.line
    mine = rank % 2
    barrier = pltpu.get_barrier_semaphore()
    for k in range(1, group):
        pl.semaphore_signal(
            barrier,
            inc=1,
            device_id={"expert": lax.rem(rank + k, group)},
            device_id_type=MESH,
        )
    for k in range(1, packs.count):
        peer = 2 * lax.rem(line // 2 + k, packs.count) + line % 2
        pl.semaphore_signal(barrier, inc=1, device_id={"dp": peer}, device_id_type=MESH)
    pl.semaphore_signal(
        barrier, inc=1, device_id={"dp": line + 1 - 2 * (line % 2)}, device_id_type=MESH
    )
    pl.semaphore_wait(barrier, group - 1 + packs.count)

    def far(src, dst, send, recv, peer):
        return pltpu.make_async_remote_copy(
            src_ref=src,
            dst_ref=dst,
            send_sem=send,
            recv_sem=recv,
            device_id={"expert": peer},
            device_id_type=MESH,
        )

    def cut(k):
        peer = lax.rem(rank + k, group)
        return far(w_ref.at[peer], pk_ref.at[line, rank], wa_s.at[k - 1], wa_r.at[k - 1], peer)

    def gates(k):
        peer = lax.rem(rank + k, group)
        return far(t_ref, to_ref.at[rank], ta_s.at[k - 1], ta_r.at[k - 1], peer)

    def down():
        return far(d_ref, do_ref.at[line, mine], da_s.at[0], da_r.at[0], chain.side)

    down().start()
    for k in range(1, group):
        cut(k).start()
        gates(k).start()
    chain.start()
    pk_ref[line, rank] = w_ref[rank]
    do_ref[line, mine] = d_ref[...]
    to_ref[rank] = t_ref[...]
    o_ref[rank] = x_ref[...]
    down().wait_recv()
    downs.start()
    for k in range(1, group):
        cut(k).wait_recv()
    packs.start()
    for s in range(1, chain.last):
        chain.step(s)
    downs.middle()
    packs.middle()
    chain.step(chain.last)
    chain.finish()
    down().wait_send()
    for k in range(1, group):
        cut(k).wait_send()
        gates(k).wait()
    downs.finish()
    packs.finish()


def prologue(x, cuts, down, gates, spread, call_id, chunks=2):
    group = cuts.shape[0]
    dma = pltpu.SemaphoreType.DMA
    vmem = pl.BlockSpec(memory_space=pltpu.VMEM)
    return pl.pallas_call(
        functools.partial(prologue_kernel, chunks),
        out_shape=[
            jax.ShapeDtypeStruct((group,) + x.shape, x.dtype),
            jax.ShapeDtypeStruct((spread,) + cuts.shape, cuts.dtype),
            jax.ShapeDtypeStruct((spread, 2) + down.shape, down.dtype),
            jax.ShapeDtypeStruct((group,) + gates.shape, gates.dtype),
        ],
        in_specs=[vmem] * 4,
        out_specs=[vmem] * 4,
        scratch_shapes=[dma((group - 1,))] * 4
        + [dma((1,))] * 2
        + [dma((spread // 2,))] * 8
        + chain_sems(group, chunks),
        compiler_params=pltpu.CompilerParams(
            collective_id=call_id, has_side_effects=True, vmem_limit_bytes=VMEM_LIMIT
        ),
        cost_estimate=WIRE,
        name="prologue",
    )(x, cuts, down, gates)


def ring_pairs(group):
    half = group // 2
    side = [(r, r + 1 - 2 * (r % 2)) for r in range(group)]
    onward = [(2 * a + b, 2 * ((a + 1) % half) + b) for a in range(half) for b in range(2)]
    return side, onward


def tie(*values):
    return lax.optimization_barrier(values)


def reduce_kernel(parts, *refs):
    n = len(parts)
    p_refs, o_refs = refs[:n], refs[n : 2 * n]
    bufs = [refs[2 * n + 4 * k : 2 * n + 4 * k + 4] for k in range(n)]
    acc, sxs, rxs, sus, rus, sds, rds = refs[6 * n :]
    rank = lax.axis_index("expert")
    last = p_refs[0].shape[0] // 2 - 1
    a = rank // 2
    b = rank % 2
    greet(rank, last)
    h = a // 2
    order = [3 - 3 * h, 2 - h, 4 * h + 1 - a, a]
    pieces = []
    for k, chunks in enumerate(parts):
        rows = p_refs[k].shape[1] // chunks
        pieces += [(k, c * rows, rows) for c in range(chunks)]

    def copy(src, dst, send, recv, target):
        return pltpu.make_async_remote_copy(
            src_ref=src,
            dst_ref=dst,
            send_sem=send,
            recv_sem=recv,
            device_id={"expert": target},
            device_id_type=MESH,
        )

    for t in order:
        for c, (k, at, rows) in enumerate(pieces):
            src = p_refs[k].at[2 * t + 1 - b, pl.ds(at, rows)]
            dst = bufs[k][0].at[t, pl.ds(at, rows)]
            copy(src, dst, sxs.at[t, c], rxs.at[t, c], rank + 1 - 2 * b).start()

    def moves(t, c, k, at, rows):
        cut = pl.ds(at, rows)
        rx, st, ru, rd = (buf.at[t, cut] for buf in bufs[k])
        src = p_refs[k].at[2 * t + 1 - b, cut]
        across = copy(src, rx, sxs.at[t, c], rxs.at[t, c], rank + 1 - 2 * b)
        upward = copy(st, ru, sus.at[t, c], rus.at[t, c], rank + 2)
        downward = copy(st, rd, sds.at[t, c], rds.at[t, c], rank - 2)
        return rx, st, ru, rd, across, upward, downward

    for t in order:
        for c, (k, at, rows) in enumerate(pieces):
            rx, st, ru, rd, across, upward, downward = moves(t, c, k, at, rows)
            width = p_refs[k].shape[2]
            total = acc.at[pl.ds(0, rows), pl.ds(0, width)]
            across.wait_recv()
            total[...] = p_refs[k][2 * t + b, pl.ds(at, rows)].astype(f32) + rx[...].astype(f32)

            @pl.when((t >= a) & (a > 0))
            def _():
                upward.wait_recv()
                total[...] += ru[...].astype(f32)

            @pl.when((t <= a) & (a < last))
            def _():
                downward.wait_recv()
                total[...] += rd[...].astype(f32)

            @pl.when(t == a)
            def _():
                o_refs[k][pl.ds(at, rows)] = total[...]

            @pl.when(t > a)
            def _():
                st[...] = total[...].astype(bf16)
                upward.start()

            @pl.when(t < a)
            def _():
                st[...] = total[...].astype(bf16)
                downward.start()

    for t in order:
        for c, (k, at, rows) in enumerate(pieces):
            rx, st, ru, rd, across, upward, downward = moves(t, c, k, at, rows)
            across.wait_send()

            @pl.when(t > a)
            def _():
                upward.wait_send()

            @pl.when(t < a)
            def _():
                downward.wait_send()


def reduce_rows(operands, call_id, most):
    half = operands[0].shape[0] // 2
    parts = [
        max(c for c in range(1, most + 1) if p.shape[1] % (16 * c) == 0 and p.shape[1] // c >= 16)
        if p.shape[1] > 64
        else 1
        for p in operands
    ]
    high = max(p.shape[1] // c for p, c in zip(operands, parts))
    wide = max(p.shape[2] for p in operands)
    sem = pltpu.SemaphoreType.DMA((half, sum(parts)))
    vmem = pl.BlockSpec(memory_space=pltpu.VMEM)
    bufs = [
        pltpu.VMEM((half,) + p.shape[1:], p.dtype) for p in operands for _ in range(4)
    ]
    return pl.pallas_call(
        functools.partial(reduce_kernel, parts),
        out_shape=[jax.ShapeDtypeStruct(p.shape[1:], f32) for p in operands],
        in_specs=[vmem] * len(operands),
        out_specs=[vmem] * len(operands),
        scratch_shapes=bufs + [pltpu.VMEM((high, wide), f32)] + [sem] * 6,
        compiler_params=pltpu.CompilerParams(
            collective_id=call_id, has_side_effects=True, vmem_limit_bytes=VMEM_LIMIT
        ),
        cost_estimate=pl.CostEstimate(
            flops=0, bytes_accessed=36 * sum(p.size for p in operands) * 2, transcendentals=0
        ),
        name="reduce_rows",
    )(*operands)


def swap_halves(values):
    lane = lax.broadcasted_iota(jnp.int32, values.shape, 1)
    half = ROPE // 2
    return jnp.where(lane < half, pltpu.roll(values, KEY - NOPE - half, 1), pltpu.roll(values, half, 1))


def turns(seg_cos, seg_sin, off_cos, off_sin):
    lane = lax.broadcasted_iota(jnp.int32, off_cos.shape, 1)
    sine = seg_sin * off_cos + seg_cos * off_sin
    return seg_cos * off_cos - seg_sin * off_sin, jnp.where(lane < ROPE // 2, -sine, sine)


def project_kernel(
    heads,
    x_ref,
    wq_ref,
    wl_ref,
    we_ref,
    ag_ref,
    lg_ref,
    sc_ref,
    ss_ref,
    oc_ref,
    os_ref,
    h1_ref,
    q_ref,
    k_ref,
    v_ref,
    lat_ref,
    ckv_ref,
):
    i = pl.program_id(0)
    x = x_ref[...].astype(f32)
    power = jnp.mean(x * x, axis=-1, keepdims=True)
    h1 = (x * lax.rsqrt(power + epsilon) * ag_ref[...]).astype(bf16)
    h1_ref[...] = h1
    cosine, sine = turns(sc_ref[pl.ds(i, 1)], ss_ref[pl.ds(i, 1)], oc_ref[...], os_ref[...])

    def turn(values):
        return (values * cosine + swap_halves(values) * sine).astype(bf16)

    query = matmul(h1, wq_ref[...])
    for h in range(heads):
        at = h * KEY
        q_ref[:, at : at + NOPE] = query[:, at : at + NOPE].astype(bf16)
        q_ref[:, at + NOPE : at + KEY] = turn(query[:, at + NOPE : at + KEY])
    latent = matmul(h1, wl_ref[...])
    lat_ref[...] = latent
    low = latent[:, :KV]
    power = jnp.mean(low * low, axis=-1, keepdims=True)
    ckv = (low * lax.rsqrt(power + epsilon) * lg_ref[...]).astype(bf16)
    ckv_ref[...] = ckv
    krope = turn(latent[:, KV:])
    kv = matmul(ckv, we_ref[...]).astype(bf16)
    for h in range(heads):
        at = h * KEY
        k_ref[:, at : at + NOPE] = kv[:, at : at + NOPE]
        k_ref[:, at + NOPE : at + KEY] = krope
        v_ref[:, h * VD : (h + 1) * VD] = kv[:, at + NOPE : at + KEY]


def project(x, packed, lat_pack, we, a_gain, l_gain, tables, heads):
    tree, width = x.shape
    segs = tree // SEG
    lat_width = lat_pack.shape[1]
    fixed = lambda arr: pl.BlockSpec(arr.shape, lambda i: (0, 0))
    part = lambda cols: pl.BlockSpec((SEG, cols), lambda i: (i, 0))
    return pl.pallas_call(
        functools.partial(project_kernel, heads),
        grid=(segs,),
        in_specs=[
            part(width),
            pl.BlockSpec((width, heads * KEY), lambda i: (0, 0)),
            fixed(lat_pack),
            fixed(we),
            fixed(a_gain),
            fixed(l_gain),
        ]
        + [fixed(table) for table in tables],
        out_specs=[
            part(width),
            part(heads * KEY),
            part(heads * KEY),
            part(heads * VD),
            part(lat_width),
            part(KV),
        ],
        out_shape=[
            jax.ShapeDtypeStruct((tree, width), bf16),
            jax.ShapeDtypeStruct((tree, heads * KEY), bf16),
            jax.ShapeDtypeStruct((tree, heads * KEY), bf16),
            jax.ShapeDtypeStruct((tree, heads * VD), bf16),
            jax.ShapeDtypeStruct((tree, lat_width), f32),
            jax.ShapeDtypeStruct((tree, KV), bf16),
        ],
        compiler_params=pltpu.CompilerParams(vmem_limit_bytes=VMEM_LIMIT),
        cost_estimate=pl.CostEstimate(flops=0, bytes_accessed=60_000_000, transcendentals=0),
        name="project",
    )(x, packed, lat_pack, we, a_gain, l_gain, *tables)


def triangle():
    keys = lax.broadcasted_iota(jnp.int32, (SEG, SEG), 0)
    queries = lax.broadcasted_iota(jnp.int32, (SEG, SEG), 1)
    return keys <= queries


def attend_kernel(
    heads, segs, scale, reach_ref, q_ref, k_ref, v_ref, out_ref, full_ref, log_ref, m_s, l_s, acc_s
):
    i = pl.program_id(0)
    diag = triangle()

    def score(h, j):
        keys = k_ref[pl.ds(j * SEG, SEG), h * KEY : (h + 1) * KEY]
        return dot_last(keys, q_ref[:, h * KEY : (h + 1) * KEY]) * scale

    def weigh(h, j, weights):
        vals = v_ref[pl.ds(j * SEG, SEG), h * VD : (h + 1) * VD]
        return dot_first(vals, weights.astype(bf16))

    for h in range(heads):
        s = jnp.where(diag, score(h, i), -1e30)
        top = jnp.max(s, axis=0, keepdims=True)
        w = jnp.where(diag, jnp.exp(s - top), 0.0)
        m_s[h : h + 1] = top
        l_s[h : h + 1] = jnp.sum(w, axis=0, keepdims=True)
        acc_s[h] = weigh(h, i, w)

    def step(j, carry):
        @pl.when(reach_ref[i * segs + j] > 0)
        def _():
            for h in range(heads):
                s = score(h, j)
                old = m_s[h : h + 1]
                top = jnp.maximum(old, jnp.max(s, axis=0, keepdims=True))
                w = jnp.exp(s - top)
                fade = jnp.exp(old - top)
                m_s[h : h + 1] = top
                l_s[h : h + 1] = l_s[h : h + 1] * fade + jnp.sum(w, axis=0, keepdims=True)
                acc_s[h] = acc_s[h] * fade + weigh(h, j, w)

        return carry

    lax.fori_loop(0, i, step, 0)
    for h in range(heads):
        total = l_s[h : h + 1]
        rows = (acc_s[h] * (1.0 / total)).T
        full_ref[:, h * VD : (h + 1) * VD] = rows
        out_ref[:, h * VD : (h + 1) * VD] = rows.astype(bf16)
        log_ref[h : h + 1] = m_s[h : h + 1] + jnp.log(total)


def attend(reach, q, k, v, scale):
    tree = q.shape[0]
    segs = tree // SEG
    heads = q.shape[1] // KEY
    whole = lambda width: pl.BlockSpec((tree, width), lambda i, r: (0, 0))
    part = lambda width: pl.BlockSpec((SEG, width), lambda i, r: (i, 0))
    return pl.pallas_call(
        functools.partial(attend_kernel, heads, segs, scale),
        grid_spec=pltpu.PrefetchScalarGridSpec(
            num_scalar_prefetch=1,
            grid=(segs,),
            in_specs=[part(heads * KEY), whole(heads * KEY), whole(heads * VD)],
            out_specs=[
                part(heads * VD),
                part(heads * VD),
                pl.BlockSpec((heads, SEG), lambda i, r: (0, i)),
            ],
            scratch_shapes=[
                pltpu.VMEM((heads, SEG), f32),
                pltpu.VMEM((heads, SEG), f32),
                pltpu.VMEM((heads, VD, SEG), f32),
            ],
        ),
        out_shape=[
            jax.ShapeDtypeStruct((tree, heads * VD), bf16),
            jax.ShapeDtypeStruct((tree, heads * VD), f32),
            jax.ShapeDtypeStruct((heads, tree), f32),
        ],
        compiler_params=pltpu.CompilerParams(vmem_limit_bytes=VMEM_LIMIT),
        cost_estimate=pl.CostEstimate(flops=0, bytes_accessed=70_000_000, transcendentals=0),
        name="attend",
    )(reach, q, k, v)


def attend_back_kernel(
    heads,
    segs,
    scale,
    reach_ref,
    q_ref,
    k_ref,
    v_ref,
    g_ref,
    att_ref,
    log_ref,
    we_ref,
    sc_ref,
    ss_ref,
    oc_ref,
    os_ref,
    gq_ref,
    dkv_ref,
    lat_ref,
    dq_s,
    dk_s,
    dv_s,
    delta_s,
):
    j = pl.program_id(0)
    diag = triangle()

    @pl.when(j == 0)
    def _():
        def prepare(i, carry):
            rows = pl.ds(i * SEG, SEG)
            for h in range(heads):
                vcols = slice(h * VD, (h + 1) * VD)
                both = g_ref[rows, vcols].astype(f32) * att_ref[rows, vcols]
                delta_s[h : h + 1, rows] = jnp.sum(both.T, axis=0, keepdims=True)
            dq_s[rows] = jnp.zeros((SEG, heads * KEY), f32)
            return carry

        lax.fori_loop(0, segs, prepare, 0)

    dk_s[...] = jnp.zeros_like(dk_s)
    dv_s[...] = jnp.zeros_like(dv_s)

    def block(i, masked):
        rows = pl.ds(i * SEG, SEG)
        for h in range(heads):
            kcols = slice(h * KEY, (h + 1) * KEY)
            vcols = slice(h * VD, (h + 1) * VD)
            q = q_ref[rows, kcols]
            k = k_ref[:, kcols]
            g = g_ref[rows, vcols]
            s = dot_last(k, q) * scale
            w = jnp.exp(s - log_ref[h : h + 1, rows])
            if masked:
                w = jnp.where(diag, w, 0.0)
            dw = dot_last(v_ref[:, vcols], g)
            ds = (w * (dw - delta_s[h : h + 1, rows])).astype(bf16)
            dv_s[h] += matmul(w.astype(bf16), g)
            dk_s[h] += matmul(ds, q)
            dq_s[rows, kcols] += dot_first(ds, k)

    block(j, True)

    def step(i, carry):
        @pl.when(reach_ref[i * segs + j] > 0)
        def _():
            block(i, False)

        return carry

    lax.fori_loop(j + 1, segs, step, 0)
    rope = jnp.zeros((SEG, KEY - NOPE), f32)
    for h in range(heads):
        dkv_ref[:, h * KEY : h * KEY + NOPE] = (dk_s[h, :, :NOPE] * scale).astype(bf16)
        dkv_ref[:, h * KEY + NOPE : (h + 1) * KEY] = dv_s[h].astype(bf16)
        rope = rope + dk_s[h, :, NOPE:]
    lat_ref[:, :KV] = dot_last(dkv_ref[...], we_ref[...]).astype(bf16)
    lat_ref[:, KV:] = (rope * scale).astype(bf16)

    @pl.when(j == segs - 1)
    def _():
        def finish(i, carry):
            rows = pl.ds(i * SEG, SEG)
            cosine, sine = turns(
                sc_ref[pl.ds(i, 1)], ss_ref[pl.ds(i, 1)], oc_ref[...], os_ref[...]
            )
            for h in range(heads):
                at = h * KEY
                gq_ref[rows, at : at + NOPE] = (dq_s[rows, at : at + NOPE] * scale).astype(bf16)
                turned = dq_s[rows, at + NOPE : at + KEY] * scale
                gq_ref[rows, at + NOPE : at + KEY] = (
                    turned * cosine - swap_halves(turned) * sine
                ).astype(bf16)
            return carry

        lax.fori_loop(0, segs, finish, 0)


def attend_back(reach, q, k, v, g, attended, log_total, we, tables, scale):
    tree = q.shape[0]
    segs = tree // SEG
    heads = q.shape[1] // KEY
    whole = lambda width: pl.BlockSpec((tree, width), lambda j, r: (0, 0))
    part = lambda width: pl.BlockSpec((SEG, width), lambda j, r: (j, 0))
    fixed = lambda arr: pl.BlockSpec(arr.shape, lambda j, r: (0, 0))
    lat_width = KV + KEY - NOPE
    return pl.pallas_call(
        functools.partial(attend_back_kernel, heads, segs, scale),
        grid_spec=pltpu.PrefetchScalarGridSpec(
            num_scalar_prefetch=1,
            grid=(segs,),
            in_specs=[
                whole(heads * KEY),
                part(heads * KEY),
                part(heads * VD),
                whole(heads * VD),
                whole(heads * VD),
                fixed(log_total),
                fixed(we),
            ]
            + [fixed(table) for table in tables],
            out_specs=[whole(heads * KEY), part(heads * KEY), part(lat_width)],
            scratch_shapes=[
                pltpu.VMEM((tree, heads * KEY), f32),
                pltpu.VMEM((heads, SEG, KEY), f32),
                pltpu.VMEM((heads, SEG, VD), f32),
                pltpu.VMEM((heads, tree), f32),
            ],
        ),
        out_shape=[
            jax.ShapeDtypeStruct((tree, heads * KEY), bf16),
            jax.ShapeDtypeStruct((tree, heads * KEY), bf16),
            jax.ShapeDtypeStruct((tree, lat_width), bf16),
        ],
        compiler_params=pltpu.CompilerParams(vmem_limit_bytes=VMEM_LIMIT),
        cost_estimate=pl.CostEstimate(flops=0, bytes_accessed=90_000_000, transcendentals=0),
        name="attend_back",
    )(reach, q, k, v, g, attended, log_total, we, *tables)


def per_device(
    tokens,
    grad_out,
    routes,
    gate_values,
    parents,
    attn_gain,
    w_query,
    w_latent,
    latent_gain,
    w_expand,
    w_output,
    ffn_gain,
    shared_gate,
    shared_up,
    shared_down,
    expert_gate,
    expert_up,
    expert_down,
):
    group = lax.axis_size("expert")
    spread = lax.axis_size("dp")
    rank = lax.axis_index("expert")
    tok_dev, width = tokens.shape
    tree = tok_dev * group
    segs = parents.shape[1]
    per_token = routes.shape[1]
    capacity = tok_dev * per_token * 9 // (8 * group)
    slots = -(-capacity // 16) * 16
    scale = (NOPE + ROPE) ** (-0.5)
    mine = HEADS // group
    rows_w = w_query.shape[0]
    rows_l = w_expand.shape[0]
    ff_cut = shared_down.shape[0]
    half = group // 2
    ff_own = 2 * ff_cut * spread
    ff_pad = -(-ff_own // 128) * 128
    q_own = mine * KEY
    e_own = mine * (NOPE + VD)
    e_fold = rows_l * e_own // rows_w

    wq_cut = jnp.pad(
        w_query.reshape(rows_w, group, mine, NOPE + ROPE),
        ((0, 0), (0, 0), (0, 0), (0, KEY - NOPE - ROPE)),
    ).reshape(rows_w, group, q_own)

    def ff_columns(weight):
        cut = weight.reshape(rows_w, spread, half, 2 * ff_cut).transpose(2, 0, 1, 3)
        cut = jnp.pad(
            cut.reshape(half, 1, rows_w, ff_own),
            ((0, 0), (0, 0), (0, 0), (0, ff_pad - ff_own)),
        )
        return jnp.broadcast_to(cut, (half, 2, rows_w, ff_pad)).reshape(group, rows_w, ff_pad)

    we_cut = (
        w_expand.reshape(rows_l, group, e_own).transpose(1, 0, 2).reshape(group, rows_w, e_fold)
    )
    packed = jnp.concatenate(
        [
            wq_cut.transpose(1, 0, 2),
            we_cut,
            ff_columns(shared_gate),
            ff_columns(shared_up),
        ],
        axis=2,
    )
    expert_ids = jnp.arange(group, dtype=jnp.int32)
    gate_of = jnp.sum(
        jnp.where(routes[:, :, None] == expert_ids[None, None, :], gate_values[:, :, None], 0.0),
        axis=1,
    ).T
    x_all, packed, sd, gate_of = prologue(tokens, packed, shared_down, gate_of, spread, 0)
    x_all, parents, gate_of = lax.optimization_barrier(
        (x_all.reshape(tree, width), parents, gate_of)
    )
    packed = packed.reshape(width, -1)
    wq = packed[:, :q_own]
    we = packed[:, q_own : q_own + e_fold].reshape(KV, e_own)
    sg = packed[:, q_own + e_fold : q_own + e_fold + ff_pad]
    su = packed[:, q_own + e_fold + ff_pad :]
    sd = jnp.pad(sd.reshape(ff_own, width), ((0, ff_pad - ff_own), (0, 0)))

    lat_w = KV + ROPE
    gains = jnp.stack(
        [attn_gain, ffn_gain, jnp.pad(latent_gain, (0, rows_w - rows_l))], axis=1
    )
    gains = jnp.pad(gains, ((0, 0), (0, ROPE - 3)))
    lat_pack = lax.all_gather(
        jnp.concatenate([w_latent, gains], axis=1), EVERY, axis=0, tiled=True
    )
    wl = lat_pack[:, :lat_w]
    a_gain = lat_pack[:, lat_w].astype(f32)
    f_gain = lat_pack[:, lat_w + 1].astype(f32)
    l_gain = lat_pack[:, lat_w + 2].reshape(-1, rows_w)[:, :rows_l].reshape(KV).astype(f32)
    wo = lax.all_gather(w_output, EVERY, axis=0, tiled=True)
    reachable = ancestry(parents[0], segs)
    depth = jnp.sum(reachable, axis=1) - 1.0
    reach = reachable.astype(jnp.int32).reshape(segs * segs)
    half_width = ROPE // 2
    freq = 10000.0 ** (-2.0 * jnp.arange(half_width, dtype=f32) / ROPE)
    seg_angle = (depth * SEG)[:, None] * freq[None, :]
    off_angle = jnp.arange(SEG, dtype=f32)[:, None] * freq[None, :]

    def lanes(values):
        return jnp.pad(
            jnp.concatenate([values, values], axis=1), ((0, 0), (0, KEY - NOPE - ROPE))
        )

    tables = [
        lanes(jnp.cos(seg_angle)),
        lanes(jnp.sin(seg_angle)),
        lanes(jnp.cos(off_angle)),
        lanes(jnp.sin(off_angle)),
    ]
    seg_cos = lax.dynamic_slice_in_dim(tables[0], rank, 1, 0)[:, :half_width]
    seg_sin = lax.dynamic_slice_in_dim(tables[1], rank, 1, 0)[:, :half_width]
    off_cos = tables[2][:, :half_width]
    off_sin = tables[3][:, :half_width]
    own_cos = seg_cos * off_cos - seg_sin * off_sin
    own_sin = seg_sin * off_cos + seg_cos * off_sin

    def own(values):
        return lax.dynamic_slice_in_dim(values, rank * tok_dev, tok_dev, 0)

    h1, q_att, k_att, v_att, latent, ckv = project(
        x_all, packed, lat_pack, we, a_gain[None], l_gain[None], tables, mine
    )
    side, ring = ring_pairs(group)

    def across(values):
        return lax.ppermute(values, "expert", side)

    def onward(values):
        return lax.ppermute(values, "expert", ring)

    def behind(values, s, far):
        at = 2 * lax.rem(rank // 2 - s + half, half) + lax.rem(rank + far, 2)
        return lax.dynamic_index_in_dim(values, at, 0, keepdims=False)

    def line_swap(values, m):
        own_bit = lax.rem(lax.axis_index("dp") // (1 << m), 2)
        at = spread.bit_length() - 2 - m
        keep = lax.dynamic_index_in_dim(values, own_bit, at, False)
        send = lax.dynamic_index_in_dim(values, 1 - own_bit, at, False)
        swap = [(d, d ^ (1 << m)) for d in range(spread)]
        return keep, lax.ppermute(send, "dp", swap)

    def both_halves(keep, other):
        return (keep.astype(f32) + other.astype(f32)).astype(bf16)

    def ring_sum(values):
        steps = list(range(1, half)) + [0]
        arrived = across(jnp.stack([behind(values, s, 1) for s in steps]))
        total = None
        for k, s in enumerate(steps):
            term = behind(values, s, 0).astype(f32) + arrived[k].astype(f32)
            if total is not None:
                term = term + onward(total.astype(bf16)).astype(f32)
            total = term
        return total

    q_att, g0 = tie(q_att, grad_out)
    g1 = onward(g0)
    attn_heads, attended, log_total = attend(reach, q_att, k_att, v_att, scale)
    attn_heads, g1 = tie(attn_heads, g1)
    g2 = onward(g1)
    attn_own = lax.all_to_all(attn_heads, "expert", split_axis=0, concat_axis=1, tiled=True)
    tokens_f = tokens.astype(f32)
    resid = tokens_f + matmul(attn_own, wo)
    second_normed, second_norm_back = jax.vjp(norm_rows, resid, f_gain)
    b0 = second_normed.astype(bf16)

    b1 = onward(b0)
    gate_of = jnp.concatenate(
        [
            lax.dynamic_slice(
                gate_of,
                (2 * lax.rem(rank // 2 - s + half, half) + rank % 2, rank + k - 2 * k * (rank % 2), 0),
                (1, 1, tok_dev),
            )[0]
            for s in range(half)
            for k in range(2)
        ],
        axis=0,
    )
    routed = gate_of > 0.0
    upto = (
        jnp.arange(tok_dev, dtype=jnp.int32)[:, None]
        <= jnp.arange(tok_dev, dtype=jnp.int32)[None, :]
    )
    place = matmul(routed.astype(bf16), upto.astype(bf16)).astype(jnp.int32) - 1
    chosen = (
        place[:, None, :] == jnp.arange(slots, dtype=jnp.int32)[None, :, None]
    ) & routed[:, None, :]
    pick_all = chosen.astype(bf16).reshape(half, 2 * slots, tok_dev)
    gates_all = jnp.sum(jnp.where(chosen, gate_of[:, None, :], 0.0), axis=2).reshape(
        half, 2 * slots, 1
    )

    def take(s, rows, weights=None):
        picked = matmul(pick_all[s], rows)
        if weights is not None:
            picked = picked * weights
        return picked.astype(bf16)

    def shared(h2, g_rows):
        s_act, s_gating_back = jax.vjp(gating, matmul(h2, sg), matmul(h2, su))
        s_act = s_act.astype(bf16)
        grad_s_act = dot_last(g_rows, sd).astype(bf16)
        gate_part, up_part = s_gating_back(grad_s_act.astype(f32))
        gate_part = gate_part.astype(bf16)
        up_part = up_part.astype(bf16)
        near = dot_last(gate_part, sg) + dot_last(up_part, su)
        return near, s_act, gate_part, up_part

    def expert(e_rows, e_grad):
        activated, e_gating_back = jax.vjp(
            gating, matmul(e_rows, expert_gate[0]), matmul(e_rows, expert_up[0])
        )
        activated = activated.astype(bf16)
        grad_e_act = dot_last(e_grad, expert_down[0]).astype(bf16)
        gate_part, up_part = e_gating_back(grad_e_act.astype(f32))
        gate_part = gate_part.astype(bf16)
        up_part = up_part.astype(bf16)
        grad_rows = (
            dot_last(gate_part, expert_gate[0]) + dot_last(up_part, expert_up[0])
        ).astype(bf16)
        return grad_rows, activated, gate_part, up_part

    def join(mine, arrived):
        return jnp.concatenate([mine[:slots], arrived], axis=0)

    def spread_back(s, near, mine, arrived, *more):
        total = near + dot_first(pick_all[s], join(mine, arrived))
        for other in more:
            total = total + other.astype(f32)
        return total

    e0 = take(0, b0)
    e0_in = across(e0[slots:])
    w0, w1 = (take(s, g, gates_all[s]) for s, g in enumerate((g0, g1)))
    w0_in, w1_in = (across(w[slots:]) for w in (w0, w1))
    n0_near, *s0 = shared(b0, g0)
    n0_near, b1, e0_in, w0_in, w1_in, g2 = tie(n0_near, b1, e0_in, w0_in, w1_in, g2)
    b2, g3 = onward(b1), onward(g2)
    w2 = take(2, g2, gates_all[2])
    w2_in = across(w2[slots:])
    e1 = take(1, b1)
    e1_in = across(e1[slots:])
    r0, w0 = join(e0, e0_in), join(w0, w0_in)
    n0, *k0 = expert(r0, w0)
    n0, b1 = tie(n0, b1)
    n0_in = across(n0[slots:])
    n1_near, *s1 = shared(b1, g1)
    n1_near, b2, e1_in, n0_in, w2_in, g3 = tie(n1_near, b2, e1_in, n0_in, w2_in, g3)
    w3 = take(3, g3, gates_all[3])
    w3_in = across(w3[slots:])
    b3 = onward(b2)
    e2 = take(2, b2)
    e2_in = across(e2[slots:])
    r1, w1 = join(e1, e1_in), join(w1, w1_in)
    n1, *k1 = expert(r1, w1)
    n1, b2 = tie(n1, b2)
    n1_in = across(n1[slots:])
    n2_near, *s2 = shared(b2, g2)
    n2_near, b3, e2_in, n1_in, w3_in = tie(n2_near, b3, e2_in, n1_in, w3_in)
    ring1 = onward(spread_back(1, n1_near, n1, n1_in).astype(bf16))
    e3 = take(3, b3)
    e3_in = across(e3[slots:])
    r2, w2 = join(e2, e2_in), join(w2, w2_in)
    n2, *k2 = expert(r2, w2)
    n2, b3 = tie(n2, b3)
    n2_in = across(n2[slots:])
    n3_near, *s3 = shared(b3, g3)
    n3_near, e3_in, n2_in, ring1 = tie(n3_near, e3_in, n2_in, ring1)
    ring2 = onward(spread_back(2, n2_near, n2, n2_in, ring1).astype(bf16))
    r3, w3 = join(e3, e3_in), join(w3, w3_in)
    n3, *k3 = expert(r3, w3)
    n3, ring2 = tie(n3, ring2)
    n3_in = across(n3[slots:])
    s_act, s_gate_part, s_up_part = (
        jnp.concatenate(pieces, axis=0) for pieces in zip(s0, s1, s2, s3)
    )
    b_all = jnp.concatenate([b0, b1, b2, b3], axis=0)
    g_all = jnp.concatenate([g0, g1, g2, g3], axis=0)
    grad_s_cols = dot_first(b_all, jnp.concatenate([s_gate_part, s_up_part], axis=1)).astype(bf16)
    grad_s_cols, n3_in = tie(grad_s_cols, n3_in)
    ring3 = onward(spread_back(3, n3_near, n3, n3_in, ring2).astype(bf16))
    e_rows = jnp.concatenate([r0, r1, r2, r3], axis=0)
    e_grad = jnp.concatenate([w0, w1, w2, w3], axis=0)
    activated, gate_part, up_part = (
        jnp.concatenate(pieces, axis=0) for pieces in zip(k0, k1, k2, k3)
    )
    grad_e_gate = dot_first(e_rows, gate_part).astype(bf16)
    grad_e_up = dot_first(e_rows, up_part).astype(bf16)
    e_result = matmul(activated, expert_down[0]).astype(bf16).reshape(half, 2 * slots, width)
    grad_e_gate, grad_e_up, ring3, activated, s_act, e_result = tie(
        grad_e_gate, grad_e_up, ring3, activated, s_act, e_result
    )
    grad_second = spread_back(0, n0_near, n0, n0_in, ring3)
    o_in = across(e_result[:, slots:])
    grad_e_down = dot_first(activated, e_grad).astype(bf16)
    grad_s_down = dot_first(s_act, g_all).astype(bf16)

    def out_term(s, *more):
        weighed = (join(e_result[s], o_in[s]).astype(f32) * gates_all[s]).astype(bf16)
        total = matmul(s_act[s * tok_dev : (s + 1) * tok_dev], sd) + dot_first(
            pick_all[s], weighed
        )
        for other in more:
            total = total + other.astype(f32)
        return total

    grad_e_gate = lax.psum_scatter(grad_e_gate, "dp", scatter_dimension=0, tiled=True)
    grad_e_up = lax.psum_scatter(grad_e_up, "dp", scatter_dimension=0, tiled=True)
    grad_e_down_all, grad_s_down = grad_e_down, grad_s_down[:ff_own]

    def sum_columns(grads):
        return lax.psum_scatter(grads, "dp", scatter_dimension=0, tiled=True)

    grad_s_cols = sum_columns(grad_s_cols)

    def ff_restore(cut):
        both = cut[:, :, :ff_own].astype(f32).reshape(half, 2, rows_w, spread, 2 * ff_cut)
        return (both[:, 0] + both[:, 1]).transpose(1, 2, 0, 3).reshape(rows_w, -1)

    grad_f = grad_out.astype(f32)
    grad_resid_norm, grad_f_gain = second_norm_back(grad_second)
    grad_resid = grad_f + grad_resid_norm
    grad_attn_out = grad_resid.astype(bf16)
    grad_w_out = dot_first(attn_own, grad_attn_out).astype(bf16)
    grad_attended = dot_last(grad_attn_out, wo).astype(bf16)
    grad_attended, o_in = tie(grad_attended, o_in)
    grad_heads = lax.all_to_all(grad_attended, "expert", split_axis=1, concat_axis=0, tiled=True)
    grad_heads, o1, grad_w_out, grad_s_cols, grad_e_down, grad_s_down, grad_e_gate = tie(
        grad_heads,
        out_term(1).astype(bf16),
        grad_w_out,
        grad_s_cols,
        grad_e_down_all,
        grad_s_down,
        grad_e_gate,
    )
    s_keep, s_other = line_swap(
        grad_s_down.reshape((2,) * (spread.bit_length() - 1) + (2, ff_cut, width)), 0
    )
    ring1 = onward(o1)
    grad_s_cut = lax.all_to_all(
        grad_s_cols.reshape(group, rows_w, -1), "expert", split_axis=0, concat_axis=0, tiled=True
    )
    grad_w_out = lax.psum_scatter(grad_w_out, "dp", scatter_dimension=0, tiled=True)
    grad_q_lin, grad_kv, lat_part = attend_back(
        reach, q_att, k_att, v_att, grad_heads, attended, log_total, we, tables, scale
    )
    lat_part, grad_q_lin, ring1, grad_e_down, s_other = tie(
        lat_part, grad_q_lin, ring1, grad_e_down, s_other
    )
    ring2 = onward(out_term(2, ring1).astype(bf16))
    grad_s_down = both_halves(s_keep, s_other)
    for m in range(1, spread.bit_length() - 1):
        s_keep, s_other = line_swap(grad_s_down, m)
        if m < spread.bit_length() - 2:
            grad_s_down = both_halves(s_keep, s_other)
    (grad_lat_sum,) = reduce_rows([lat_part.reshape(group, tok_dev, -1)], 5, 2)
    grad_lat_sum, grad_q_lin, ring2, s_other, grad_w_out, grad_e_down = tie(
        grad_lat_sum, grad_q_lin, ring2, s_other, grad_w_out, grad_e_down
    )
    grad_s_down = both_halves(s_keep, s_other)
    own_side = rank % 2
    s_keep = lax.dynamic_index_in_dim(grad_s_down, own_side, 0, False)
    s_other = across(lax.dynamic_index_in_dim(grad_s_down, 1 - own_side, 0, False))
    ring3 = onward(out_term(3, ring2).astype(bf16))
    first_part = dot_last(grad_q_lin, wq).astype(bf16).reshape(group, tok_dev, width)
    grad_a_cols = jnp.concatenate(
        [dot_first(h1, grad_q_lin), dot_first(ckv, grad_kv).reshape(width, e_fold)], axis=1
    ).astype(bf16)

    def latent_parts(latent_in, gain_vec):
        return (
            norm_rows(latent_in[:, :KV], gain_vec),
            rotate(latent_in[:, KV : KV + ROPE], own_cos, own_sin),
        )

    unused, latent_back = jax.vjp(latent_parts, own(latent), l_gain)
    grad_latent, grad_l_gain = latent_back(
        (grad_lat_sum[:, :KV], grad_lat_sum[:, KV : KV + ROPE])
    )
    grad_latent = grad_latent.astype(bf16)
    grad_w_lat = dot_first(own(h1), grad_latent)[:, : KV + ROPE]
    grad_gains = jnp.stack(
        [
            grad_f_gain,
            jnp.pad(grad_l_gain.reshape(-1, rows_l), ((0, 0), (0, rows_w - rows_l))).reshape(width),
        ],
        axis=1,
    )
    lat_grads_in = jnp.concatenate(
        [grad_w_lat, jnp.pad(grad_gains, ((0, 0), (0, ROPE - 2)))], axis=1
    ).astype(bf16)
    first_part, lat_grads, grad_a_cols = tie(first_part, lat_grads_in, grad_a_cols)
    lat_grads = lax.psum_scatter(lat_grads, "dp", scatter_dimension=0, tiled=True)
    grad_a_cols = lax.psum_scatter(grad_a_cols, "dp", scatter_dimension=0, tiled=True)
    grad_e_down = lax.psum_scatter(grad_e_down, "dp", scatter_dimension=1, tiled=True)
    first_sum, grad_w_out = reduce_rows(
        [first_part, grad_w_out.reshape(group, rows_w, width)], 6, 4
    )
    (
        first_sum,
        lat_grads,
        ring3,
        s_keep,
        s_other,
        grad_a_cols,
        grad_s_cut,
        grad_e_gate,
        grad_e_up,
    ) = tie(
        first_sum,
        lat_grads,
        ring3,
        s_keep,
        s_other,
        grad_a_cols,
        grad_s_cut,
        grad_e_gate,
        grad_e_up,
    )
    grad_s_down = s_keep.astype(f32) + s_other.astype(f32)
    block_out = (resid + out_term(0, ring3)).astype(bf16)
    lat_grads = ring_sum(lat_grads.reshape(group, rows_w, -1))
    grad_w_lat = lat_grads[:, :lat_w]
    grad_f_gain = lat_grads[:, lat_w]
    grad_l_gain = lat_grads[:rows_l, lat_w + 1]
    grad_s_gate = ff_restore(grad_s_cut[:, :, :ff_pad])
    grad_s_up = ff_restore(grad_s_cut[:, :, ff_pad:])
    grad_a_cols = lax.all_to_all(
        grad_a_cols.reshape(group, rows_w, -1), "expert", split_axis=0, concat_axis=0, tiled=True
    )
    grad_w_q = (
        grad_a_cols[:, :, :q_own]
        .reshape(group, rows_w, mine, KEY)[..., : NOPE + ROPE]
        .transpose(1, 0, 2, 3)
        .reshape(rows_w, -1)
        .astype(f32)
    )
    grad_w_exp = (
        grad_a_cols[:, :, q_own:]
        .reshape(group, rows_l, e_own)
        .transpose(1, 0, 2)
        .reshape(rows_l, -1)
        .astype(f32)
    )
    grad_a_gain = (
        jnp.sum(grad_w_q * w_query.astype(f32), axis=1)
        + jnp.sum(grad_w_lat * w_latent.astype(f32), axis=1)
    ) / attn_gain.astype(f32)

    grad_first = first_sum + dot_last(grad_latent[:, :lat_w], wl)
    unused, first_norm_back = jax.vjp(
        lambda v: norm_rows(v, a_gain), tokens_f
    )
    (grad_tokens_norm,) = first_norm_back(grad_first)
    grad_tokens = grad_resid + grad_tokens_norm
    return (
        block_out,
        grad_tokens,
        grad_a_gain,
        grad_w_q,
        grad_w_lat,
        grad_l_gain,
        grad_w_exp,
        grad_w_out,
        grad_f_gain,
        grad_s_gate,
        grad_s_up,
        grad_s_down,
        grad_e_gate.astype(f32)[None],
        grad_e_up.astype(f32)[None],
        grad_e_down.astype(f32)[None],
    )


def solution(mesh):
    placed = (
        P(EVERY, None),
        P(EVERY, None),
        P(EVERY, None),
        P(EVERY, None),
        P("dp", None),
        P(EVERY),
        P(EVERY, None),
        P(EVERY, None),
        P(EVERY),
        P(EVERY, None),
        P(EVERY, None),
        P(EVERY),
        P(EVERY, None),
        P(EVERY, None),
        P(EVERY, None),
        P("expert", None, None),
        P("expert", None, None),
        P("expert", None, None),
    )
    return jax.shard_map(
        per_device,
        mesh=mesh,
        in_specs=placed,
        out_specs=(
            P(EVERY, None),
            P(EVERY, None),
            P(EVERY),
            P(EVERY, None),
            P(EVERY, None),
            P(EVERY),
            P(EVERY, None),
            P(EVERY, None),
            P(EVERY),
            P(EVERY, None),
            P(EVERY, None),
            P(EVERY, None),
            P("expert", "dp", None),
            P("expert", "dp", None),
            P("expert", None, "dp"),
        ),
        check_vma=False,
    )
```

```python
import functools

import jax
import jax.numpy as jnp
from jax import lax
from jax.experimental import pallas as pl
from jax.experimental.pallas import tpu as pltpu
from jax.sharding import PartitionSpec as P

HEADS = 16
NOPE = 128
ROPE = 64
KV = 512
VD = 128
SEG = 256
KEY = 256

epsilon = 1e-06
bf16 = jnp.bfloat16
f32 = jnp.float32
EVERY = ("dp", "expert")
MESH = pl.DeviceIdType.MESH
VMEM_LIMIT = 60 << 20
WIRE = pl.CostEstimate(flops=0, bytes_accessed=300_000_000, transcendentals=0)


def norm_rows(values, gain_vec):
    return (
        values * lax.rsqrt(jnp.mean(values * values, axis=-1, keepdims=True) + epsilon) * gain_vec
    )


def rotate(values, cos_table, sin_table):
    half_width = values.shape[-1] // 2
    first_half = values[..., :half_width]
    second_half = values[..., half_width:]
    return jnp.concatenate(
        [
            first_half * cos_table - second_half * sin_table,
            second_half * cos_table + first_half * sin_table,
        ],
        axis=-1,
    )


def gating(gate_part, up_part):
    return jax.nn.silu(gate_part) * up_part


def ancestry(parent_row, seg_count):
    identity = jnp.eye(seg_count, dtype=f32)
    parent_hot = (parent_row[:, None] == jnp.arange(seg_count, dtype=jnp.int32)[None, :]).astype(
        f32
    )
    reachable = identity
    for _ in range(seg_count - 1):
        reachable = jnp.maximum(identity, jnp.dot(parent_hot, reachable))
    return reachable


def matmul(left, right):
    return jnp.dot(left, right, preferred_element_type=f32)


def dot_last(left, right):
    return lax.dot_general(left, right, (((1,), (1,)), ((), ())), preferred_element_type=f32)


def dot_first(left, right):
    return lax.dot_general(left, right, (((0,), (0,)), ((), ())), preferred_element_type=f32)


def greet(rank, last):
    barrier = pltpu.get_barrier_semaphore()
    a = rank // 2

    def hail(other):
        pl.semaphore_signal(barrier, inc=1, device_id={"expert": other}, device_id_type=MESH)

    hail(rank + 1 - 2 * (rank % 2))

    @pl.when(a < last)
    def _():
        hail(rank + 2)

    @pl.when(a > 0)
    def _():
        hail(rank - 2)

    pl.semaphore_wait(barrier, 1 + (a + last - 1) // last + (2 * last - 1 - a) // last)


class Chain:
    def __init__(self, chunks, x_ref, o_ref, sx, rx, su, ru, sd, rd):
        self.chunks, self.x, self.o = chunks, x_ref, o_ref
        self.sems = (sx, rx, su, ru, sd, rd)
        self.rank = lax.axis_index("expert")
        self.last = o_ref.shape[0] // 2 - 1
        self.a = self.rank // 2
        self.side = self.rank + 1 - 2 * (self.rank % 2)
        self.rows = x_ref.shape[0] // chunks

    def piece(self, ref, c):
        return ref.at[pl.ds(c * self.rows, self.rows)]

    def to(self, src, block, c, send, recv, target):
        return pltpu.make_async_remote_copy(
            src_ref=src,
            dst_ref=self.piece(self.o.at[block], c),
            send_sem=send,
            recv_sem=recv,
            device_id={"expert": target},
            device_id_type=MESH,
        )

    def start(self):
        sx, rx, su, ru, sd, rd = self.sems
        rank, a, last, to = self.rank, self.a, self.last, self.to
        for c in range(self.chunks):
            own = self.piece(self.x, c)
            to(own, rank, c, sx.at[0, c], rx.at[0, c], self.side).start()

            @pl.when(a < last)
            def _():
                to(own, rank, c, su.at[0, c], ru.at[0, c], rank + 2).start()

            @pl.when(a > 0)
            def _():
                to(own, rank, c, sd.at[0, c], rd.at[0, c], rank - 2).start()

    def step(self, s):
        sx, rx, su, ru, sd, rd = self.sems
        rank, a, last, to = self.rank, self.a, self.last, self.to
        for c in range(self.chunks):

            @pl.when(a >= s)
            def _():
                block = rank - 2 * s
                src = self.piece(self.o.at[block], c)
                to(src, block, c, su.at[s - 1, c], ru.at[s - 1, c], rank + 2).wait_recv()
                to(src, block, c, sx.at[s, c], rx.at[s, c], self.side).start()

                @pl.when(a < last)
                def _():
                    to(src, block, c, su.at[s, c], ru.at[s, c], rank + 2).start()

            @pl.when(a + s <= last)
            def _():
                block = rank + 2 * s
                src = self.piece(self.o.at[block], c)
                to(src, block, c, sd.at[s - 1, c], rd.at[s - 1, c], rank - 2).wait_recv()
                to(src, block, c, sx.at[last + s, c], rx.at[last + s, c], self.side).start()

                @pl.when(a > 0)
                def _():
                    to(src, block, c, sd.at[s, c], rd.at[s, c], rank - 2).start()

    def finish(self):
        sx, rx, su, ru, sd, rd = self.sems
        rank, a, last, to, side = self.rank, self.a, self.last, self.to, self.side
        for c in range(self.chunks):
            own = self.piece(self.x, c)
            to(own, side, c, sx.at[0, c], rx.at[0, c], side).wait()

            @pl.when(a < last)
            def _():
                to(own, rank, c, su.at[0, c], ru.at[0, c], rank + 2).wait_send()

            @pl.when(a > 0)
            def _():
                to(own, rank, c, sd.at[0, c], rd.at[0, c], rank - 2).wait_send()

        for s in range(1, last + 1):
            for c in range(self.chunks):

                @pl.when(a >= s)
                def _():
                    block = rank - 2 * s
                    src = self.piece(self.o.at[block], c)
                    to(src, side - 2 * s, c, sx.at[s, c], rx.at[s, c], side).wait()

                    @pl.when(a < last)
                    def _():
                        to(src, block, c, su.at[s, c], ru.at[s, c], rank + 2).wait_send()

                @pl.when(a + s <= last)
                def _():
                    block = rank + 2 * s
                    src = self.piece(self.o.at[block], c)
                    to(src, side + 2 * s, c, sx.at[last + s, c], rx.at[last + s, c], side).wait()

                    @pl.when(a > 0)
                    def _():
                        to(src, block, c, sd.at[s, c], rd.at[s, c], rank - 2).wait_send()


def chain_sems(count, chunks):
    half = count // 2
    dma = pltpu.SemaphoreType.DMA
    return [dma((2 * half, chunks))] * 2 + [dma((half, chunks))] * 4


class Share:
    def __init__(self, ref, send_out, recv_out, send_pass, recv_pass):
        self.ref = ref
        self.sems = (send_out, recv_out, send_pass, recv_pass)
        self.line = lax.axis_index("dp")
        self.count = ref.shape[0] // 2

    def out(self, k):
        peer = 2 * lax.rem(self.line // 2 + k, self.count) + self.line % 2
        return pltpu.make_async_remote_copy(
            src_ref=self.ref.at[self.line],
            dst_ref=self.ref.at[self.line],
            send_sem=self.sems[0].at[k],
            recv_sem=self.sems[1].at[k],
            device_id={"dp": peer},
            device_id_type=MESH,
        )

    def hand(self, k):
        slab = 2 * lax.rem(self.line // 2 + self.count - k, self.count) + self.line % 2
        return pltpu.make_async_remote_copy(
            src_ref=self.ref.at[slab],
            dst_ref=self.ref.at[slab],
            send_sem=self.sems[2].at[k],
            recv_sem=self.sems[3].at[k],
            device_id={"dp": self.line + 1 - 2 * (self.line % 2)},
            device_id_type=MESH,
        )

    def start(self):
        for k in range(1, self.count):
            self.out(k).start()
        self.hand(0).start()

    def middle(self):
        for k in range(1, self.count):
            self.out(k).wait_recv()
            self.hand(k).start()

    def finish(self):
        for k in range(1, self.count):
            self.out(k).wait_send()
        for k in range(self.count):
            self.hand(k).wait()


def prologue_kernel(
    chunks,
    x_ref,
    w_ref,
    d_ref,
    t_ref,
    o_ref,
    pk_ref,
    do_ref,
    to_ref,
    wa_s,
    wa_r,
    ta_s,
    ta_r,
    da_s,
    da_r,
    *sems,
):
    group, spread = o_ref.shape[0], pk_ref.shape[0]
    packs, downs = Share(pk_ref, *sems[:4]), Share(do_ref, *sems[4:8])
    chain = Chain(chunks, x_ref, o_ref, *sems[8:])
    rank, line = chain.rank, packs.line
    mine = rank % 2
    barrier = pltpu.get_barrier_semaphore()
    for k in range(1, group):
        pl.semaphore_signal(
            barrier,
            inc=1,
            device_id={"expert": lax.rem(rank + k, group)},
            device_id_type=MESH,
        )
    for k in range(1, packs.count):
        peer = 2 * lax.rem(line // 2 + k, packs.count) + line % 2
        pl.semaphore_signal(barrier, inc=1, device_id={"dp": peer}, device_id_type=MESH)
    pl.semaphore_signal(
        barrier, inc=1, device_id={"dp": line + 1 - 2 * (line % 2)}, device_id_type=MESH
    )
    pl.semaphore_wait(barrier, group - 1 + packs.count)

    def far(src, dst, send, recv, peer):
        return pltpu.make_async_remote_copy(
            src_ref=src,
            dst_ref=dst,
            send_sem=send,
            recv_sem=recv,
            device_id={"expert": peer},
            device_id_type=MESH,
        )

    def cut(k):
        peer = lax.rem(rank + k, group)
        return far(w_ref.at[peer], pk_ref.at[line, rank], wa_s.at[k - 1], wa_r.at[k - 1], peer)

    def gates(k):
        peer = lax.rem(rank + k, group)
        return far(t_ref, to_ref.at[rank], ta_s.at[k - 1], ta_r.at[k - 1], peer)

    def down():
        return far(d_ref, do_ref.at[line, mine], da_s.at[0], da_r.at[0], chain.side)

    down().start()
    for k in range(1, group):
        cut(k).start()
        gates(k).start()
    chain.start()
    pk_ref[line, rank] = w_ref[rank]
    do_ref[line, mine] = d_ref[...]
    to_ref[rank] = t_ref[...]
    o_ref[rank] = x_ref[...]
    down().wait_recv()
    downs.start()
    for k in range(1, group):
        cut(k).wait_recv()
    packs.start()
    for s in range(1, chain.last):
        chain.step(s)
    downs.middle()
    packs.middle()
    chain.step(chain.last)
    chain.finish()
    down().wait_send()
    for k in range(1, group):
        cut(k).wait_send()
        gates(k).wait()
    downs.finish()
    packs.finish()


def prologue(x, cuts, down, gates, spread, call_id, chunks=2):
    group = cuts.shape[0]
    dma = pltpu.SemaphoreType.DMA
    vmem = pl.BlockSpec(memory_space=pltpu.VMEM)
    return pl.pallas_call(
        functools.partial(prologue_kernel, chunks),
        out_shape=[
            jax.ShapeDtypeStruct((group,) + x.shape, x.dtype),
            jax.ShapeDtypeStruct((spread,) + cuts.shape, cuts.dtype),
            jax.ShapeDtypeStruct((spread, 2) + down.shape, down.dtype),
            jax.ShapeDtypeStruct((group,) + gates.shape, gates.dtype),
        ],
        in_specs=[vmem] * 4,
        out_specs=[vmem] * 4,
        scratch_shapes=[dma((group - 1,))] * 4
        + [dma((1,))] * 2
        + [dma((spread // 2,))] * 8
        + chain_sems(group, chunks),
        compiler_params=pltpu.CompilerParams(
            collective_id=call_id, has_side_effects=True, vmem_limit_bytes=VMEM_LIMIT
        ),
        cost_estimate=WIRE,
        name="prologue",
    )(x, cuts, down, gates)


def ring_pairs(group):
    half = group // 2
    side = [(r, r + 1 - 2 * (r % 2)) for r in range(group)]
    onward = [(2 * a + b, 2 * ((a + 1) % half) + b) for a in range(half) for b in range(2)]
    return side, onward


def tie(*values):
    return lax.optimization_barrier(values)


def reduce_kernel(parts, *refs):
    n = len(parts)
    p_refs, o_refs = refs[:n], refs[n : 2 * n]
    bufs = [refs[2 * n + 4 * k : 2 * n + 4 * k + 4] for k in range(n)]
    acc, sxs, rxs, sus, rus, sds, rds = refs[6 * n :]
    rank = lax.axis_index("expert")
    last = p_refs[0].shape[0] // 2 - 1
    a = rank // 2
    b = rank % 2
    greet(rank, last)
    h = a // 2
    order = [3 - 3 * h, 2 - h, 4 * h + 1 - a, a]
    pieces = []
    for k, chunks in enumerate(parts):
        rows = p_refs[k].shape[1] // chunks
        pieces += [(k, c * rows, rows) for c in range(chunks)]

    def copy(src, dst, send, recv, target):
        return pltpu.make_async_remote_copy(
            src_ref=src,
            dst_ref=dst,
            send_sem=send,
            recv_sem=recv,
            device_id={"expert": target},
            device_id_type=MESH,
        )

    for t in order:
        for c, (k, at, rows) in enumerate(pieces):
            src = p_refs[k].at[2 * t + 1 - b, pl.ds(at, rows)]
            dst = bufs[k][0].at[t, pl.ds(at, rows)]
            copy(src, dst, sxs.at[t, c], rxs.at[t, c], rank + 1 - 2 * b).start()

    def moves(t, c, k, at, rows):
        cut = pl.ds(at, rows)
        rx, st, ru, rd = (buf.at[t, cut] for buf in bufs[k])
        src = p_refs[k].at[2 * t + 1 - b, cut]
        across = copy(src, rx, sxs.at[t, c], rxs.at[t, c], rank + 1 - 2 * b)
        upward = copy(st, ru, sus.at[t, c], rus.at[t, c], rank + 2)
        downward = copy(st, rd, sds.at[t, c], rds.at[t, c], rank - 2)
        return rx, st, ru, rd, across, upward, downward

    for t in order:
        for c, (k, at, rows) in enumerate(pieces):
            rx, st, ru, rd, across, upward, downward = moves(t, c, k, at, rows)
            width = p_refs[k].shape[2]
            total = acc.at[pl.ds(0, rows), pl.ds(0, width)]
            across.wait_recv()
            total[...] = p_refs[k][2 * t + b, pl.ds(at, rows)].astype(f32) + rx[...].astype(f32)

            @pl.when((t >= a) & (a > 0))
            def _():
                upward.wait_recv()
                total[...] += ru[...].astype(f32)

            @pl.when((t <= a) & (a < last))
            def _():
                downward.wait_recv()
                total[...] += rd[...].astype(f32)

            @pl.when(t == a)
            def _():
                o_refs[k][pl.ds(at, rows)] = total[...]

            @pl.when(t > a)
            def _():
                st[...] = total[...].astype(bf16)
                upward.start()

            @pl.when(t < a)
            def _():
                st[...] = total[...].astype(bf16)
                downward.start()

    for t in order:
        for c, (k, at, rows) in enumerate(pieces):
            rx, st, ru, rd, across, upward, downward = moves(t, c, k, at, rows)
            across.wait_send()

            @pl.when(t > a)
            def _():
                upward.wait_send()

            @pl.when(t < a)
            def _():
                downward.wait_send()


def reduce_rows(operands, call_id, most):
    half = operands[0].shape[0] // 2
    parts = [
        max(c for c in range(1, most + 1) if p.shape[1] % (16 * c) == 0 and p.shape[1] // c >= 16)
        if p.shape[1] > 64
        else 1
        for p in operands
    ]
    high = max(p.shape[1] // c for p, c in zip(operands, parts))
    wide = max(p.shape[2] for p in operands)
    sem = pltpu.SemaphoreType.DMA((half, sum(parts)))
    vmem = pl.BlockSpec(memory_space=pltpu.VMEM)
    bufs = [
        pltpu.VMEM((half,) + p.shape[1:], p.dtype) for p in operands for _ in range(4)
    ]
    return pl.pallas_call(
        functools.partial(reduce_kernel, parts),
        out_shape=[jax.ShapeDtypeStruct(p.shape[1:], f32) for p in operands],
        in_specs=[vmem] * len(operands),
        out_specs=[vmem] * len(operands),
        scratch_shapes=bufs + [pltpu.VMEM((high, wide), f32)] + [sem] * 6,
        compiler_params=pltpu.CompilerParams(
            collective_id=call_id, has_side_effects=True, vmem_limit_bytes=VMEM_LIMIT
        ),
        cost_estimate=pl.CostEstimate(
            flops=0, bytes_accessed=36 * sum(p.size for p in operands) * 2, transcendentals=0
        ),
        name="reduce_rows",
    )(*operands)


def swap_halves(values):
    lane = lax.broadcasted_iota(jnp.int32, values.shape, 1)
    half = ROPE // 2
    return jnp.where(lane < half, pltpu.roll(values, KEY - NOPE - half, 1), pltpu.roll(values, half, 1))


def turns(seg_cos, seg_sin, off_cos, off_sin):
    lane = lax.broadcasted_iota(jnp.int32, off_cos.shape, 1)
    sine = seg_sin * off_cos + seg_cos * off_sin
    return seg_cos * off_cos - seg_sin * off_sin, jnp.where(lane < ROPE // 2, -sine, sine)


def project_kernel(
    heads,
    x_ref,
    wq_ref,
    wl_ref,
    we_ref,
    ag_ref,
    lg_ref,
    sc_ref,
    ss_ref,
    oc_ref,
    os_ref,
    h1_ref,
    q_ref,
    k_ref,
    v_ref,
    lat_ref,
    ckv_ref,
):
    i = pl.program_id(0)
    x = x_ref[...].astype(f32)
    power = jnp.mean(x * x, axis=-1, keepdims=True)
    h1 = (x * lax.rsqrt(power + epsilon) * ag_ref[...]).astype(bf16)
    h1_ref[...] = h1
    cosine, sine = turns(sc_ref[pl.ds(i, 1)], ss_ref[pl.ds(i, 1)], oc_ref[...], os_ref[...])

    def turn(values):
        return (values * cosine + swap_halves(values) * sine).astype(bf16)

    query = matmul(h1, wq_ref[...])
    for h in range(heads):
        at = h * KEY
        q_ref[:, at : at + NOPE] = query[:, at : at + NOPE].astype(bf16)
        q_ref[:, at + NOPE : at + KEY] = turn(query[:, at + NOPE : at + KEY])
    latent = matmul(h1, wl_ref[...])
    lat_ref[...] = latent
    low = latent[:, :KV]
    power = jnp.mean(low * low, axis=-1, keepdims=True)
    ckv = (low * lax.rsqrt(power + epsilon) * lg_ref[...]).astype(bf16)
    ckv_ref[...] = ckv
    krope = turn(latent[:, KV:])
    kv = matmul(ckv, we_ref[...]).astype(bf16)
    for h in range(heads):
        at = h * KEY
        k_ref[:, at : at + NOPE] = kv[:, at : at + NOPE]
        k_ref[:, at + NOPE : at + KEY] = krope
        v_ref[:, h * VD : (h + 1) * VD] = kv[:, at + NOPE : at + KEY]


def project(x, packed, lat_pack, we, a_gain, l_gain, tables, heads):
    tree, width = x.shape
    segs = tree // SEG
    lat_width = lat_pack.shape[1]
    fixed = lambda arr: pl.BlockSpec(arr.shape, lambda i: (0, 0))
    part = lambda cols: pl.BlockSpec((SEG, cols), lambda i: (i, 0))
    return pl.pallas_call(
        functools.partial(project_kernel, heads),
        grid=(segs,),
        in_specs=[
            part(width),
            pl.BlockSpec((width, heads * KEY), lambda i: (0, 0)),
            fixed(lat_pack),
            fixed(we),
            fixed(a_gain),
            fixed(l_gain),
        ]
        + [fixed(table) for table in tables],
        out_specs=[
            part(width),
            part(heads * KEY),
            part(heads * KEY),
            part(heads * VD),
            part(lat_width),
            part(KV),
        ],
        out_shape=[
            jax.ShapeDtypeStruct((tree, width), bf16),
            jax.ShapeDtypeStruct((tree, heads * KEY), bf16),
            jax.ShapeDtypeStruct((tree, heads * KEY), bf16),
            jax.ShapeDtypeStruct((tree, heads * VD), bf16),
            jax.ShapeDtypeStruct((tree, lat_width), f32),
            jax.ShapeDtypeStruct((tree, KV), bf16),
        ],
        compiler_params=pltpu.CompilerParams(vmem_limit_bytes=VMEM_LIMIT),
        cost_estimate=pl.CostEstimate(flops=0, bytes_accessed=60_000_000, transcendentals=0),
        name="project",
    )(x, packed, lat_pack, we, a_gain, l_gain, *tables)


def triangle():
    keys = lax.broadcasted_iota(jnp.int32, (SEG, SEG), 0)
    queries = lax.broadcasted_iota(jnp.int32, (SEG, SEG), 1)
    return keys <= queries


def attend_kernel(
    heads, segs, scale, reach_ref, q_ref, k_ref, v_ref, out_ref, full_ref, log_ref, m_s, l_s, acc_s
):
    i = pl.program_id(0)
    diag = triangle()

    def score(h, j):
        keys = k_ref[pl.ds(j * SEG, SEG), h * KEY : (h + 1) * KEY]
        return dot_last(keys, q_ref[:, h * KEY : (h + 1) * KEY]) * scale

    def weigh(h, j, weights):
        vals = v_ref[pl.ds(j * SEG, SEG), h * VD : (h + 1) * VD]
        return dot_first(vals, weights.astype(bf16))

    for h in range(heads):
        s = jnp.where(diag, score(h, i), -1e30)
        top = jnp.max(s, axis=0, keepdims=True)
        w = jnp.where(diag, jnp.exp(s - top), 0.0)
        m_s[h : h + 1] = top
        l_s[h : h + 1] = jnp.sum(w, axis=0, keepdims=True)
        acc_s[h] = weigh(h, i, w)

    def step(j, carry):
        @pl.when(reach_ref[i * segs + j] > 0)
        def _():
            for h in range(heads):
                s = score(h, j)
                old = m_s[h : h + 1]
                top = jnp.maximum(old, jnp.max(s, axis=0, keepdims=True))
                w = jnp.exp(s - top)
                fade = jnp.exp(old - top)
                m_s[h : h + 1] = top
                l_s[h : h + 1] = l_s[h : h + 1] * fade + jnp.sum(w, axis=0, keepdims=True)
                acc_s[h] = acc_s[h] * fade + weigh(h, j, w)

        return carry

    lax.fori_loop(0, i, step, 0)
    for h in range(heads):
        total = l_s[h : h + 1]
        rows = (acc_s[h] * (1.0 / total)).T
        full_ref[:, h * VD : (h + 1) * VD] = rows
        out_ref[:, h * VD : (h + 1) * VD] = rows.astype(bf16)
        log_ref[h : h + 1] = m_s[h : h + 1] + jnp.log(total)


def attend(reach, q, k, v, scale):
    tree = q.shape[0]
    segs = tree // SEG
    heads = q.shape[1] // KEY
    whole = lambda width: pl.BlockSpec((tree, width), lambda i, r: (0, 0))
    part = lambda width: pl.BlockSpec((SEG, width), lambda i, r: (i, 0))
    return pl.pallas_call(
        functools.partial(attend_kernel, heads, segs, scale),
        grid_spec=pltpu.PrefetchScalarGridSpec(
            num_scalar_prefetch=1,
            grid=(segs,),
            in_specs=[part(heads * KEY), whole(heads * KEY), whole(heads * VD)],
            out_specs=[
                part(heads * VD),
                part(heads * VD),
                pl.BlockSpec((heads, SEG), lambda i, r: (0, i)),
            ],
            scratch_shapes=[
                pltpu.VMEM((heads, SEG), f32),
                pltpu.VMEM((heads, SEG), f32),
                pltpu.VMEM((heads, VD, SEG), f32),
            ],
        ),
        out_shape=[
            jax.ShapeDtypeStruct((tree, heads * VD), bf16),
            jax.ShapeDtypeStruct((tree, heads * VD), f32),
            jax.ShapeDtypeStruct((heads, tree), f32),
        ],
        compiler_params=pltpu.CompilerParams(vmem_limit_bytes=VMEM_LIMIT),
        cost_estimate=pl.CostEstimate(flops=0, bytes_accessed=70_000_000, transcendentals=0),
        name="attend",
    )(reach, q, k, v)


def attend_back_kernel(
    heads,
    segs,
    scale,
    reach_ref,
    q_ref,
    k_ref,
    v_ref,
    g_ref,
    att_ref,
    log_ref,
    we_ref,
    sc_ref,
    ss_ref,
    oc_ref,
    os_ref,
    gq_ref,
    dkv_ref,
    lat_ref,
    dq_s,
    dk_s,
    dv_s,
    delta_s,
):
    j = pl.program_id(0)
    diag = triangle()

    @pl.when(j == 0)
    def _():
        def prepare(i, carry):
            rows = pl.ds(i * SEG, SEG)
            for h in range(heads):
                vcols = slice(h * VD, (h + 1) * VD)
                both = g_ref[rows, vcols].astype(f32) * att_ref[rows, vcols]
                delta_s[h : h + 1, rows] = jnp.sum(both.T, axis=0, keepdims=True)
            dq_s[rows] = jnp.zeros((SEG, heads * KEY), f32)
            return carry

        lax.fori_loop(0, segs, prepare, 0)

    dk_s[...] = jnp.zeros_like(dk_s)
    dv_s[...] = jnp.zeros_like(dv_s)

    def block(i, masked):
        rows = pl.ds(i * SEG, SEG)
        for h in range(heads):
            kcols = slice(h * KEY, (h + 1) * KEY)
            vcols = slice(h * VD, (h + 1) * VD)
            q = q_ref[rows, kcols]
            k = k_ref[:, kcols]
            g = g_ref[rows, vcols]
            s = dot_last(k, q) * scale
            w = jnp.exp(s - log_ref[h : h + 1, rows])
            if masked:
                w = jnp.where(diag, w, 0.0)
            dw = dot_last(v_ref[:, vcols], g)
            ds = (w * (dw - delta_s[h : h + 1, rows])).astype(bf16)
            dv_s[h] += matmul(w.astype(bf16), g)
            dk_s[h] += matmul(ds, q)
            dq_s[rows, kcols] += dot_first(ds, k)

    block(j, True)

    def step(i, carry):
        @pl.when(reach_ref[i * segs + j] > 0)
        def _():
            block(i, False)

        return carry

    lax.fori_loop(j + 1, segs, step, 0)
    rope = jnp.zeros((SEG, KEY - NOPE), f32)
    for h in range(heads):
        dkv_ref[:, h * KEY : h * KEY + NOPE] = (dk_s[h, :, :NOPE] * scale).astype(bf16)
        dkv_ref[:, h * KEY + NOPE : (h + 1) * KEY] = dv_s[h].astype(bf16)
        rope = rope + dk_s[h, :, NOPE:]
    lat_ref[:, :KV] = dot_last(dkv_ref[...], we_ref[...]).astype(bf16)
    lat_ref[:, KV:] = (rope * scale).astype(bf16)

    @pl.when(j == segs - 1)
    def _():
        def finish(i, carry):
            rows = pl.ds(i * SEG, SEG)
            cosine, sine = turns(
                sc_ref[pl.ds(i, 1)], ss_ref[pl.ds(i, 1)], oc_ref[...], os_ref[...]
            )
            for h in range(heads):
                at = h * KEY
                gq_ref[rows, at : at + NOPE] = (dq_s[rows, at : at + NOPE] * scale).astype(bf16)
                turned = dq_s[rows, at + NOPE : at + KEY] * scale
                gq_ref[rows, at + NOPE : at + KEY] = (
                    turned * cosine - swap_halves(turned) * sine
                ).astype(bf16)
            return carry

        lax.fori_loop(0, segs, finish, 0)


def attend_back(reach, q, k, v, g, attended, log_total, we, tables, scale):
    tree = q.shape[0]
    segs = tree // SEG
    heads = q.shape[1] // KEY
    whole = lambda width: pl.BlockSpec((tree, width), lambda j, r: (0, 0))
    part = lambda width: pl.BlockSpec((SEG, width), lambda j, r: (j, 0))
    fixed = lambda arr: pl.BlockSpec(arr.shape, lambda j, r: (0, 0))
    lat_width = KV + KEY - NOPE
    return pl.pallas_call(
        functools.partial(attend_back_kernel, heads, segs, scale),
        grid_spec=pltpu.PrefetchScalarGridSpec(
            num_scalar_prefetch=1,
            grid=(segs,),
            in_specs=[
                whole(heads * KEY),
                part(heads * KEY),
                part(heads * VD),
                whole(heads * VD),
                whole(heads * VD),
                fixed(log_total),
                fixed(we),
            ]
            + [fixed(table) for table in tables],
            out_specs=[whole(heads * KEY), part(heads * KEY), part(lat_width)],
            scratch_shapes=[
                pltpu.VMEM((tree, heads * KEY), f32),
                pltpu.VMEM((heads, SEG, KEY), f32),
                pltpu.VMEM((heads, SEG, VD), f32),
                pltpu.VMEM((heads, tree), f32),
            ],
        ),
        out_shape=[
            jax.ShapeDtypeStruct((tree, heads * KEY), bf16),
            jax.ShapeDtypeStruct((tree, heads * KEY), bf16),
            jax.ShapeDtypeStruct((tree, lat_width), bf16),
        ],
        compiler_params=pltpu.CompilerParams(vmem_limit_bytes=VMEM_LIMIT),
        cost_estimate=pl.CostEstimate(flops=0, bytes_accessed=90_000_000, transcendentals=0),
        name="attend_back",
    )(reach, q, k, v, g, attended, log_total, we, *tables)


def per_device(
    tokens,
    grad_out,
    routes,
    gate_values,
    parents,
    attn_gain,
    w_query,
    w_latent,
    latent_gain,
    w_expand,
    w_output,
    ffn_gain,
    shared_gate,
    shared_up,
    shared_down,
    expert_gate,
    expert_up,
    expert_down,
):
    group = lax.axis_size("expert")
    spread = lax.axis_size("dp")
    rank = lax.axis_index("expert")
    tok_dev, width = tokens.shape
    tree = tok_dev * group
    segs = parents.shape[1]
    per_token = routes.shape[1]
    capacity = tok_dev * per_token * 9 // (8 * group)
    slots = -(-capacity // 16) * 16
    scale = (NOPE + ROPE) ** (-0.5)
    mine = HEADS // group
    rows_w = w_query.shape[0]
    rows_l = w_expand.shape[0]
    ff_cut = shared_down.shape[0]
    half = group // 2
    ff_own = 2 * ff_cut * spread
    ff_pad = -(-ff_own // 128) * 128
    q_own = mine * KEY
    e_own = mine * (NOPE + VD)
    e_fold = rows_l * e_own // rows_w

    wq_cut = jnp.pad(
        w_query.reshape(rows_w, group, mine, NOPE + ROPE),
        ((0, 0), (0, 0), (0, 0), (0, KEY - NOPE - ROPE)),
    ).reshape(rows_w, group, q_own)

    def ff_columns(weight):
        cut = weight.reshape(rows_w, spread, half, 2 * ff_cut).transpose(2, 0, 1, 3)
        cut = jnp.pad(
            cut.reshape(half, 1, rows_w, ff_own),
            ((0, 0), (0, 0), (0, 0), (0, ff_pad - ff_own)),
        )
        return jnp.broadcast_to(cut, (half, 2, rows_w, ff_pad)).reshape(group, rows_w, ff_pad)

    we_cut = (
        w_expand.reshape(rows_l, group, e_own).transpose(1, 0, 2).reshape(group, rows_w, e_fold)
    )
    packed = jnp.concatenate(
        [
            wq_cut.transpose(1, 0, 2),
            we_cut,
            ff_columns(shared_gate),
            ff_columns(shared_up),
        ],
        axis=2,
    )
    expert_ids = jnp.arange(group, dtype=jnp.int32)
    gate_of = jnp.sum(
        jnp.where(routes[:, :, None] == expert_ids[None, None, :], gate_values[:, :, None], 0.0),
        axis=1,
    ).T
    x_all, packed, sd, gate_of = prologue(tokens, packed, shared_down, gate_of, spread, 0)
    x_all, parents, gate_of = lax.optimization_barrier(
        (x_all.reshape(tree, width), parents, gate_of)
    )
    packed = packed.reshape(width, -1)
    wq = packed[:, :q_own]
    we = packed[:, q_own : q_own + e_fold].reshape(KV, e_own)
    sg = packed[:, q_own + e_fold : q_own + e_fold + ff_pad]
    su = packed[:, q_own + e_fold + ff_pad :]
    sd = jnp.pad(sd.reshape(ff_own, width), ((0, ff_pad - ff_own), (0, 0)))

    lat_w = KV + ROPE
    gains = jnp.stack(
        [attn_gain, ffn_gain, jnp.pad(latent_gain, (0, rows_w - rows_l))], axis=1
    )
    gains = jnp.pad(gains, ((0, 0), (0, ROPE - 3)))
    lat_pack = lax.all_gather(
        jnp.concatenate([w_latent, gains], axis=1), EVERY, axis=0, tiled=True
    )
    wl = lat_pack[:, :lat_w]
    a_gain = lat_pack[:, lat_w].astype(f32)
    f_gain = lat_pack[:, lat_w + 1].astype(f32)
    l_gain = lat_pack[:, lat_w + 2].reshape(-1, rows_w)[:, :rows_l].reshape(KV).astype(f32)
    wo = lax.all_gather(w_output, EVERY, axis=0, tiled=True)
    reachable = ancestry(parents[0], segs)
    depth = jnp.sum(reachable, axis=1) - 1.0
    reach = reachable.astype(jnp.int32).reshape(segs * segs)
    half_width = ROPE // 2
    freq = 10000.0 ** (-2.0 * jnp.arange(half_width, dtype=f32) / ROPE)
    seg_angle = (depth * SEG)[:, None] * freq[None, :]
    off_angle = jnp.arange(SEG, dtype=f32)[:, None] * freq[None, :]

    def lanes(values):
        return jnp.pad(
            jnp.concatenate([values, values], axis=1), ((0, 0), (0, KEY - NOPE - ROPE))
        )

    tables = [
        lanes(jnp.cos(seg_angle)),
        lanes(jnp.sin(seg_angle)),
        lanes(jnp.cos(off_angle)),
        lanes(jnp.sin(off_angle)),
    ]
    seg_cos = lax.dynamic_slice_in_dim(tables[0], rank, 1, 0)[:, :half_width]
    seg_sin = lax.dynamic_slice_in_dim(tables[1], rank, 1, 0)[:, :half_width]
    off_cos = tables[2][:, :half_width]
    off_sin = tables[3][:, :half_width]
    own_cos = seg_cos * off_cos - seg_sin * off_sin
    own_sin = seg_sin * off_cos + seg_cos * off_sin

    def own(values):
        return lax.dynamic_slice_in_dim(values, rank * tok_dev, tok_dev, 0)

    h1, q_att, k_att, v_att, latent, ckv = project(
        x_all, packed, lat_pack, we, a_gain[None], l_gain[None], tables, mine
    )
    side, ring = ring_pairs(group)

    def across(values):
        return lax.ppermute(values, "expert", side)

    def onward(values):
        return lax.ppermute(values, "expert", ring)

    def behind(values, s, far):
        at = 2 * lax.rem(rank // 2 - s + half, half) + lax.rem(rank + far, 2)
        return lax.dynamic_index_in_dim(values, at, 0, keepdims=False)

    def line_swap(values, m):
        own_bit = lax.rem(lax.axis_index("dp") // (1 << m), 2)
        at = spread.bit_length() - 2 - m
        keep = lax.dynamic_index_in_dim(values, own_bit, at, False)
        send = lax.dynamic_index_in_dim(values, 1 - own_bit, at, False)
        swap = [(d, d ^ (1 << m)) for d in range(spread)]
        return keep, lax.ppermute(send, "dp", swap)

    def both_halves(keep, other):
        return (keep.astype(f32) + other.astype(f32)).astype(bf16)

    q_att, g0 = tie(q_att, grad_out)
    g1 = onward(g0)
    attn_heads, attended, log_total = attend(reach, q_att, k_att, v_att, scale)
    attn_heads, g1 = tie(attn_heads, g1)
    g2 = onward(g1)
    attn_own = lax.all_to_all(attn_heads, "expert", split_axis=0, concat_axis=1, tiled=True)
    tokens_f = tokens.astype(f32)
    resid = tokens_f + matmul(attn_own, wo)
    second_normed, second_norm_back = jax.vjp(norm_rows, resid, f_gain)
    b0 = second_normed.astype(bf16)

    b1 = onward(b0)
    gate_of = jnp.concatenate(
        [
            lax.dynamic_slice(
                gate_of,
                (2 * lax.rem(rank // 2 - s + half, half) + rank % 2, rank + k - 2 * k * (rank % 2), 0),
                (1, 1, tok_dev),
            )[0]
            for s in range(half)
            for k in range(2)
        ],
        axis=0,
    )
    routed = gate_of > 0.0
    upto = (
        jnp.arange(tok_dev, dtype=jnp.int32)[:, None]
        <= jnp.arange(tok_dev, dtype=jnp.int32)[None, :]
    )
    place = matmul(routed.astype(bf16), upto.astype(bf16)).astype(jnp.int32) - 1
    chosen = (
        place[:, None, :] == jnp.arange(slots, dtype=jnp.int32)[None, :, None]
    ) & routed[:, None, :]
    pick_all = chosen.astype(bf16).reshape(half, 2 * slots, tok_dev)
    gates_all = jnp.sum(jnp.where(chosen, gate_of[:, None, :], 0.0), axis=2).reshape(
        half, 2 * slots, 1
    )

    def take(s, rows, weights=None):
        picked = matmul(pick_all[s], rows)
        if weights is not None:
            picked = picked * weights
        return picked.astype(bf16)

    def shared(h2, g_rows):
        s_act, s_gating_back = jax.vjp(gating, matmul(h2, sg), matmul(h2, su))
        s_act = s_act.astype(bf16)
        grad_s_act = dot_last(g_rows, sd).astype(bf16)
        gate_part, up_part = s_gating_back(grad_s_act.astype(f32))
        gate_part = gate_part.astype(bf16)
        up_part = up_part.astype(bf16)
        near = dot_last(gate_part, sg) + dot_last(up_part, su)
        return near, s_act, gate_part, up_part

    def expert(e_rows, e_grad):
        activated, e_gating_back = jax.vjp(
            gating, matmul(e_rows, expert_gate[0]), matmul(e_rows, expert_up[0])
        )
        activated = activated.astype(bf16)
        grad_e_act = dot_last(e_grad, expert_down[0]).astype(bf16)
        gate_part, up_part = e_gating_back(grad_e_act.astype(f32))
        gate_part = gate_part.astype(bf16)
        up_part = up_part.astype(bf16)
        grad_rows = (
            dot_last(gate_part, expert_gate[0]) + dot_last(up_part, expert_up[0])
        ).astype(bf16)
        return grad_rows, activated, gate_part, up_part

    def join(mine, arrived):
        return jnp.concatenate([mine[:slots], arrived], axis=0)

    def spread_back(s, near, mine, arrived, *more):
        total = near + dot_first(pick_all[s], join(mine, arrived))
        for other in more:
            total = total + other.astype(f32)
        return total

    e0 = take(0, b0)
    e0_in = across(e0[slots:])
    w0, w1 = (take(s, g, gates_all[s]) for s, g in enumerate((g0, g1)))
    w0_in, w1_in = (across(w[slots:]) for w in (w0, w1))
    n0_near, *s0 = shared(b0, g0)
    n0_near, b1, e0_in, w0_in, w1_in, g2 = tie(n0_near, b1, e0_in, w0_in, w1_in, g2)
    b2, g3 = onward(b1), onward(g2)
    w2 = take(2, g2, gates_all[2])
    w2_in = across(w2[slots:])
    e1 = take(1, b1)
    e1_in = across(e1[slots:])
    r0, w0 = join(e0, e0_in), join(w0, w0_in)
    n0, *k0 = expert(r0, w0)
    n0, b1, e1_in, w2_in = tie(n0, b1, e1_in, w2_in)
    n0_in = across(n0[slots:])
    n1_near, *s1 = shared(b1, g1)
    n1_near, b2, e1_in, n0_in, w2_in, g3 = tie(n1_near, b2, e1_in, n0_in, w2_in, g3)
    w3 = take(3, g3, gates_all[3])
    w3_in = across(w3[slots:])
    b3 = onward(b2)
    e2 = take(2, b2)
    e2_in = across(e2[slots:])
    r1, w1 = join(e1, e1_in), join(w1, w1_in)
    n1, *k1 = expert(r1, w1)
    n1, b2, e2_in, w3_in = tie(n1, b2, e2_in, w3_in)
    n1_in = across(n1[slots:])
    n2_near, *s2 = shared(b2, g2)
    n2_near, b3, e2_in, n1_in, w3_in = tie(n2_near, b3, e2_in, n1_in, w3_in)
    ring1 = onward(spread_back(1, n1_near, n1, n1_in).astype(bf16))
    e3 = take(3, b3)
    e3_in = across(e3[slots:])
    r2, w2 = join(e2, e2_in), join(w2, w2_in)
    n2, *k2 = expert(r2, w2)
    n2, b3, e3_in = tie(n2, b3, e3_in)
    n2_in = across(n2[slots:])
    n3_near, *s3 = shared(b3, g3)
    n3_near, e3_in, n2_in, ring1 = tie(n3_near, e3_in, n2_in, ring1)
    ring2 = onward(spread_back(2, n2_near, n2, n2_in, ring1).astype(bf16))
    r3, w3 = join(e3, e3_in), join(w3, w3_in)
    n3, *k3 = expert(r3, w3)
    n3, ring2 = tie(n3, ring2)
    n3_in = across(n3[slots:])
    s_act, s_gate_part, s_up_part = (
        jnp.concatenate(pieces, axis=0) for pieces in zip(s0, s1, s2, s3)
    )
    b_all = jnp.concatenate([b0, b1, b2, b3], axis=0)
    g_all = jnp.concatenate([g0, g1, g2, g3], axis=0)
    grad_s_cols = dot_first(b_all, jnp.concatenate([s_gate_part, s_up_part], axis=1)).astype(bf16)
    grad_s_cols, n3_in = tie(grad_s_cols, n3_in)
    ring3 = onward(spread_back(3, n3_near, n3, n3_in, ring2).astype(bf16))
    e_rows = jnp.concatenate([r0, r1, r2, r3], axis=0)
    e_grad = jnp.concatenate([w0, w1, w2, w3], axis=0)
    activated, gate_part, up_part = (
        jnp.concatenate(pieces, axis=0) for pieces in zip(k0, k1, k2, k3)
    )
    grad_e_gate = dot_first(e_rows, gate_part).astype(bf16)
    grad_e_up = dot_first(e_rows, up_part).astype(bf16)
    e_result = matmul(activated, expert_down[0]).astype(bf16).reshape(half, 2 * slots, width)
    grad_s_down = dot_first(s_act, g_all).astype(bf16)
    grad_e_gate, grad_e_up, ring3, activated, s_act, e_result, grad_s_down = tie(
        grad_e_gate, grad_e_up, ring3, activated, s_act, e_result, grad_s_down
    )
    grad_second = spread_back(0, n0_near, n0, n0_in, ring3)
    o_in = across(e_result[:, slots:])
    grad_e_down = dot_first(activated, e_grad).astype(bf16)

    def out_term(s, *more):
        weighed = (join(e_result[s], o_in[s]).astype(f32) * gates_all[s]).astype(bf16)
        total = matmul(s_act[s * tok_dev : (s + 1) * tok_dev], sd) + dot_first(
            pick_all[s], weighed
        )
        for other in more:
            total = total + other.astype(f32)
        return total

    grad_e_gate = lax.psum_scatter(grad_e_gate, "dp", scatter_dimension=0, tiled=True)
    grad_e_up = lax.psum_scatter(grad_e_up, "dp", scatter_dimension=0, tiled=True)
    grad_e_down_all, grad_s_down = grad_e_down, grad_s_down[:ff_own]

    def sum_columns(grads):
        return lax.psum_scatter(grads, "dp", scatter_dimension=0, tiled=True)

    grad_s_cols = sum_columns(grad_s_cols)

    def ff_restore(cut):
        both = cut[:, :, :ff_own].astype(f32).reshape(half, 2, rows_w, spread, 2 * ff_cut)
        return (both[:, 0] + both[:, 1]).transpose(1, 2, 0, 3).reshape(rows_w, -1)

    grad_f = grad_out.astype(f32)
    grad_resid_norm, grad_f_gain = second_norm_back(grad_second)
    grad_resid = grad_f + grad_resid_norm
    grad_attn_out = grad_resid.astype(bf16)
    grad_w_out = dot_first(attn_own, grad_attn_out).astype(bf16)
    grad_attended = dot_last(grad_attn_out, wo).astype(bf16)
    grad_heads = lax.all_to_all(grad_attended, "expert", split_axis=1, concat_axis=0, tiled=True)
    grad_heads, o_in, grad_w_out, grad_s_cols, grad_e_down, grad_s_down, grad_e_gate = tie(
        grad_heads,
        o_in,
        grad_w_out,
        grad_s_cols,
        grad_e_down_all,
        grad_s_down,
        grad_e_gate,
    )
    s_keep, s_other = line_swap(
        grad_s_down.reshape((2,) * (spread.bit_length() - 1) + (2, ff_cut, width)), 0
    )
    grad_heads, o1 = tie(grad_heads, out_term(1).astype(bf16))
    ring1 = onward(o1)
    grad_s_cut = lax.all_to_all(
        grad_s_cols.reshape(group, rows_w, -1), "expert", split_axis=0, concat_axis=0, tiled=True
    )
    grad_w_out = lax.psum_scatter(grad_w_out, "dp", scatter_dimension=0, tiled=True)
    grad_q_lin, grad_kv, lat_part = attend_back(
        reach, q_att, k_att, v_att, grad_heads, attended, log_total, we, tables, scale
    )
    lat_part, grad_q_lin, ring1, grad_e_down, s_other = tie(
        lat_part, grad_q_lin, ring1, grad_e_down, s_other
    )
    ring2 = onward(out_term(2, ring1).astype(bf16))
    grad_s_down = both_halves(s_keep, s_other)
    for m in range(1, spread.bit_length() - 1):
        s_keep, s_other = line_swap(grad_s_down, m)
        if m < spread.bit_length() - 2:
            grad_s_down = both_halves(s_keep, s_other)
    (grad_lat_sum,) = reduce_rows([lat_part.reshape(group, tok_dev, -1)], 5, 2)
    grad_lat_sum, grad_q_lin, ring2, s_other, grad_w_out, grad_e_down = tie(
        grad_lat_sum, grad_q_lin, ring2, s_other, grad_w_out, grad_e_down
    )
    grad_s_down = both_halves(s_keep, s_other)
    own_side = rank % 2
    s_keep = lax.dynamic_index_in_dim(grad_s_down, own_side, 0, False)
    s_other = across(lax.dynamic_index_in_dim(grad_s_down, 1 - own_side, 0, False))
    ring3 = onward(out_term(3, ring2).astype(bf16))
    first_part = dot_last(grad_q_lin, wq).astype(bf16).reshape(group, tok_dev, width)
    steps = list(range(1, half)) + [0]
    w_blocks = grad_w_out.reshape(group, rows_w, width)
    w_in = across(jnp.stack([behind(w_blocks, s, 1) for s in steps]))

    def ring_term(blocks, arrived, k, *more):
        total = behind(blocks, steps[k], 0).astype(f32) + arrived[k].astype(f32)
        for other in more:
            total = total + other.astype(f32)
        return total

    def latent_parts(latent_in, gain_vec):
        return (
            norm_rows(latent_in[:, :KV], gain_vec),
            rotate(latent_in[:, KV : KV + ROPE], own_cos, own_sin),
        )

    unused, latent_back = jax.vjp(latent_parts, own(latent), l_gain)
    grad_latent, grad_l_gain = latent_back(
        (grad_lat_sum[:, :KV], grad_lat_sum[:, KV : KV + ROPE])
    )
    grad_latent = grad_latent.astype(bf16)
    grad_w_lat = dot_first(own(h1), grad_latent)[:, : KV + ROPE]
    grad_gains = jnp.stack(
        [
            grad_f_gain,
            jnp.pad(grad_l_gain.reshape(-1, rows_l), ((0, 0), (0, rows_w - rows_l))).reshape(width),
        ],
        axis=1,
    )
    lat_grads_in = jnp.concatenate(
        [grad_w_lat, jnp.pad(grad_gains, ((0, 0), (0, ROPE - 2)))], axis=1
    ).astype(bf16)
    first_part, lat_grads, w_in, grad_q_lin = tie(first_part, lat_grads_in, w_in, grad_q_lin)
    lat_grads = lax.psum_scatter(lat_grads, "dp", scatter_dimension=0, tiled=True)
    w_ring = onward(ring_term(w_blocks, w_in, 0).astype(bf16))
    grad_a_cols = jnp.concatenate(
        [dot_first(h1, grad_q_lin), dot_first(ckv, grad_kv).reshape(width, e_fold)], axis=1
    ).astype(bf16)
    first_part, grad_a_cols, w_ring = tie(first_part, grad_a_cols, w_ring)
    grad_a_cols = lax.psum_scatter(grad_a_cols, "dp", scatter_dimension=0, tiled=True)
    w_ring = onward(ring_term(w_blocks, w_in, 1, w_ring).astype(bf16))
    grad_e_down = lax.psum_scatter(grad_e_down, "dp", scatter_dimension=1, tiled=True)
    (first_sum,) = reduce_rows([first_part], 6, 4)
    (
        first_sum,
        lat_grads,
        ring3,
        w_ring,
        s_keep,
        s_other,
        grad_a_cols,
        grad_s_cut,
        grad_e_gate,
        grad_e_up,
    ) = tie(
        first_sum,
        lat_grads,
        ring3,
        w_ring,
        s_keep,
        s_other,
        grad_a_cols,
        grad_s_cut,
        grad_e_gate,
        grad_e_up,
    )
    w_ring = onward(ring_term(w_blocks, w_in, 2, w_ring).astype(bf16))
    lat_blocks = lat_grads.reshape(group, rows_w, -1)
    lat_in = across(jnp.stack([behind(lat_blocks, s, 1) for s in steps]))
    grad_first = first_sum + dot_last(grad_latent[:, :lat_w], wl)
    unused, first_norm_back = jax.vjp(lambda v: norm_rows(v, a_gain), tokens_f)
    (grad_tokens_norm,) = first_norm_back(grad_first)
    grad_tokens = grad_resid + grad_tokens_norm
    grad_tokens, lat_in, w_ring = tie(grad_tokens, lat_in, w_ring)
    grad_w_out = ring_term(w_blocks, w_in, 3, w_ring)
    lat_ring = onward(ring_term(lat_blocks, lat_in, 0).astype(bf16))
    block_out = (resid + out_term(0, ring3)).astype(bf16)
    block_out, lat_ring = tie(block_out, lat_ring)
    lat_ring = onward(ring_term(lat_blocks, lat_in, 1, lat_ring).astype(bf16))
    grad_s_gate = ff_restore(grad_s_cut[:, :, :ff_pad])
    grad_s_up = ff_restore(grad_s_cut[:, :, ff_pad:])
    grad_s_gate, grad_s_up, lat_ring = tie(grad_s_gate, grad_s_up, lat_ring)
    lat_ring = onward(ring_term(lat_blocks, lat_in, 2, lat_ring).astype(bf16))
    lat_grads = ring_term(lat_blocks, lat_in, 3, lat_ring)
    grad_s_down = s_keep.astype(f32) + s_other.astype(f32)
    grad_w_lat = lat_grads[:, :lat_w]
    grad_f_gain = lat_grads[:, lat_w]
    grad_l_gain = lat_grads[:rows_l, lat_w + 1]
    grad_a_cols = lax.all_to_all(
        grad_a_cols.reshape(group, rows_w, -1), "expert", split_axis=0, concat_axis=0, tiled=True
    )
    grad_w_q = (
        grad_a_cols[:, :, :q_own]
        .reshape(group, rows_w, mine, KEY)[..., : NOPE + ROPE]
        .transpose(1, 0, 2, 3)
        .reshape(rows_w, -1)
        .astype(f32)
    )
    grad_w_exp = (
        grad_a_cols[:, :, q_own:]
        .reshape(group, rows_l, e_own)
        .transpose(1, 0, 2)
        .reshape(rows_l, -1)
        .astype(f32)
    )
    grad_a_gain = (
        jnp.sum(grad_w_q * w_query.astype(f32), axis=1)
        + jnp.sum(grad_w_lat * w_latent.astype(f32), axis=1)
    ) / attn_gain.astype(f32)

    return (
        block_out,
        grad_tokens,
        grad_a_gain,
        grad_w_q,
        grad_w_lat,
        grad_l_gain,
        grad_w_exp,
        grad_w_out,
        grad_f_gain,
        grad_s_gate,
        grad_s_up,
        grad_s_down,
        grad_e_gate.astype(f32)[None],
        grad_e_up.astype(f32)[None],
        grad_e_down.astype(f32)[None],
    )


def solution(mesh):
    placed = (
        P(EVERY, None),
        P(EVERY, None),
        P(EVERY, None),
        P(EVERY, None),
        P("dp", None),
        P(EVERY),
        P(EVERY, None),
        P(EVERY, None),
        P(EVERY),
        P(EVERY, None),
        P(EVERY, None),
        P(EVERY),
        P(EVERY, None),
        P(EVERY, None),
        P(EVERY, None),
        P("expert", None, None),
        P("expert", None, None),
        P("expert", None, None),
    )
    return jax.shard_map(
        per_device,
        mesh=mesh,
        in_specs=placed,
        out_specs=(
            P(EVERY, None),
            P(EVERY, None),
            P(EVERY),
            P(EVERY, None),
            P(EVERY, None),
            P(EVERY),
            P(EVERY, None),
            P(EVERY, None),
            P(EVERY),
            P(EVERY, None),
            P(EVERY, None),
            P(EVERY, None),
            P("expert", "dp", None),
            P("expert", "dp", None),
            P("expert", None, "dp"),
        ),
        check_vma=False,
    )
```

```python
import functools

import jax
import jax.numpy as jnp
from jax import lax
from jax.experimental import pallas as pl
from jax.experimental.pallas import tpu as pltpu
from jax.sharding import PartitionSpec as P

HEADS = 16
NOPE = 128
ROPE = 64
KV = 512
VD = 128
SEG = 256
KEY = 256

epsilon = 1e-06
bf16 = jnp.bfloat16
f32 = jnp.float32
EVERY = ("dp", "expert")
MESH = pl.DeviceIdType.MESH
VMEM_LIMIT = 60 << 20
WIRE = pl.CostEstimate(flops=0, bytes_accessed=300_000_000, transcendentals=0)


def norm_rows(values, gain_vec):
    return (
        values * lax.rsqrt(jnp.mean(values * values, axis=-1, keepdims=True) + epsilon) * gain_vec
    )


def rotate(values, cos_table, sin_table):
    half_width = values.shape[-1] // 2
    first_half = values[..., :half_width]
    second_half = values[..., half_width:]
    return jnp.concatenate(
        [
            first_half * cos_table - second_half * sin_table,
            second_half * cos_table + first_half * sin_table,
        ],
        axis=-1,
    )


def gating(gate_part, up_part):
    return jax.nn.silu(gate_part) * up_part


def ancestry(parent_row, seg_count):
    identity = jnp.eye(seg_count, dtype=f32)
    parent_hot = (parent_row[:, None] == jnp.arange(seg_count, dtype=jnp.int32)[None, :]).astype(
        f32
    )
    reachable = identity
    for _ in range(seg_count - 1):
        reachable = jnp.maximum(identity, jnp.dot(parent_hot, reachable))
    return reachable


def matmul(left, right):
    return jnp.dot(left, right, preferred_element_type=f32)


def dot_last(left, right):
    return lax.dot_general(left, right, (((1,), (1,)), ((), ())), preferred_element_type=f32)


def dot_first(left, right):
    return lax.dot_general(left, right, (((0,), (0,)), ((), ())), preferred_element_type=f32)


def greet(rank, last):
    barrier = pltpu.get_barrier_semaphore()
    a = rank // 2

    def hail(other):
        pl.semaphore_signal(barrier, inc=1, device_id={"expert": other}, device_id_type=MESH)

    hail(rank + 1 - 2 * (rank % 2))

    @pl.when(a < last)
    def _():
        hail(rank + 2)

    @pl.when(a > 0)
    def _():
        hail(rank - 2)

    pl.semaphore_wait(barrier, 1 + (a + last - 1) // last + (2 * last - 1 - a) // last)


class Chain:
    def __init__(self, chunks, x_ref, o_ref, sx, rx, su, ru, sd, rd):
        self.chunks, self.x, self.o = chunks, x_ref, o_ref
        self.sems = (sx, rx, su, ru, sd, rd)
        self.rank = lax.axis_index("expert")
        self.last = o_ref.shape[0] // 2 - 1
        self.a = self.rank // 2
        self.side = self.rank + 1 - 2 * (self.rank % 2)
        self.rows = x_ref.shape[0] // chunks

    def piece(self, ref, c):
        return ref.at[pl.ds(c * self.rows, self.rows)]

    def to(self, src, block, c, send, recv, target):
        return pltpu.make_async_remote_copy(
            src_ref=src,
            dst_ref=self.piece(self.o.at[block], c),
            send_sem=send,
            recv_sem=recv,
            device_id={"expert": target},
            device_id_type=MESH,
        )

    def start(self):
        sx, rx, su, ru, sd, rd = self.sems
        rank, a, last, to = self.rank, self.a, self.last, self.to
        for c in range(self.chunks):
            own = self.piece(self.x, c)
            to(own, rank, c, sx.at[0, c], rx.at[0, c], self.side).start()

            @pl.when(a < last)
            def _():
                to(own, rank, c, su.at[0, c], ru.at[0, c], rank + 2).start()

            @pl.when(a > 0)
            def _():
                to(own, rank, c, sd.at[0, c], rd.at[0, c], rank - 2).start()

    def step(self, s):
        sx, rx, su, ru, sd, rd = self.sems
        rank, a, last, to = self.rank, self.a, self.last, self.to
        for c in range(self.chunks):

            @pl.when(a >= s)
            def _():
                block = rank - 2 * s
                src = self.piece(self.o.at[block], c)
                to(src, block, c, su.at[s - 1, c], ru.at[s - 1, c], rank + 2).wait_recv()
                to(src, block, c, sx.at[s, c], rx.at[s, c], self.side).start()

                @pl.when(a < last)
                def _():
                    to(src, block, c, su.at[s, c], ru.at[s, c], rank + 2).start()

            @pl.when(a + s <= last)
            def _():
                block = rank + 2 * s
                src = self.piece(self.o.at[block], c)
                to(src, block, c, sd.at[s - 1, c], rd.at[s - 1, c], rank - 2).wait_recv()
                to(src, block, c, sx.at[last + s, c], rx.at[last + s, c], self.side).start()

                @pl.when(a > 0)
                def _():
                    to(src, block, c, sd.at[s, c], rd.at[s, c], rank - 2).start()

    def finish(self):
        sx, rx, su, ru, sd, rd = self.sems
        rank, a, last, to, side = self.rank, self.a, self.last, self.to, self.side
        for c in range(self.chunks):
            own = self.piece(self.x, c)
            to(own, side, c, sx.at[0, c], rx.at[0, c], side).wait()

            @pl.when(a < last)
            def _():
                to(own, rank, c, su.at[0, c], ru.at[0, c], rank + 2).wait_send()

            @pl.when(a > 0)
            def _():
                to(own, rank, c, sd.at[0, c], rd.at[0, c], rank - 2).wait_send()

        for s in range(1, last + 1):
            for c in range(self.chunks):

                @pl.when(a >= s)
                def _():
                    block = rank - 2 * s
                    src = self.piece(self.o.at[block], c)
                    to(src, side - 2 * s, c, sx.at[s, c], rx.at[s, c], side).wait()

                    @pl.when(a < last)
                    def _():
                        to(src, block, c, su.at[s, c], ru.at[s, c], rank + 2).wait_send()

                @pl.when(a + s <= last)
                def _():
                    block = rank + 2 * s
                    src = self.piece(self.o.at[block], c)
                    to(src, side + 2 * s, c, sx.at[last + s, c], rx.at[last + s, c], side).wait()

                    @pl.when(a > 0)
                    def _():
                        to(src, block, c, sd.at[s, c], rd.at[s, c], rank - 2).wait_send()


def chain_sems(count, chunks):
    half = count // 2
    dma = pltpu.SemaphoreType.DMA
    return [dma((2 * half, chunks))] * 2 + [dma((half, chunks))] * 4


class Share:
    def __init__(self, ref, send_out, recv_out, send_pass, recv_pass):
        self.ref = ref
        self.sems = (send_out, recv_out, send_pass, recv_pass)
        self.line = lax.axis_index("dp")
        self.count = ref.shape[0] // 2

    def out(self, k):
        peer = 2 * lax.rem(self.line // 2 + k, self.count) + self.line % 2
        return pltpu.make_async_remote_copy(
            src_ref=self.ref.at[self.line],
            dst_ref=self.ref.at[self.line],
            send_sem=self.sems[0].at[k],
            recv_sem=self.sems[1].at[k],
            device_id={"dp": peer},
            device_id_type=MESH,
        )

    def hand(self, k):
        slab = 2 * lax.rem(self.line // 2 + self.count - k, self.count) + self.line % 2
        return pltpu.make_async_remote_copy(
            src_ref=self.ref.at[slab],
            dst_ref=self.ref.at[slab],
            send_sem=self.sems[2].at[k],
            recv_sem=self.sems[3].at[k],
            device_id={"dp": self.line + 1 - 2 * (self.line % 2)},
            device_id_type=MESH,
        )

    def start(self):
        for k in range(1, self.count):
            self.out(k).start()
        self.hand(0).start()

    def middle(self):
        for k in range(1, self.count):
            self.out(k).wait_recv()
            self.hand(k).start()

    def finish(self):
        for k in range(1, self.count):
            self.out(k).wait_send()
        for k in range(self.count):
            self.hand(k).wait()


def prologue_kernel(
    chunks,
    x_ref,
    w_ref,
    d_ref,
    t_ref,
    o_ref,
    pk_ref,
    do_ref,
    to_ref,
    wa_s,
    wa_r,
    ta_s,
    ta_r,
    da_s,
    da_r,
    *sems,
):
    group, spread = o_ref.shape[0], pk_ref.shape[0]
    packs, downs = Share(pk_ref, *sems[:4]), Share(do_ref, *sems[4:8])
    chain = Chain(chunks, x_ref, o_ref, *sems[8:])
    rank, line = chain.rank, packs.line
    mine = rank % 2
    barrier = pltpu.get_barrier_semaphore()
    for k in range(1, group):
        pl.semaphore_signal(
            barrier,
            inc=1,
            device_id={"expert": lax.rem(rank + k, group)},
            device_id_type=MESH,
        )
    for k in range(1, packs.count):
        peer = 2 * lax.rem(line // 2 + k, packs.count) + line % 2
        pl.semaphore_signal(barrier, inc=1, device_id={"dp": peer}, device_id_type=MESH)
    pl.semaphore_signal(
        barrier, inc=1, device_id={"dp": line + 1 - 2 * (line % 2)}, device_id_type=MESH
    )
    pl.semaphore_wait(barrier, group - 1 + packs.count)

    def far(src, dst, send, recv, peer):
        return pltpu.make_async_remote_copy(
            src_ref=src,
            dst_ref=dst,
            send_sem=send,
            recv_sem=recv,
            device_id={"expert": peer},
            device_id_type=MESH,
        )

    def cut(k):
        peer = lax.rem(rank + k, group)
        return far(w_ref.at[peer], pk_ref.at[line, rank], wa_s.at[k - 1], wa_r.at[k - 1], peer)

    def gates(k):
        peer = lax.rem(rank + k, group)
        return far(t_ref, to_ref.at[rank], ta_s.at[k - 1], ta_r.at[k - 1], peer)

    def down():
        return far(d_ref, do_ref.at[line, mine], da_s.at[0], da_r.at[0], chain.side)

    down().start()
    for k in range(1, group):
        cut(k).start()
        gates(k).start()
    chain.start()
    pk_ref[line, rank] = w_ref[rank]
    do_ref[line, mine] = d_ref[...]
    to_ref[rank] = t_ref[...]
    o_ref[rank] = x_ref[...]
    down().wait_recv()
    downs.start()
    for k in range(1, group):
        cut(k).wait_recv()
    packs.start()
    for s in range(1, chain.last):
        chain.step(s)
    downs.middle()
    packs.middle()
    chain.step(chain.last)
    chain.finish()
    down().wait_send()
    for k in range(1, group):
        cut(k).wait_send()
        gates(k).wait()
    downs.finish()
    packs.finish()


def prologue(x, cuts, down, gates, spread, call_id, chunks=2):
    group = cuts.shape[0]
    dma = pltpu.SemaphoreType.DMA
    vmem = pl.BlockSpec(memory_space=pltpu.VMEM)
    return pl.pallas_call(
        functools.partial(prologue_kernel, chunks),
        out_shape=[
            jax.ShapeDtypeStruct((group,) + x.shape, x.dtype),
            jax.ShapeDtypeStruct((spread,) + cuts.shape, cuts.dtype),
            jax.ShapeDtypeStruct((spread, 2) + down.shape, down.dtype),
            jax.ShapeDtypeStruct((group,) + gates.shape, gates.dtype),
        ],
        in_specs=[vmem] * 4,
        out_specs=[vmem] * 4,
        scratch_shapes=[dma((group - 1,))] * 4
        + [dma((1,))] * 2
        + [dma((spread // 2,))] * 8
        + chain_sems(group, chunks),
        compiler_params=pltpu.CompilerParams(
            collective_id=call_id, has_side_effects=True, vmem_limit_bytes=VMEM_LIMIT
        ),
        cost_estimate=WIRE,
        name="prologue",
    )(x, cuts, down, gates)


def ring_pairs(group):
    half = group // 2
    side = [(r, r + 1 - 2 * (r % 2)) for r in range(group)]
    onward = [(2 * a + b, 2 * ((a + 1) % half) + b) for a in range(half) for b in range(2)]
    return side, onward


def tie(*values):
    return lax.optimization_barrier(values)


def reduce_kernel(parts, *refs):
    n = len(parts)
    p_refs, o_refs = refs[:n], refs[n : 2 * n]
    bufs = [refs[2 * n + 4 * k : 2 * n + 4 * k + 4] for k in range(n)]
    acc, sxs, rxs, sus, rus, sds, rds = refs[6 * n :]
    rank = lax.axis_index("expert")
    last = p_refs[0].shape[0] // 2 - 1
    a = rank // 2
    b = rank % 2
    greet(rank, last)
    h = a // 2
    order = [3 - 3 * h, 2 - h, 4 * h + 1 - a, a]
    pieces = []
    for k, chunks in enumerate(parts):
        rows = p_refs[k].shape[1] // chunks
        pieces += [(k, c * rows, rows) for c in range(chunks)]

    def copy(src, dst, send, recv, target):
        return pltpu.make_async_remote_copy(
            src_ref=src,
            dst_ref=dst,
            send_sem=send,
            recv_sem=recv,
            device_id={"expert": target},
            device_id_type=MESH,
        )

    for t in order:
        for c, (k, at, rows) in enumerate(pieces):
            src = p_refs[k].at[2 * t + 1 - b, pl.ds(at, rows)]
            dst = bufs[k][0].at[t, pl.ds(at, rows)]
            copy(src, dst, sxs.at[t, c], rxs.at[t, c], rank + 1 - 2 * b).start()

    def moves(t, c, k, at, rows):
        cut = pl.ds(at, rows)
        rx, st, ru, rd = (buf.at[t, cut] for buf in bufs[k])
        src = p_refs[k].at[2 * t + 1 - b, cut]
        across = copy(src, rx, sxs.at[t, c], rxs.at[t, c], rank + 1 - 2 * b)
        upward = copy(st, ru, sus.at[t, c], rus.at[t, c], rank + 2)
        downward = copy(st, rd, sds.at[t, c], rds.at[t, c], rank - 2)
        return rx, st, ru, rd, across, upward, downward

    for t in order:
        for c, (k, at, rows) in enumerate(pieces):
            rx, st, ru, rd, across, upward, downward = moves(t, c, k, at, rows)
            width = p_refs[k].shape[2]
            total = acc.at[pl.ds(0, rows), pl.ds(0, width)]
            across.wait_recv()
            total[...] = p_refs[k][2 * t + b, pl.ds(at, rows)].astype(f32) + rx[...].astype(f32)

            @pl.when((t >= a) & (a > 0))
            def _():
                upward.wait_recv()
                total[...] += ru[...].astype(f32)

            @pl.when((t <= a) & (a < last))
            def _():
                downward.wait_recv()
                total[...] += rd[...].astype(f32)

            @pl.when(t == a)
            def _():
                o_refs[k][pl.ds(at, rows)] = total[...]

            @pl.when(t > a)
            def _():
                st[...] = total[...].astype(bf16)
                upward.start()

            @pl.when(t < a)
            def _():
                st[...] = total[...].astype(bf16)
                downward.start()

    for t in order:
        for c, (k, at, rows) in enumerate(pieces):
            rx, st, ru, rd, across, upward, downward = moves(t, c, k, at, rows)
            across.wait_send()

            @pl.when(t > a)
            def _():
                upward.wait_send()

            @pl.when(t < a)
            def _():
                downward.wait_send()


def reduce_rows(operands, call_id, most):
    half = operands[0].shape[0] // 2
    parts = [
        max(c for c in range(1, most + 1) if p.shape[1] % (16 * c) == 0 and p.shape[1] // c >= 16)
        if p.shape[1] > 64
        else 1
        for p in operands
    ]
    high = max(p.shape[1] // c for p, c in zip(operands, parts))
    wide = max(p.shape[2] for p in operands)
    sem = pltpu.SemaphoreType.DMA((half, sum(parts)))
    vmem = pl.BlockSpec(memory_space=pltpu.VMEM)
    bufs = [
        pltpu.VMEM((half,) + p.shape[1:], p.dtype) for p in operands for _ in range(4)
    ]
    return pl.pallas_call(
        functools.partial(reduce_kernel, parts),
        out_shape=[jax.ShapeDtypeStruct(p.shape[1:], f32) for p in operands],
        in_specs=[vmem] * len(operands),
        out_specs=[vmem] * len(operands),
        scratch_shapes=bufs + [pltpu.VMEM((high, wide), f32)] + [sem] * 6,
        compiler_params=pltpu.CompilerParams(
            collective_id=call_id, has_side_effects=True, vmem_limit_bytes=VMEM_LIMIT
        ),
        cost_estimate=pl.CostEstimate(
            flops=0, bytes_accessed=36 * sum(p.size for p in operands) * 2, transcendentals=0
        ),
        name="reduce_rows",
    )(*operands)


def swap_halves(values):
    lane = lax.broadcasted_iota(jnp.int32, values.shape, 1)
    half = ROPE // 2
    return jnp.where(lane < half, pltpu.roll(values, KEY - NOPE - half, 1), pltpu.roll(values, half, 1))


def turns(seg_cos, seg_sin, off_cos, off_sin):
    lane = lax.broadcasted_iota(jnp.int32, off_cos.shape, 1)
    sine = seg_sin * off_cos + seg_cos * off_sin
    return seg_cos * off_cos - seg_sin * off_sin, jnp.where(lane < ROPE // 2, -sine, sine)


def project_kernel(
    heads,
    x_ref,
    wq_ref,
    wl_ref,
    we_ref,
    ag_ref,
    lg_ref,
    sc_ref,
    ss_ref,
    oc_ref,
    os_ref,
    h1_ref,
    q_ref,
    k_ref,
    v_ref,
    lat_ref,
    ckv_ref,
):
    i = pl.program_id(0)
    x = x_ref[...].astype(f32)
    power = jnp.mean(x * x, axis=-1, keepdims=True)
    h1 = (x * lax.rsqrt(power + epsilon) * ag_ref[...]).astype(bf16)
    h1_ref[...] = h1
    cosine, sine = turns(sc_ref[pl.ds(i, 1)], ss_ref[pl.ds(i, 1)], oc_ref[...], os_ref[...])

    def turn(values):
        return (values * cosine + swap_halves(values) * sine).astype(bf16)

    query = matmul(h1, wq_ref[...])
    for h in range(heads):
        at = h * KEY
        q_ref[:, at : at + NOPE] = query[:, at : at + NOPE].astype(bf16)
        q_ref[:, at + NOPE : at + KEY] = turn(query[:, at + NOPE : at + KEY])
    latent = matmul(h1, wl_ref[...])
    lat_ref[...] = latent
    low = latent[:, :KV]
    power = jnp.mean(low * low, axis=-1, keepdims=True)
    ckv = (low * lax.rsqrt(power + epsilon) * lg_ref[...]).astype(bf16)
    ckv_ref[...] = ckv
    krope = turn(latent[:, KV:])
    kv = matmul(ckv, we_ref[...]).astype(bf16)
    for h in range(heads):
        at = h * KEY
        k_ref[:, at : at + NOPE] = kv[:, at : at + NOPE]
        k_ref[:, at + NOPE : at + KEY] = krope
        v_ref[:, h * VD : (h + 1) * VD] = kv[:, at + NOPE : at + KEY]


def project(x, packed, lat_pack, we, a_gain, l_gain, tables, heads):
    tree, width = x.shape
    segs = tree // SEG
    lat_width = lat_pack.shape[1]
    fixed = lambda arr: pl.BlockSpec(arr.shape, lambda i: (0, 0))
    part = lambda cols: pl.BlockSpec((SEG, cols), lambda i: (i, 0))
    return pl.pallas_call(
        functools.partial(project_kernel, heads),
        grid=(segs,),
        in_specs=[
            part(width),
            pl.BlockSpec((width, heads * KEY), lambda i: (0, 0)),
            fixed(lat_pack),
            fixed(we),
            fixed(a_gain),
            fixed(l_gain),
        ]
        + [fixed(table) for table in tables],
        out_specs=[
            part(width),
            part(heads * KEY),
            part(heads * KEY),
            part(heads * VD),
            part(lat_width),
            part(KV),
        ],
        out_shape=[
            jax.ShapeDtypeStruct((tree, width), bf16),
            jax.ShapeDtypeStruct((tree, heads * KEY), bf16),
            jax.ShapeDtypeStruct((tree, heads * KEY), bf16),
            jax.ShapeDtypeStruct((tree, heads * VD), bf16),
            jax.ShapeDtypeStruct((tree, lat_width), f32),
            jax.ShapeDtypeStruct((tree, KV), bf16),
        ],
        compiler_params=pltpu.CompilerParams(vmem_limit_bytes=VMEM_LIMIT),
        cost_estimate=pl.CostEstimate(flops=0, bytes_accessed=60_000_000, transcendentals=0),
        name="project",
    )(x, packed, lat_pack, we, a_gain, l_gain, *tables)


def triangle():
    keys = lax.broadcasted_iota(jnp.int32, (SEG, SEG), 0)
    queries = lax.broadcasted_iota(jnp.int32, (SEG, SEG), 1)
    return keys <= queries


def attend_kernel(
    heads, segs, scale, reach_ref, q_ref, k_ref, v_ref, out_ref, full_ref, log_ref, m_s, l_s, acc_s
):
    i = pl.program_id(0)
    diag = triangle()

    def score(h, j):
        keys = k_ref[pl.ds(j * SEG, SEG), h * KEY : (h + 1) * KEY]
        return dot_last(keys, q_ref[:, h * KEY : (h + 1) * KEY]) * scale

    def weigh(h, j, weights):
        vals = v_ref[pl.ds(j * SEG, SEG), h * VD : (h + 1) * VD]
        return dot_first(vals, weights.astype(bf16))

    for h in range(heads):
        s = jnp.where(diag, score(h, i), -1e30)
        top = jnp.max(s, axis=0, keepdims=True)
        w = jnp.where(diag, jnp.exp(s - top), 0.0)
        m_s[h : h + 1] = top
        l_s[h : h + 1] = jnp.sum(w, axis=0, keepdims=True)
        acc_s[h] = weigh(h, i, w)

    def step(j, carry):
        @pl.when(reach_ref[i * segs + j] > 0)
        def _():
            for h in range(heads):
                s = score(h, j)
                old = m_s[h : h + 1]
                top = jnp.maximum(old, jnp.max(s, axis=0, keepdims=True))
                w = jnp.exp(s - top)
                fade = jnp.exp(old - top)
                m_s[h : h + 1] = top
                l_s[h : h + 1] = l_s[h : h + 1] * fade + jnp.sum(w, axis=0, keepdims=True)
                acc_s[h] = acc_s[h] * fade + weigh(h, j, w)

        return carry

    lax.fori_loop(0, i, step, 0)
    for h in range(heads):
        total = l_s[h : h + 1]
        rows = (acc_s[h] * (1.0 / total)).T
        full_ref[:, h * VD : (h + 1) * VD] = rows
        out_ref[:, h * VD : (h + 1) * VD] = rows.astype(bf16)
        log_ref[h : h + 1] = m_s[h : h + 1] + jnp.log(total)


def attend(reach, q, k, v, scale):
    tree = q.shape[0]
    segs = tree // SEG
    heads = q.shape[1] // KEY
    whole = lambda width: pl.BlockSpec((tree, width), lambda i, r: (0, 0))
    part = lambda width: pl.BlockSpec((SEG, width), lambda i, r: (i, 0))
    return pl.pallas_call(
        functools.partial(attend_kernel, heads, segs, scale),
        grid_spec=pltpu.PrefetchScalarGridSpec(
            num_scalar_prefetch=1,
            grid=(segs,),
            in_specs=[part(heads * KEY), whole(heads * KEY), whole(heads * VD)],
            out_specs=[
                part(heads * VD),
                part(heads * VD),
                pl.BlockSpec((heads, SEG), lambda i, r: (0, i)),
            ],
            scratch_shapes=[
                pltpu.VMEM((heads, SEG), f32),
                pltpu.VMEM((heads, SEG), f32),
                pltpu.VMEM((heads, VD, SEG), f32),
            ],
        ),
        out_shape=[
            jax.ShapeDtypeStruct((tree, heads * VD), bf16),
            jax.ShapeDtypeStruct((tree, heads * VD), f32),
            jax.ShapeDtypeStruct((heads, tree), f32),
        ],
        compiler_params=pltpu.CompilerParams(vmem_limit_bytes=VMEM_LIMIT),
        cost_estimate=pl.CostEstimate(flops=0, bytes_accessed=70_000_000, transcendentals=0),
        name="attend",
    )(reach, q, k, v)


def attend_back_kernel(
    heads,
    segs,
    scale,
    reach_ref,
    q_ref,
    k_ref,
    v_ref,
    g_ref,
    att_ref,
    log_ref,
    we_ref,
    sc_ref,
    ss_ref,
    oc_ref,
    os_ref,
    gq_ref,
    dkv_ref,
    lat_ref,
    dq_s,
    dk_s,
    dv_s,
    delta_s,
):
    j = pl.program_id(0)
    diag = triangle()

    @pl.when(j == 0)
    def _():
        def prepare(i, carry):
            rows = pl.ds(i * SEG, SEG)
            for h in range(heads):
                vcols = slice(h * VD, (h + 1) * VD)
                both = g_ref[rows, vcols].astype(f32) * att_ref[rows, vcols]
                delta_s[h : h + 1, rows] = jnp.sum(both.T, axis=0, keepdims=True)
            dq_s[rows] = jnp.zeros((SEG, heads * KEY), f32)
            return carry

        lax.fori_loop(0, segs, prepare, 0)

    dk_s[...] = jnp.zeros_like(dk_s)
    dv_s[...] = jnp.zeros_like(dv_s)

    def block(i, masked):
        rows = pl.ds(i * SEG, SEG)
        for h in range(heads):
            kcols = slice(h * KEY, (h + 1) * KEY)
            vcols = slice(h * VD, (h + 1) * VD)
            q = q_ref[rows, kcols]
            k = k_ref[:, kcols]
            g = g_ref[rows, vcols]
            s = dot_last(k, q) * scale
            w = jnp.exp(s - log_ref[h : h + 1, rows])
            if masked:
                w = jnp.where(diag, w, 0.0)
            dw = dot_last(v_ref[:, vcols], g)
            ds = (w * (dw - delta_s[h : h + 1, rows])).astype(bf16)
            dv_s[h] += matmul(w.astype(bf16), g)
            dk_s[h] += matmul(ds, q)
            dq_s[rows, kcols] += dot_first(ds, k)

    block(j, True)

    def step(i, carry):
        @pl.when(reach_ref[i * segs + j] > 0)
        def _():
            block(i, False)

        return carry

    lax.fori_loop(j + 1, segs, step, 0)
    rope = jnp.zeros((SEG, KEY - NOPE), f32)
    for h in range(heads):
        dkv_ref[:, h * KEY : h * KEY + NOPE] = (dk_s[h, :, :NOPE] * scale).astype(bf16)
        dkv_ref[:, h * KEY + NOPE : (h + 1) * KEY] = dv_s[h].astype(bf16)
        rope = rope + dk_s[h, :, NOPE:]
    lat_ref[:, :KV] = dot_last(dkv_ref[...], we_ref[...]).astype(bf16)
    lat_ref[:, KV:] = (rope * scale).astype(bf16)

    @pl.when(j == segs - 1)
    def _():
        def finish(i, carry):
            rows = pl.ds(i * SEG, SEG)
            cosine, sine = turns(
                sc_ref[pl.ds(i, 1)], ss_ref[pl.ds(i, 1)], oc_ref[...], os_ref[...]
            )
            for h in range(heads):
                at = h * KEY
                gq_ref[rows, at : at + NOPE] = (dq_s[rows, at : at + NOPE] * scale).astype(bf16)
                turned = dq_s[rows, at + NOPE : at + KEY] * scale
                gq_ref[rows, at + NOPE : at + KEY] = (
                    turned * cosine - swap_halves(turned) * sine
                ).astype(bf16)
            return carry

        lax.fori_loop(0, segs, finish, 0)


def attend_back(reach, q, k, v, g, attended, log_total, we, tables, scale):
    tree = q.shape[0]
    segs = tree // SEG
    heads = q.shape[1] // KEY
    whole = lambda width: pl.BlockSpec((tree, width), lambda j, r: (0, 0))
    part = lambda width: pl.BlockSpec((SEG, width), lambda j, r: (j, 0))
    fixed = lambda arr: pl.BlockSpec(arr.shape, lambda j, r: (0, 0))
    lat_width = KV + KEY - NOPE
    return pl.pallas_call(
        functools.partial(attend_back_kernel, heads, segs, scale),
        grid_spec=pltpu.PrefetchScalarGridSpec(
            num_scalar_prefetch=1,
            grid=(segs,),
            in_specs=[
                whole(heads * KEY),
                part(heads * KEY),
                part(heads * VD),
                whole(heads * VD),
                whole(heads * VD),
                fixed(log_total),
                fixed(we),
            ]
            + [fixed(table) for table in tables],
            out_specs=[whole(heads * KEY), part(heads * KEY), part(lat_width)],
            scratch_shapes=[
                pltpu.VMEM((tree, heads * KEY), f32),
                pltpu.VMEM((heads, SEG, KEY), f32),
                pltpu.VMEM((heads, SEG, VD), f32),
                pltpu.VMEM((heads, tree), f32),
            ],
        ),
        out_shape=[
            jax.ShapeDtypeStruct((tree, heads * KEY), bf16),
            jax.ShapeDtypeStruct((tree, heads * KEY), bf16),
            jax.ShapeDtypeStruct((tree, lat_width), bf16),
        ],
        compiler_params=pltpu.CompilerParams(vmem_limit_bytes=VMEM_LIMIT),
        cost_estimate=pl.CostEstimate(flops=0, bytes_accessed=90_000_000, transcendentals=0),
        name="attend_back",
    )(reach, q, k, v, g, attended, log_total, we, *tables)


def per_device(
    tokens,
    grad_out,
    routes,
    gate_values,
    parents,
    attn_gain,
    w_query,
    w_latent,
    latent_gain,
    w_expand,
    w_output,
    ffn_gain,
    shared_gate,
    shared_up,
    shared_down,
    expert_gate,
    expert_up,
    expert_down,
):
    group = lax.axis_size("expert")
    spread = lax.axis_size("dp")
    rank = lax.axis_index("expert")
    tok_dev, width = tokens.shape
    tree = tok_dev * group
    segs = parents.shape[1]
    per_token = routes.shape[1]
    capacity = tok_dev * per_token * 9 // (8 * group)
    slots = -(-capacity // 16) * 16
    scale = (NOPE + ROPE) ** (-0.5)
    mine = HEADS // group
    rows_w = w_query.shape[0]
    rows_l = w_expand.shape[0]
    ff_cut = shared_down.shape[0]
    half = group // 2
    ff_own = 2 * ff_cut * spread
    ff_pad = -(-ff_own // 128) * 128
    q_own = mine * KEY
    e_own = mine * (NOPE + VD)
    e_fold = rows_l * e_own // rows_w

    wq_cut = jnp.pad(
        w_query.reshape(rows_w, group, mine, NOPE + ROPE),
        ((0, 0), (0, 0), (0, 0), (0, KEY - NOPE - ROPE)),
    ).reshape(rows_w, group, q_own)

    def ff_columns(weight):
        cut = weight.reshape(rows_w, spread, half, 2 * ff_cut).transpose(2, 0, 1, 3)
        cut = jnp.pad(
            cut.reshape(half, 1, rows_w, ff_own),
            ((0, 0), (0, 0), (0, 0), (0, ff_pad - ff_own)),
        )
        return jnp.broadcast_to(cut, (half, 2, rows_w, ff_pad)).reshape(group, rows_w, ff_pad)

    we_cut = (
        w_expand.reshape(rows_l, group, e_own).transpose(1, 0, 2).reshape(group, rows_w, e_fold)
    )
    packed = jnp.concatenate(
        [
            wq_cut.transpose(1, 0, 2),
            we_cut,
            ff_columns(shared_gate),
            ff_columns(shared_up),
        ],
        axis=2,
    )
    expert_ids = jnp.arange(group, dtype=jnp.int32)
    gate_of = jnp.sum(
        jnp.where(routes[:, :, None] == expert_ids[None, None, :], gate_values[:, :, None], 0.0),
        axis=1,
    ).T
    x_all, packed, sd, gate_of = prologue(tokens, packed, shared_down, gate_of, spread, 0)
    x_all, parents, gate_of = lax.optimization_barrier(
        (x_all.reshape(tree, width), parents, gate_of)
    )
    packed = packed.reshape(width, -1)
    wq = packed[:, :q_own]
    we = packed[:, q_own : q_own + e_fold].reshape(KV, e_own)
    sg = packed[:, q_own + e_fold : q_own + e_fold + ff_pad]
    su = packed[:, q_own + e_fold + ff_pad :]
    sd = jnp.pad(sd.reshape(ff_own, width), ((0, ff_pad - ff_own), (0, 0)))

    lat_w = KV + ROPE
    gains = jnp.stack(
        [attn_gain, ffn_gain, jnp.pad(latent_gain, (0, rows_w - rows_l))], axis=1
    )
    gains = jnp.pad(gains, ((0, 0), (0, ROPE - 3)))
    lat_pack = lax.all_gather(
        jnp.concatenate([w_latent, gains], axis=1), EVERY, axis=0, tiled=True
    )
    wl = lat_pack[:, :lat_w]
    a_gain = lat_pack[:, lat_w].astype(f32)
    f_gain = lat_pack[:, lat_w + 1].astype(f32)
    l_gain = lat_pack[:, lat_w + 2].reshape(-1, rows_w)[:, :rows_l].reshape(KV).astype(f32)
    wo = lax.all_gather(w_output, EVERY, axis=0, tiled=True)
    reachable = ancestry(parents[0], segs)
    depth = jnp.sum(reachable, axis=1) - 1.0
    reach = reachable.astype(jnp.int32).reshape(segs * segs)
    half_width = ROPE // 2
    freq = 10000.0 ** (-2.0 * jnp.arange(half_width, dtype=f32) / ROPE)
    seg_angle = (depth * SEG)[:, None] * freq[None, :]
    off_angle = jnp.arange(SEG, dtype=f32)[:, None] * freq[None, :]

    def lanes(values):
        return jnp.pad(
            jnp.concatenate([values, values], axis=1), ((0, 0), (0, KEY - NOPE - ROPE))
        )

    tables = [
        lanes(jnp.cos(seg_angle)),
        lanes(jnp.sin(seg_angle)),
        lanes(jnp.cos(off_angle)),
        lanes(jnp.sin(off_angle)),
    ]
    seg_cos = lax.dynamic_slice_in_dim(tables[0], rank, 1, 0)[:, :half_width]
    seg_sin = lax.dynamic_slice_in_dim(tables[1], rank, 1, 0)[:, :half_width]
    off_cos = tables[2][:, :half_width]
    off_sin = tables[3][:, :half_width]
    own_cos = seg_cos * off_cos - seg_sin * off_sin
    own_sin = seg_sin * off_cos + seg_cos * off_sin

    def own(values):
        return lax.dynamic_slice_in_dim(values, rank * tok_dev, tok_dev, 0)

    side, ring = ring_pairs(group)

    def across(values):
        return lax.ppermute(values, "expert", side)

    def onward(values):
        return lax.ppermute(values, "expert", ring)

    x_all, g0 = tie(x_all, grad_out)
    g1 = onward(g0)
    h1, q_att, k_att, v_att, latent, ckv = project(
        x_all, packed, lat_pack, we, a_gain[None], l_gain[None], tables, mine
    )
    def behind(values, s, far):
        at = 2 * lax.rem(rank // 2 - s + half, half) + lax.rem(rank + far, 2)
        return lax.dynamic_index_in_dim(values, at, 0, keepdims=False)

    def line_swap(values, m):
        own_bit = lax.rem(lax.axis_index("dp") // (1 << m), 2)
        at = spread.bit_length() - 2 - m
        keep = lax.dynamic_index_in_dim(values, own_bit, at, False)
        send = lax.dynamic_index_in_dim(values, 1 - own_bit, at, False)
        swap = [(d, d ^ (1 << m)) for d in range(spread)]
        return keep, lax.ppermute(send, "dp", swap)

    def both_halves(keep, other):
        return (keep.astype(f32) + other.astype(f32)).astype(bf16)

    gate_of = jnp.concatenate(
        [
            lax.dynamic_slice(
                gate_of,
                (2 * lax.rem(rank // 2 - s + half, half) + rank % 2, rank + k - 2 * k * (rank % 2), 0),
                (1, 1, tok_dev),
            )[0]
            for s in range(half)
            for k in range(2)
        ],
        axis=0,
    )
    routed = gate_of > 0.0
    upto = (
        jnp.arange(tok_dev, dtype=jnp.int32)[:, None]
        <= jnp.arange(tok_dev, dtype=jnp.int32)[None, :]
    )
    place = matmul(routed.astype(bf16), upto.astype(bf16)).astype(jnp.int32) - 1
    chosen = (
        place[:, None, :] == jnp.arange(slots, dtype=jnp.int32)[None, :, None]
    ) & routed[:, None, :]
    pick_all = chosen.astype(bf16).reshape(half, 2 * slots, tok_dev)
    gates_all = jnp.sum(jnp.where(chosen, gate_of[:, None, :], 0.0), axis=2).reshape(
        half, 2 * slots, 1
    )

    def take(s, rows, weights=None):
        picked = matmul(pick_all[s], rows)
        if weights is not None:
            picked = picked * weights
        return picked.astype(bf16)

    q_att, g1 = tie(q_att, g1)
    g2 = onward(g1)
    attn_heads, attended, log_total = attend(reach, q_att, k_att, v_att, scale)
    attn_heads, g2 = tie(attn_heads, g2)
    attn_own = lax.all_to_all(attn_heads, "expert", split_axis=0, concat_axis=1, tiled=True)
    w0, w1, w2 = (take(s, g, gates_all[s]) for s, g in enumerate((g0, g1, g2)))
    far0, far1, far2 = (dot_last(g, sd).astype(bf16) for g in (g0, g1, g2))
    attn_own, w0, w1, w2, far0, far1, far2, g2 = tie(
        attn_own, w0, w1, w2, far0, far1, far2, g2
    )
    g3 = onward(g2)
    tokens_f = tokens.astype(f32)
    resid = tokens_f + matmul(attn_own, wo)
    second_normed, second_norm_back = jax.vjp(norm_rows, resid, f_gain)
    b0, g3 = tie(second_normed.astype(bf16), g3)

    b1 = onward(b0)
    def shared(h2, grad_s_act):
        s_act, s_gating_back = jax.vjp(gating, matmul(h2, sg), matmul(h2, su))
        s_act = s_act.astype(bf16)
        gate_part, up_part = s_gating_back(grad_s_act.astype(f32))
        gate_part = gate_part.astype(bf16)
        up_part = up_part.astype(bf16)
        near = dot_last(gate_part, sg) + dot_last(up_part, su)
        return near, s_act, gate_part, up_part

    def expert(e_rows, e_grad):
        activated, e_gating_back = jax.vjp(
            gating, matmul(e_rows, expert_gate[0]), matmul(e_rows, expert_up[0])
        )
        activated = activated.astype(bf16)
        grad_e_act = dot_last(e_grad, expert_down[0]).astype(bf16)
        gate_part, up_part = e_gating_back(grad_e_act.astype(f32))
        gate_part = gate_part.astype(bf16)
        up_part = up_part.astype(bf16)
        grad_rows = (
            dot_last(gate_part, expert_gate[0]) + dot_last(up_part, expert_up[0])
        ).astype(bf16)
        return grad_rows, activated, gate_part, up_part

    def join(mine, arrived):
        return jnp.concatenate([mine[:slots], arrived], axis=0)

    def spread_back(s, near, mine, arrived, *more):
        total = near + dot_first(pick_all[s], join(mine, arrived))
        for other in more:
            total = total + other.astype(f32)
        return total

    e0 = take(0, b0)
    e0_in = across(e0[slots:])
    w0_in, w1_in = (across(w[slots:]) for w in (w0, w1))
    n0_near, *s0 = shared(b0, far0)
    n0_near, b1, e0_in, w0_in, w1_in = tie(n0_near, b1, e0_in, w0_in, w1_in)
    b2 = onward(b1)
    w2_in = across(w2[slots:])
    e1 = take(1, b1)
    e1_in = across(e1[slots:])
    r0, w0 = join(e0, e0_in), join(w0, w0_in)
    n0, *k0 = expert(r0, w0)
    n0, b1, e1_in, w2_in = tie(n0, b1, e1_in, w2_in)
    n0_in = across(n0[slots:])
    n1_near, *s1 = shared(b1, far1)
    n1_near, b2, e1_in, n0_in, w2_in = tie(n1_near, b2, e1_in, n0_in, w2_in)
    w3 = take(3, g3, gates_all[3])
    w3_in = across(w3[slots:])
    b3 = onward(b2)
    e2 = take(2, b2)
    e2_in = across(e2[slots:])
    r1, w1 = join(e1, e1_in), join(w1, w1_in)
    n1, *k1 = expert(r1, w1)
    n1, b2, e2_in, w3_in = tie(n1, b2, e2_in, w3_in)
    n1_in = across(n1[slots:])
    n2_near, *s2 = shared(b2, far2)
    n2_near, b3, e2_in, n1_in, w3_in = tie(n2_near, b3, e2_in, n1_in, w3_in)
    ring1 = onward(spread_back(1, n1_near, n1, n1_in).astype(bf16))
    e3 = take(3, b3)
    e3_in = across(e3[slots:])
    r2, w2 = join(e2, e2_in), join(w2, w2_in)
    n2, *k2 = expert(r2, w2)
    n2, b3, e3_in = tie(n2, b3, e3_in)
    n2_in = across(n2[slots:])
    n3_near, *s3 = shared(b3, dot_last(g3, sd).astype(bf16))
    n3_near, e3_in, n2_in, ring1 = tie(n3_near, e3_in, n2_in, ring1)
    ring2 = onward(spread_back(2, n2_near, n2, n2_in, ring1).astype(bf16))
    r3, w3 = join(e3, e3_in), join(w3, w3_in)
    n3, *k3 = expert(r3, w3)
    n3, ring2 = tie(n3, ring2)
    n3_in = across(n3[slots:])
    s_act, s_gate_part, s_up_part = (
        jnp.concatenate(pieces, axis=0) for pieces in zip(s0, s1, s2, s3)
    )
    b_all = jnp.concatenate([b0, b1, b2, b3], axis=0)
    g_all = jnp.concatenate([g0, g1, g2, g3], axis=0)
    grad_s_cols = dot_first(b_all, jnp.concatenate([s_gate_part, s_up_part], axis=1)).astype(bf16)
    grad_s_cols, n3_in = tie(grad_s_cols, n3_in)
    ring3 = onward(spread_back(3, n3_near, n3, n3_in, ring2).astype(bf16))
    e_rows = jnp.concatenate([r0, r1, r2, r3], axis=0)
    e_grad = jnp.concatenate([w0, w1, w2, w3], axis=0)
    activated, gate_part, up_part = (
        jnp.concatenate(pieces, axis=0) for pieces in zip(k0, k1, k2, k3)
    )
    grad_e_gate = dot_first(e_rows, gate_part).astype(bf16)
    grad_e_up = dot_first(e_rows, up_part).astype(bf16)
    e_result = matmul(activated, expert_down[0]).astype(bf16).reshape(half, 2 * slots, width)
    grad_s_down = dot_first(s_act, g_all).astype(bf16)
    grad_e_gate, grad_e_up, ring3, activated, s_act, e_result, grad_s_down = tie(
        grad_e_gate, grad_e_up, ring3, activated, s_act, e_result, grad_s_down
    )
    grad_second = spread_back(0, n0_near, n0, n0_in, ring3)
    o_in = across(e_result[:, slots:])
    grad_e_down = dot_first(activated, e_grad).astype(bf16)

    def out_term(s, *more):
        weighed = (join(e_result[s], o_in[s]).astype(f32) * gates_all[s]).astype(bf16)
        total = matmul(s_act[s * tok_dev : (s + 1) * tok_dev], sd) + dot_first(
            pick_all[s], weighed
        )
        for other in more:
            total = total + other.astype(f32)
        return total

    grad_e_gate = lax.psum_scatter(grad_e_gate, "dp", scatter_dimension=0, tiled=True)
    grad_e_up = lax.psum_scatter(grad_e_up, "dp", scatter_dimension=0, tiled=True)
    grad_e_down_all, grad_s_down = grad_e_down, grad_s_down[:ff_own]

    def sum_columns(grads):
        return lax.psum_scatter(grads, "dp", scatter_dimension=0, tiled=True)

    grad_s_cols = sum_columns(grad_s_cols)

    def ff_restore(cut):
        both = cut[:, :, :ff_own].astype(f32).reshape(half, 2, rows_w, spread, 2 * ff_cut)
        return (both[:, 0] + both[:, 1]).transpose(1, 2, 0, 3).reshape(rows_w, -1)

    grad_f = grad_out.astype(f32)
    grad_resid_norm, grad_f_gain = second_norm_back(grad_second)
    grad_resid = grad_f + grad_resid_norm
    grad_attn_out = grad_resid.astype(bf16)
    grad_w_out = dot_first(attn_own, grad_attn_out).astype(bf16)
    grad_attended = dot_last(grad_attn_out, wo).astype(bf16)
    grad_heads = lax.all_to_all(grad_attended, "expert", split_axis=1, concat_axis=0, tiled=True)
    grad_heads, grad_w_out, grad_s_cols, grad_e_down, grad_s_down, grad_e_gate = tie(
        grad_heads,
        grad_w_out,
        grad_s_cols,
        grad_e_down_all,
        grad_s_down,
        grad_e_gate,
    )
    s_keep, s_other = line_swap(
        grad_s_down.reshape((2,) * (spread.bit_length() - 1) + (2, ff_cut, width)), 0
    )
    grad_s_cut = lax.all_to_all(
        grad_s_cols.reshape(group, rows_w, -1), "expert", split_axis=0, concat_axis=0, tiled=True
    )
    grad_w_out = lax.psum_scatter(grad_w_out, "dp", scatter_dimension=0, tiled=True)
    grad_q_lin, grad_kv, lat_part = attend_back(
        reach, q_att, k_att, v_att, grad_heads, attended, log_total, we, tables, scale
    )
    lat_part, grad_q_lin, o_in, grad_e_down, s_other = tie(
        lat_part, grad_q_lin, o_in, grad_e_down, s_other
    )
    ring1 = onward(out_term(1).astype(bf16))
    grad_s_down = both_halves(s_keep, s_other)
    for m in range(1, spread.bit_length() - 1):
        s_keep, s_other = line_swap(grad_s_down, m)
        if m < spread.bit_length() - 2:
            grad_s_down = both_halves(s_keep, s_other)
    (grad_lat_sum,) = reduce_rows([lat_part.reshape(group, tok_dev, -1)], 5, 2)
    grad_lat_sum, grad_q_lin, ring1, s_other, grad_w_out, grad_e_down = tie(
        grad_lat_sum, grad_q_lin, ring1, s_other, grad_w_out, grad_e_down
    )
    grad_s_down = both_halves(s_keep, s_other)
    own_side = rank % 2
    s_keep = lax.dynamic_index_in_dim(grad_s_down, own_side, 0, False)
    s_other = across(lax.dynamic_index_in_dim(grad_s_down, 1 - own_side, 0, False))
    ring2 = onward(out_term(2, ring1).astype(bf16))
    first_part = dot_last(grad_q_lin, wq).astype(bf16).reshape(group, tok_dev, width)
    steps = list(range(1, half)) + [0]
    w_blocks = grad_w_out.reshape(group, rows_w, width)
    w_in = across(jnp.stack([behind(w_blocks, s, 1) for s in steps]))

    def ring_term(blocks, arrived, k, *more):
        total = behind(blocks, steps[k], 0).astype(f32) + arrived[k].astype(f32)
        for other in more:
            total = total + other.astype(f32)
        return total

    def latent_parts(latent_in, gain_vec):
        return (
            norm_rows(latent_in[:, :KV], gain_vec),
            rotate(latent_in[:, KV : KV + ROPE], own_cos, own_sin),
        )

    unused, latent_back = jax.vjp(latent_parts, own(latent), l_gain)
    grad_latent, grad_l_gain = latent_back(
        (grad_lat_sum[:, :KV], grad_lat_sum[:, KV : KV + ROPE])
    )
    grad_latent = grad_latent.astype(bf16)
    grad_w_lat = dot_first(own(h1), grad_latent)[:, : KV + ROPE]
    grad_gains = jnp.stack(
        [
            grad_f_gain,
            jnp.pad(grad_l_gain.reshape(-1, rows_l), ((0, 0), (0, rows_w - rows_l))).reshape(width),
        ],
        axis=1,
    )
    lat_grads_in = jnp.concatenate(
        [grad_w_lat, jnp.pad(grad_gains, ((0, 0), (0, ROPE - 2)))], axis=1
    ).astype(bf16)
    first_part, lat_grads, w_in, grad_q_lin = tie(first_part, lat_grads_in, w_in, grad_q_lin)
    lat_grads = lax.psum_scatter(lat_grads, "dp", scatter_dimension=0, tiled=True)
    w_ring = onward(ring_term(w_blocks, w_in, 0).astype(bf16))
    grad_a_cols = jnp.concatenate(
        [dot_first(h1, grad_q_lin), dot_first(ckv, grad_kv).reshape(width, e_fold)], axis=1
    ).astype(bf16)
    first_part, grad_a_cols, w_ring, ring2 = tie(first_part, grad_a_cols, w_ring, ring2)
    ring3 = onward(out_term(3, ring2).astype(bf16))
    grad_a_cols = lax.psum_scatter(grad_a_cols, "dp", scatter_dimension=0, tiled=True)
    w_ring = onward(ring_term(w_blocks, w_in, 1, w_ring).astype(bf16))
    grad_e_down = lax.psum_scatter(grad_e_down, "dp", scatter_dimension=1, tiled=True)
    (first_sum,) = reduce_rows([first_part], 6, 4)
    (
        first_sum,
        lat_grads,
        ring3,
        w_ring,
        s_keep,
        s_other,
        grad_a_cols,
        grad_s_cut,
        grad_e_gate,
        grad_e_up,
    ) = tie(
        first_sum,
        lat_grads,
        ring3,
        w_ring,
        s_keep,
        s_other,
        grad_a_cols,
        grad_s_cut,
        grad_e_gate,
        grad_e_up,
    )
    w_ring = onward(ring_term(w_blocks, w_in, 2, w_ring).astype(bf16))
    lat_blocks = lat_grads.reshape(group, rows_w, -1)
    lat_in = across(jnp.stack([behind(lat_blocks, s, 1) for s in steps]))
    grad_first = first_sum + dot_last(grad_latent[:, :lat_w], wl)
    unused, first_norm_back = jax.vjp(lambda v: norm_rows(v, a_gain), tokens_f)
    (grad_tokens_norm,) = first_norm_back(grad_first)
    grad_tokens = grad_resid + grad_tokens_norm
    grad_tokens, lat_in, w_ring = tie(grad_tokens, lat_in, w_ring)
    grad_w_out = ring_term(w_blocks, w_in, 3, w_ring)
    lat_ring = onward(ring_term(lat_blocks, lat_in, 0).astype(bf16))
    block_out = (resid + out_term(0, ring3)).astype(bf16)
    block_out, lat_ring = tie(block_out, lat_ring)
    lat_ring = onward(ring_term(lat_blocks, lat_in, 1, lat_ring).astype(bf16))
    grad_s_gate = ff_restore(grad_s_cut[:, :, :ff_pad])
    grad_s_up = ff_restore(grad_s_cut[:, :, ff_pad:])
    grad_s_gate, grad_s_up, lat_ring = tie(grad_s_gate, grad_s_up, lat_ring)
    lat_ring = onward(ring_term(lat_blocks, lat_in, 2, lat_ring).astype(bf16))
    lat_grads = ring_term(lat_blocks, lat_in, 3, lat_ring)
    grad_s_down = s_keep.astype(f32) + s_other.astype(f32)
    grad_w_lat = lat_grads[:, :lat_w]
    grad_f_gain = lat_grads[:, lat_w]
    grad_l_gain = lat_grads[:rows_l, lat_w + 1]
    grad_a_cols = lax.all_to_all(
        grad_a_cols.reshape(group, rows_w, -1), "expert", split_axis=0, concat_axis=0, tiled=True
    )
    grad_w_q = (
        grad_a_cols[:, :, :q_own]
        .reshape(group, rows_w, mine, KEY)[..., : NOPE + ROPE]
        .transpose(1, 0, 2, 3)
        .reshape(rows_w, -1)
        .astype(f32)
    )
    grad_w_exp = (
        grad_a_cols[:, :, q_own:]
        .reshape(group, rows_l, e_own)
        .transpose(1, 0, 2)
        .reshape(rows_l, -1)
        .astype(f32)
    )
    grad_a_gain = (
        jnp.sum(grad_w_q * w_query.astype(f32), axis=1)
        + jnp.sum(grad_w_lat * w_latent.astype(f32), axis=1)
    ) / attn_gain.astype(f32)

    return (
        block_out,
        grad_tokens,
        grad_a_gain,
        grad_w_q,
        grad_w_lat,
        grad_l_gain,
        grad_w_exp,
        grad_w_out,
        grad_f_gain,
        grad_s_gate,
        grad_s_up,
        grad_s_down,
        grad_e_gate.astype(f32)[None],
        grad_e_up.astype(f32)[None],
        grad_e_down.astype(f32)[None],
    )


def solution(mesh):
    placed = (
        P(EVERY, None),
        P(EVERY, None),
        P(EVERY, None),
        P(EVERY, None),
        P("dp", None),
        P(EVERY),
        P(EVERY, None),
        P(EVERY, None),
        P(EVERY),
        P(EVERY, None),
        P(EVERY, None),
        P(EVERY),
        P(EVERY, None),
        P(EVERY, None),
        P(EVERY, None),
        P("expert", None, None),
        P("expert", None, None),
        P("expert", None, None),
    )
    return jax.shard_map(
        per_device,
        mesh=mesh,
        in_specs=placed,
        out_specs=(
            P(EVERY, None),
            P(EVERY, None),
            P(EVERY),
            P(EVERY, None),
            P(EVERY, None),
            P(EVERY),
            P(EVERY, None),
            P(EVERY, None),
            P(EVERY),
            P(EVERY, None),
            P(EVERY, None),
            P(EVERY, None),
            P("expert", "dp", None),
            P("expert", "dp", None),
            P("expert", None, "dp"),
        ),
        check_vma=False,
    )
```

```python
import functools

import jax
import jax.numpy as jnp
from jax import lax
from jax.experimental import pallas as pl
from jax.experimental.pallas import tpu as pltpu
from jax.sharding import PartitionSpec as P

HEADS = 16
NOPE = 128
ROPE = 64
KV = 512
VD = 128
SEG = 256
KEY = 256

epsilon = 1e-06
bf16 = jnp.bfloat16
f32 = jnp.float32
EVERY = ("dp", "expert")
MESH = pl.DeviceIdType.MESH
VMEM_LIMIT = 60 << 20
WIRE = pl.CostEstimate(flops=0, bytes_accessed=300_000_000, transcendentals=0)


def norm_rows(values, gain_vec):
    return (
        values * lax.rsqrt(jnp.mean(values * values, axis=-1, keepdims=True) + epsilon) * gain_vec
    )


def rotate(values, cos_table, sin_table):
    half_width = values.shape[-1] // 2
    first_half = values[..., :half_width]
    second_half = values[..., half_width:]
    return jnp.concatenate(
        [
            first_half * cos_table - second_half * sin_table,
            second_half * cos_table + first_half * sin_table,
        ],
        axis=-1,
    )


def gating(gate_part, up_part):
    return jax.nn.silu(gate_part) * up_part


def ancestry(parent_row, seg_count):
    identity = jnp.eye(seg_count, dtype=f32)
    parent_hot = (parent_row[:, None] == jnp.arange(seg_count, dtype=jnp.int32)[None, :]).astype(
        f32
    )
    reachable = identity
    for _ in range(seg_count - 1):
        reachable = jnp.maximum(identity, jnp.dot(parent_hot, reachable))
    return reachable


def matmul(left, right):
    return jnp.dot(left, right, preferred_element_type=f32)


def dot_last(left, right):
    return lax.dot_general(left, right, (((1,), (1,)), ((), ())), preferred_element_type=f32)


def dot_first(left, right):
    return lax.dot_general(left, right, (((0,), (0,)), ((), ())), preferred_element_type=f32)


def greet(rank, last):
    barrier = pltpu.get_barrier_semaphore()
    a = rank // 2

    def hail(other):
        pl.semaphore_signal(barrier, inc=1, device_id={"expert": other}, device_id_type=MESH)

    hail(rank + 1 - 2 * (rank % 2))

    @pl.when(a < last)
    def _():
        hail(rank + 2)

    @pl.when(a > 0)
    def _():
        hail(rank - 2)

    pl.semaphore_wait(barrier, 1 + (a + last - 1) // last + (2 * last - 1 - a) // last)


class Chain:
    def __init__(self, chunks, x_ref, o_ref, sx, rx, su, ru, sd, rd):
        self.chunks, self.x, self.o = chunks, x_ref, o_ref
        self.sems = (sx, rx, su, ru, sd, rd)
        self.rank = lax.axis_index("expert")
        self.last = o_ref.shape[0] // 2 - 1
        self.a = self.rank // 2
        self.side = self.rank + 1 - 2 * (self.rank % 2)
        self.rows = x_ref.shape[0] // chunks

    def piece(self, ref, c):
        return ref.at[pl.ds(c * self.rows, self.rows)]

    def to(self, src, block, c, send, recv, target):
        return pltpu.make_async_remote_copy(
            src_ref=src,
            dst_ref=self.piece(self.o.at[block], c),
            send_sem=send,
            recv_sem=recv,
            device_id={"expert": target},
            device_id_type=MESH,
        )

    def start(self):
        sx, rx, su, ru, sd, rd = self.sems
        rank, a, last, to = self.rank, self.a, self.last, self.to
        for c in range(self.chunks):
            own = self.piece(self.x, c)
            to(own, rank, c, sx.at[0, c], rx.at[0, c], self.side).start()

            @pl.when(a < last)
            def _():
                to(own, rank, c, su.at[0, c], ru.at[0, c], rank + 2).start()

            @pl.when(a > 0)
            def _():
                to(own, rank, c, sd.at[0, c], rd.at[0, c], rank - 2).start()

    def step(self, s):
        sx, rx, su, ru, sd, rd = self.sems
        rank, a, last, to = self.rank, self.a, self.last, self.to
        for c in range(self.chunks):

            @pl.when(a >= s)
            def _():
                block = rank - 2 * s
                src = self.piece(self.o.at[block], c)
                to(src, block, c, su.at[s - 1, c], ru.at[s - 1, c], rank + 2).wait_recv()
                to(src, block, c, sx.at[s, c], rx.at[s, c], self.side).start()

                @pl.when(a < last)
                def _():
                    to(src, block, c, su.at[s, c], ru.at[s, c], rank + 2).start()

            @pl.when(a + s <= last)
            def _():
                block = rank + 2 * s
                src = self.piece(self.o.at[block], c)
                to(src, block, c, sd.at[s - 1, c], rd.at[s - 1, c], rank - 2).wait_recv()
                to(src, block, c, sx.at[last + s, c], rx.at[last + s, c], self.side).start()

                @pl.when(a > 0)
                def _():
                    to(src, block, c, sd.at[s, c], rd.at[s, c], rank - 2).start()

    def finish(self):
        sx, rx, su, ru, sd, rd = self.sems
        rank, a, last, to, side = self.rank, self.a, self.last, self.to, self.side
        for c in range(self.chunks):
            own = self.piece(self.x, c)
            to(own, side, c, sx.at[0, c], rx.at[0, c], side).wait()

            @pl.when(a < last)
            def _():
                to(own, rank, c, su.at[0, c], ru.at[0, c], rank + 2).wait_send()

            @pl.when(a > 0)
            def _():
                to(own, rank, c, sd.at[0, c], rd.at[0, c], rank - 2).wait_send()

        for s in range(1, last + 1):
            for c in range(self.chunks):

                @pl.when(a >= s)
                def _():
                    block = rank - 2 * s
                    src = self.piece(self.o.at[block], c)
                    to(src, side - 2 * s, c, sx.at[s, c], rx.at[s, c], side).wait()

                    @pl.when(a < last)
                    def _():
                        to(src, block, c, su.at[s, c], ru.at[s, c], rank + 2).wait_send()

                @pl.when(a + s <= last)
                def _():
                    block = rank + 2 * s
                    src = self.piece(self.o.at[block], c)
                    to(src, side + 2 * s, c, sx.at[last + s, c], rx.at[last + s, c], side).wait()

                    @pl.when(a > 0)
                    def _():
                        to(src, block, c, sd.at[s, c], rd.at[s, c], rank - 2).wait_send()


def chain_sems(count, chunks):
    half = count // 2
    dma = pltpu.SemaphoreType.DMA
    return [dma((2 * half, chunks))] * 2 + [dma((half, chunks))] * 4


class Share:
    def __init__(self, ref, send_out, recv_out, send_pass, recv_pass):
        self.ref = ref
        self.sems = (send_out, recv_out, send_pass, recv_pass)
        self.line = lax.axis_index("dp")
        self.count = ref.shape[0] // 2

    def out(self, k):
        peer = 2 * lax.rem(self.line // 2 + k, self.count) + self.line % 2
        return pltpu.make_async_remote_copy(
            src_ref=self.ref.at[self.line],
            dst_ref=self.ref.at[self.line],
            send_sem=self.sems[0].at[k],
            recv_sem=self.sems[1].at[k],
            device_id={"dp": peer},
            device_id_type=MESH,
        )

    def hand(self, k):
        slab = 2 * lax.rem(self.line // 2 + self.count - k, self.count) + self.line % 2
        return pltpu.make_async_remote_copy(
            src_ref=self.ref.at[slab],
            dst_ref=self.ref.at[slab],
            send_sem=self.sems[2].at[k],
            recv_sem=self.sems[3].at[k],
            device_id={"dp": self.line + 1 - 2 * (self.line % 2)},
            device_id_type=MESH,
        )

    def start(self):
        for k in range(1, self.count):
            self.out(k).start()
        self.hand(0).start()

    def middle(self):
        for k in range(1, self.count):
            self.out(k).wait_recv()
            self.hand(k).start()

    def finish(self):
        for k in range(1, self.count):
            self.out(k).wait_send()
        for k in range(self.count):
            self.hand(k).wait()


def prologue_kernel(
    chunks,
    x_ref,
    w_ref,
    d_ref,
    t_ref,
    o_ref,
    pk_ref,
    do_ref,
    to_ref,
    wa_s,
    wa_r,
    ta_s,
    ta_r,
    da_s,
    da_r,
    *sems,
):
    group, spread = o_ref.shape[0], pk_ref.shape[0]
    packs, downs = Share(pk_ref, *sems[:4]), Share(do_ref, *sems[4:8])
    chain = Chain(chunks, x_ref, o_ref, *sems[8:])
    rank, line = chain.rank, packs.line
    mine = rank % 2
    barrier = pltpu.get_barrier_semaphore()
    for k in range(1, group):
        pl.semaphore_signal(
            barrier,
            inc=1,
            device_id={"expert": lax.rem(rank + k, group)},
            device_id_type=MESH,
        )
    for k in range(1, packs.count):
        peer = 2 * lax.rem(line // 2 + k, packs.count) + line % 2
        pl.semaphore_signal(barrier, inc=1, device_id={"dp": peer}, device_id_type=MESH)
    pl.semaphore_signal(
        barrier, inc=1, device_id={"dp": line + 1 - 2 * (line % 2)}, device_id_type=MESH
    )
    pl.semaphore_wait(barrier, group - 1 + packs.count)

    def far(src, dst, send, recv, peer):
        return pltpu.make_async_remote_copy(
            src_ref=src,
            dst_ref=dst,
            send_sem=send,
            recv_sem=recv,
            device_id={"expert": peer},
            device_id_type=MESH,
        )

    def cut(k):
        peer = lax.rem(rank + k, group)
        return far(w_ref.at[peer], pk_ref.at[line, rank], wa_s.at[k - 1], wa_r.at[k - 1], peer)

    def gates(k):
        peer = lax.rem(rank + k, group)
        return far(t_ref, to_ref.at[rank], ta_s.at[k - 1], ta_r.at[k - 1], peer)

    def down():
        return far(d_ref, do_ref.at[line, mine], da_s.at[0], da_r.at[0], chain.side)

    down().start()
    for k in range(1, group):
        cut(k).start()
        gates(k).start()
    chain.start()
    pk_ref[line, rank] = w_ref[rank]
    do_ref[line, mine] = d_ref[...]
    to_ref[rank] = t_ref[...]
    o_ref[rank] = x_ref[...]
    down().wait_recv()
    downs.start()
    for k in range(1, group):
        cut(k).wait_recv()
    packs.start()
    for s in range(1, chain.last):
        chain.step(s)
    downs.middle()
    packs.middle()
    chain.step(chain.last)
    chain.finish()
    down().wait_send()
    for k in range(1, group):
        cut(k).wait_send()
        gates(k).wait()
    downs.finish()
    packs.finish()


def prologue(x, cuts, down, gates, spread, call_id, chunks=2):
    group = cuts.shape[0]
    dma = pltpu.SemaphoreType.DMA
    vmem = pl.BlockSpec(memory_space=pltpu.VMEM)
    return pl.pallas_call(
        functools.partial(prologue_kernel, chunks),
        out_shape=[
            jax.ShapeDtypeStruct((group,) + x.shape, x.dtype),
            jax.ShapeDtypeStruct((spread,) + cuts.shape, cuts.dtype),
            jax.ShapeDtypeStruct((spread, 2) + down.shape, down.dtype),
            jax.ShapeDtypeStruct((group,) + gates.shape, gates.dtype),
        ],
        in_specs=[vmem] * 4,
        out_specs=[vmem] * 4,
        scratch_shapes=[dma((group - 1,))] * 4
        + [dma((1,))] * 2
        + [dma((spread // 2,))] * 8
        + chain_sems(group, chunks),
        compiler_params=pltpu.CompilerParams(
            collective_id=call_id, has_side_effects=True, vmem_limit_bytes=VMEM_LIMIT
        ),
        cost_estimate=WIRE,
        name="prologue",
    )(x, cuts, down, gates)


def ring_pairs(group):
    half = group // 2
    side = [(r, r + 1 - 2 * (r % 2)) for r in range(group)]
    onward = [(2 * a + b, 2 * ((a + 1) % half) + b) for a in range(half) for b in range(2)]
    return side, onward


def tie(*values):
    return lax.optimization_barrier(values)


def reduce_kernel(parts, *refs):
    n = len(parts)
    p_refs, o_refs = refs[:n], refs[n : 2 * n]
    bufs = [refs[2 * n + 4 * k : 2 * n + 4 * k + 4] for k in range(n)]
    acc, sxs, rxs, sus, rus, sds, rds = refs[6 * n :]
    rank = lax.axis_index("expert")
    last = p_refs[0].shape[0] // 2 - 1
    a = rank // 2
    b = rank % 2
    greet(rank, last)
    h = a // 2
    order = [3 - 3 * h, 2 - h, 4 * h + 1 - a, a]
    pieces = []
    for k, chunks in enumerate(parts):
        rows = p_refs[k].shape[1] // chunks
        pieces += [(k, c * rows, rows) for c in range(chunks)]

    def copy(src, dst, send, recv, target):
        return pltpu.make_async_remote_copy(
            src_ref=src,
            dst_ref=dst,
            send_sem=send,
            recv_sem=recv,
            device_id={"expert": target},
            device_id_type=MESH,
        )

    for t in order:
        for c, (k, at, rows) in enumerate(pieces):
            src = p_refs[k].at[2 * t + 1 - b, pl.ds(at, rows)]
            dst = bufs[k][0].at[t, pl.ds(at, rows)]
            copy(src, dst, sxs.at[t, c], rxs.at[t, c], rank + 1 - 2 * b).start()

    def moves(t, c, k, at, rows):
        cut = pl.ds(at, rows)
        rx, st, ru, rd = (buf.at[t, cut] for buf in bufs[k])
        src = p_refs[k].at[2 * t + 1 - b, cut]
        across = copy(src, rx, sxs.at[t, c], rxs.at[t, c], rank + 1 - 2 * b)
        upward = copy(st, ru, sus.at[t, c], rus.at[t, c], rank + 2)
        downward = copy(st, rd, sds.at[t, c], rds.at[t, c], rank - 2)
        return rx, st, ru, rd, across, upward, downward

    for t in order:
        for c, (k, at, rows) in enumerate(pieces):
            rx, st, ru, rd, across, upward, downward = moves(t, c, k, at, rows)
            width = p_refs[k].shape[2]
            total = acc.at[pl.ds(0, rows), pl.ds(0, width)]
            across.wait_recv()
            total[...] = p_refs[k][2 * t + b, pl.ds(at, rows)].astype(f32) + rx[...].astype(f32)

            @pl.when((t >= a) & (a > 0))
            def _():
                upward.wait_recv()
                total[...] += ru[...].astype(f32)

            @pl.when((t <= a) & (a < last))
            def _():
                downward.wait_recv()
                total[...] += rd[...].astype(f32)

            @pl.when(t == a)
            def _():
                o_refs[k][pl.ds(at, rows)] = total[...]

            @pl.when(t > a)
            def _():
                st[...] = total[...].astype(bf16)
                upward.start()

            @pl.when(t < a)
            def _():
                st[...] = total[...].astype(bf16)
                downward.start()

    for t in order:
        for c, (k, at, rows) in enumerate(pieces):
            rx, st, ru, rd, across, upward, downward = moves(t, c, k, at, rows)
            across.wait_send()

            @pl.when(t > a)
            def _():
                upward.wait_send()

            @pl.when(t < a)
            def _():
                downward.wait_send()


def reduce_rows(operands, call_id, most):
    half = operands[0].shape[0] // 2
    parts = [
        max(c for c in range(1, most + 1) if p.shape[1] % (16 * c) == 0 and p.shape[1] // c >= 16)
        if p.shape[1] > 64
        else 1
        for p in operands
    ]
    high = max(p.shape[1] // c for p, c in zip(operands, parts))
    wide = max(p.shape[2] for p in operands)
    sem = pltpu.SemaphoreType.DMA((half, sum(parts)))
    vmem = pl.BlockSpec(memory_space=pltpu.VMEM)
    bufs = [
        pltpu.VMEM((half,) + p.shape[1:], p.dtype) for p in operands for _ in range(4)
    ]
    return pl.pallas_call(
        functools.partial(reduce_kernel, parts),
        out_shape=[jax.ShapeDtypeStruct(p.shape[1:], f32) for p in operands],
        in_specs=[vmem] * len(operands),
        out_specs=[vmem] * len(operands),
        scratch_shapes=bufs + [pltpu.VMEM((high, wide), f32)] + [sem] * 6,
        compiler_params=pltpu.CompilerParams(
            collective_id=call_id, has_side_effects=True, vmem_limit_bytes=VMEM_LIMIT
        ),
        cost_estimate=pl.CostEstimate(
            flops=0, bytes_accessed=36 * sum(p.size for p in operands) * 2, transcendentals=0
        ),
        name="reduce_rows",
    )(*operands)


def swap_halves(values):
    lane = lax.broadcasted_iota(jnp.int32, values.shape, 1)
    half = ROPE // 2
    return jnp.where(lane < half, pltpu.roll(values, KEY - NOPE - half, 1), pltpu.roll(values, half, 1))


def turns(seg_cos, seg_sin, off_cos, off_sin):
    lane = lax.broadcasted_iota(jnp.int32, off_cos.shape, 1)
    sine = seg_sin * off_cos + seg_cos * off_sin
    return seg_cos * off_cos - seg_sin * off_sin, jnp.where(lane < ROPE // 2, -sine, sine)


def project_kernel(
    heads,
    x_ref,
    wq_ref,
    wl_ref,
    we_ref,
    ag_ref,
    lg_ref,
    sc_ref,
    ss_ref,
    oc_ref,
    os_ref,
    h1_ref,
    q_ref,
    k_ref,
    v_ref,
    lat_ref,
    ckv_ref,
):
    i = pl.program_id(0)
    x = x_ref[...].astype(f32)
    power = jnp.mean(x * x, axis=-1, keepdims=True)
    h1 = (x * lax.rsqrt(power + epsilon) * ag_ref[...]).astype(bf16)
    h1_ref[...] = h1
    cosine, sine = turns(sc_ref[pl.ds(i, 1)], ss_ref[pl.ds(i, 1)], oc_ref[...], os_ref[...])

    def turn(values):
        return (values * cosine + swap_halves(values) * sine).astype(bf16)

    query = matmul(h1, wq_ref[...])
    for h in range(heads):
        at = h * KEY
        q_ref[:, at : at + NOPE] = query[:, at : at + NOPE].astype(bf16)
        q_ref[:, at + NOPE : at + KEY] = turn(query[:, at + NOPE : at + KEY])
    latent = matmul(h1, wl_ref[...])
    lat_ref[...] = latent
    low = latent[:, :KV]
    power = jnp.mean(low * low, axis=-1, keepdims=True)
    ckv = (low * lax.rsqrt(power + epsilon) * lg_ref[...]).astype(bf16)
    ckv_ref[...] = ckv
    krope = turn(latent[:, KV:])
    kv = matmul(ckv, we_ref[...]).astype(bf16)
    for h in range(heads):
        at = h * KEY
        k_ref[:, at : at + NOPE] = kv[:, at : at + NOPE]
        k_ref[:, at + NOPE : at + KEY] = krope
        v_ref[:, h * VD : (h + 1) * VD] = kv[:, at + NOPE : at + KEY]


def project(x, packed, lat_pack, we, a_gain, l_gain, tables, heads):
    tree, width = x.shape
    segs = tree // SEG
    lat_width = lat_pack.shape[1]
    fixed = lambda arr: pl.BlockSpec(arr.shape, lambda i: (0, 0))
    part = lambda cols: pl.BlockSpec((SEG, cols), lambda i: (i, 0))
    return pl.pallas_call(
        functools.partial(project_kernel, heads),
        grid=(segs,),
        in_specs=[
            part(width),
            pl.BlockSpec((width, heads * KEY), lambda i: (0, 0)),
            fixed(lat_pack),
            fixed(we),
            fixed(a_gain),
            fixed(l_gain),
        ]
        + [fixed(table) for table in tables],
        out_specs=[
            part(width),
            part(heads * KEY),
            part(heads * KEY),
            part(heads * VD),
            part(lat_width),
            part(KV),
        ],
        out_shape=[
            jax.ShapeDtypeStruct((tree, width), bf16),
            jax.ShapeDtypeStruct((tree, heads * KEY), bf16),
            jax.ShapeDtypeStruct((tree, heads * KEY), bf16),
            jax.ShapeDtypeStruct((tree, heads * VD), bf16),
            jax.ShapeDtypeStruct((tree, lat_width), f32),
            jax.ShapeDtypeStruct((tree, KV), bf16),
        ],
        compiler_params=pltpu.CompilerParams(vmem_limit_bytes=VMEM_LIMIT),
        cost_estimate=pl.CostEstimate(flops=0, bytes_accessed=60_000_000, transcendentals=0),
        name="project",
    )(x, packed, lat_pack, we, a_gain, l_gain, *tables)


def triangle():
    keys = lax.broadcasted_iota(jnp.int32, (SEG, SEG), 0)
    queries = lax.broadcasted_iota(jnp.int32, (SEG, SEG), 1)
    return keys <= queries


def attend_kernel(
    heads, segs, scale, reach_ref, q_ref, k_ref, v_ref, out_ref, full_ref, log_ref, m_s, l_s, acc_s
):
    i = pl.program_id(0)
    diag = triangle()

    def score(h, j):
        keys = k_ref[pl.ds(j * SEG, SEG), h * KEY : (h + 1) * KEY]
        return dot_last(keys, q_ref[:, h * KEY : (h + 1) * KEY]) * scale

    def weigh(h, j, weights):
        vals = v_ref[pl.ds(j * SEG, SEG), h * VD : (h + 1) * VD]
        return dot_first(vals, weights.astype(bf16))

    for h in range(heads):
        s = jnp.where(diag, score(h, i), -1e30)
        top = jnp.max(s, axis=0, keepdims=True)
        w = jnp.where(diag, jnp.exp(s - top), 0.0)
        m_s[h : h + 1] = top
        l_s[h : h + 1] = jnp.sum(w, axis=0, keepdims=True)
        acc_s[h] = weigh(h, i, w)

    def step(j, carry):
        @pl.when(reach_ref[i * segs + j] > 0)
        def _():
            for h in range(heads):
                s = score(h, j)
                old = m_s[h : h + 1]
                top = jnp.maximum(old, jnp.max(s, axis=0, keepdims=True))
                w = jnp.exp(s - top)
                fade = jnp.exp(old - top)
                m_s[h : h + 1] = top
                l_s[h : h + 1] = l_s[h : h + 1] * fade + jnp.sum(w, axis=0, keepdims=True)
                acc_s[h] = acc_s[h] * fade + weigh(h, j, w)

        return carry

    lax.fori_loop(0, i, step, 0)
    for h in range(heads):
        total = l_s[h : h + 1]
        rows = (acc_s[h] * (1.0 / total)).T
        full_ref[:, h * VD : (h + 1) * VD] = rows
        out_ref[:, h * VD : (h + 1) * VD] = rows.astype(bf16)
        log_ref[h : h + 1] = m_s[h : h + 1] + jnp.log(total)


def attend(reach, q, k, v, scale):
    tree = q.shape[0]
    segs = tree // SEG
    heads = q.shape[1] // KEY
    whole = lambda width: pl.BlockSpec((tree, width), lambda i, r: (0, 0))
    part = lambda width: pl.BlockSpec((SEG, width), lambda i, r: (i, 0))
    return pl.pallas_call(
        functools.partial(attend_kernel, heads, segs, scale),
        grid_spec=pltpu.PrefetchScalarGridSpec(
            num_scalar_prefetch=1,
            grid=(segs,),
            in_specs=[part(heads * KEY), whole(heads * KEY), whole(heads * VD)],
            out_specs=[
                part(heads * VD),
                part(heads * VD),
                pl.BlockSpec((heads, SEG), lambda i, r: (0, i)),
            ],
            scratch_shapes=[
                pltpu.VMEM((heads, SEG), f32),
                pltpu.VMEM((heads, SEG), f32),
                pltpu.VMEM((heads, VD, SEG), f32),
            ],
        ),
        out_shape=[
            jax.ShapeDtypeStruct((tree, heads * VD), bf16),
            jax.ShapeDtypeStruct((tree, heads * VD), f32),
            jax.ShapeDtypeStruct((heads, tree), f32),
        ],
        compiler_params=pltpu.CompilerParams(vmem_limit_bytes=VMEM_LIMIT),
        cost_estimate=pl.CostEstimate(flops=0, bytes_accessed=70_000_000, transcendentals=0),
        name="attend",
    )(reach, q, k, v)


def attend_back_kernel(
    heads,
    segs,
    scale,
    reach_ref,
    q_ref,
    k_ref,
    v_ref,
    g_ref,
    att_ref,
    log_ref,
    we_ref,
    sc_ref,
    ss_ref,
    oc_ref,
    os_ref,
    gq_ref,
    dkv_ref,
    lat_ref,
    dq_s,
    dk_s,
    dv_s,
    delta_s,
):
    j = pl.program_id(0)
    diag = triangle()

    @pl.when(j == 0)
    def _():
        def prepare(i, carry):
            rows = pl.ds(i * SEG, SEG)
            for h in range(heads):
                vcols = slice(h * VD, (h + 1) * VD)
                both = g_ref[rows, vcols].astype(f32) * att_ref[rows, vcols]
                delta_s[h : h + 1, rows] = jnp.sum(both.T, axis=0, keepdims=True)
            dq_s[rows] = jnp.zeros((SEG, heads * KEY), f32)
            return carry

        lax.fori_loop(0, segs, prepare, 0)

    dk_s[...] = jnp.zeros_like(dk_s)
    dv_s[...] = jnp.zeros_like(dv_s)

    def block(i, masked):
        rows = pl.ds(i * SEG, SEG)
        for h in range(heads):
            kcols = slice(h * KEY, (h + 1) * KEY)
            vcols = slice(h * VD, (h + 1) * VD)
            q = q_ref[rows, kcols]
            k = k_ref[:, kcols]
            g = g_ref[rows, vcols]
            s = dot_last(k, q) * scale
            w = jnp.exp(s - log_ref[h : h + 1, rows])
            if masked:
                w = jnp.where(diag, w, 0.0)
            dw = dot_last(v_ref[:, vcols], g)
            ds = (w * (dw - delta_s[h : h + 1, rows])).astype(bf16)
            dv_s[h] += matmul(w.astype(bf16), g)
            dk_s[h] += matmul(ds, q)
            dq_s[rows, kcols] += dot_first(ds, k)

    block(j, True)

    def step(i, carry):
        @pl.when(reach_ref[i * segs + j] > 0)
        def _():
            block(i, False)

        return carry

    lax.fori_loop(j + 1, segs, step, 0)
    rope = jnp.zeros((SEG, KEY - NOPE), f32)
    for h in range(heads):
        dkv_ref[:, h * KEY : h * KEY + NOPE] = (dk_s[h, :, :NOPE] * scale).astype(bf16)
        dkv_ref[:, h * KEY + NOPE : (h + 1) * KEY] = dv_s[h].astype(bf16)
        rope = rope + dk_s[h, :, NOPE:]
    lat_ref[:, :KV] = dot_last(dkv_ref[...], we_ref[...]).astype(bf16)
    lat_ref[:, KV:] = (rope * scale).astype(bf16)

    @pl.when(j == segs - 1)
    def _():
        def finish(i, carry):
            rows = pl.ds(i * SEG, SEG)
            cosine, sine = turns(
                sc_ref[pl.ds(i, 1)], ss_ref[pl.ds(i, 1)], oc_ref[...], os_ref[...]
            )
            for h in range(heads):
                at = h * KEY
                gq_ref[rows, at : at + NOPE] = (dq_s[rows, at : at + NOPE] * scale).astype(bf16)
                turned = dq_s[rows, at + NOPE : at + KEY] * scale
                gq_ref[rows, at + NOPE : at + KEY] = (
                    turned * cosine - swap_halves(turned) * sine
                ).astype(bf16)
            return carry

        lax.fori_loop(0, segs, finish, 0)


def attend_back(reach, q, k, v, g, attended, log_total, we, tables, scale):
    tree = q.shape[0]
    segs = tree // SEG
    heads = q.shape[1] // KEY
    whole = lambda width: pl.BlockSpec((tree, width), lambda j, r: (0, 0))
    part = lambda width: pl.BlockSpec((SEG, width), lambda j, r: (j, 0))
    fixed = lambda arr: pl.BlockSpec(arr.shape, lambda j, r: (0, 0))
    lat_width = KV + KEY - NOPE
    return pl.pallas_call(
        functools.partial(attend_back_kernel, heads, segs, scale),
        grid_spec=pltpu.PrefetchScalarGridSpec(
            num_scalar_prefetch=1,
            grid=(segs,),
            in_specs=[
                whole(heads * KEY),
                part(heads * KEY),
                part(heads * VD),
                whole(heads * VD),
                whole(heads * VD),
                fixed(log_total),
                fixed(we),
            ]
            + [fixed(table) for table in tables],
            out_specs=[whole(heads * KEY), part(heads * KEY), part(lat_width)],
            scratch_shapes=[
                pltpu.VMEM((tree, heads * KEY), f32),
                pltpu.VMEM((heads, SEG, KEY), f32),
                pltpu.VMEM((heads, SEG, VD), f32),
                pltpu.VMEM((heads, tree), f32),
            ],
        ),
        out_shape=[
            jax.ShapeDtypeStruct((tree, heads * KEY), bf16),
            jax.ShapeDtypeStruct((tree, heads * KEY), bf16),
            jax.ShapeDtypeStruct((tree, lat_width), bf16),
        ],
        compiler_params=pltpu.CompilerParams(vmem_limit_bytes=VMEM_LIMIT),
        cost_estimate=pl.CostEstimate(flops=0, bytes_accessed=90_000_000, transcendentals=0),
        name="attend_back",
    )(reach, q, k, v, g, attended, log_total, we, *tables)


def per_device(
    tokens,
    grad_out,
    routes,
    gate_values,
    parents,
    attn_gain,
    w_query,
    w_latent,
    latent_gain,
    w_expand,
    w_output,
    ffn_gain,
    shared_gate,
    shared_up,
    shared_down,
    expert_gate,
    expert_up,
    expert_down,
):
    group = lax.axis_size("expert")
    spread = lax.axis_size("dp")
    rank = lax.axis_index("expert")
    tok_dev, width = tokens.shape
    tree = tok_dev * group
    segs = parents.shape[1]
    per_token = routes.shape[1]
    capacity = tok_dev * per_token * 9 // (8 * group)
    slots = -(-capacity // 16) * 16
    scale = (NOPE + ROPE) ** (-0.5)
    mine = HEADS // group
    rows_w = w_query.shape[0]
    rows_l = w_expand.shape[0]
    ff_cut = shared_down.shape[0]
    half = group // 2
    ff_own = 2 * ff_cut * spread
    ff_pad = -(-ff_own // 128) * 128
    q_own = mine * KEY
    e_own = mine * (NOPE + VD)
    e_fold = rows_l * e_own // rows_w

    wq_cut = jnp.pad(
        w_query.reshape(rows_w, group, mine, NOPE + ROPE),
        ((0, 0), (0, 0), (0, 0), (0, KEY - NOPE - ROPE)),
    ).reshape(rows_w, group, q_own)

    def ff_columns(weight):
        cut = weight.reshape(rows_w, spread, half, 2 * ff_cut).transpose(2, 0, 1, 3)
        cut = jnp.pad(
            cut.reshape(half, 1, rows_w, ff_own),
            ((0, 0), (0, 0), (0, 0), (0, ff_pad - ff_own)),
        )
        return jnp.broadcast_to(cut, (half, 2, rows_w, ff_pad)).reshape(group, rows_w, ff_pad)

    we_cut = (
        w_expand.reshape(rows_l, group, e_own).transpose(1, 0, 2).reshape(group, rows_w, e_fold)
    )
    packed = jnp.concatenate(
        [
            wq_cut.transpose(1, 0, 2),
            we_cut,
            ff_columns(shared_gate),
            ff_columns(shared_up),
        ],
        axis=2,
    )
    expert_ids = jnp.arange(group, dtype=jnp.int32)
    gate_of = jnp.sum(
        jnp.where(routes[:, :, None] == expert_ids[None, None, :], gate_values[:, :, None], 0.0),
        axis=1,
    ).T
    x_all, packed, sd, gate_of = prologue(tokens, packed, shared_down, gate_of, spread, 0)
    x_all, parents, gate_of = lax.optimization_barrier(
        (x_all.reshape(tree, width), parents, gate_of)
    )
    packed = packed.reshape(width, -1)
    wq = packed[:, :q_own]
    we = packed[:, q_own : q_own + e_fold].reshape(KV, e_own)
    sg = packed[:, q_own + e_fold : q_own + e_fold + ff_pad]
    su = packed[:, q_own + e_fold + ff_pad :]
    sd = jnp.pad(sd.reshape(ff_own, width), ((0, ff_pad - ff_own), (0, 0)))

    lat_w = KV + ROPE
    gains = jnp.stack(
        [attn_gain, ffn_gain, jnp.pad(latent_gain, (0, rows_w - rows_l))], axis=1
    )
    gains = jnp.pad(gains, ((0, 0), (0, ROPE - 3)))
    lat_pack = lax.all_gather(
        jnp.concatenate([w_latent, gains], axis=1), EVERY, axis=0, tiled=True
    )
    wl = lat_pack[:, :lat_w]
    a_gain = lat_pack[:, lat_w].astype(f32)
    f_gain = lat_pack[:, lat_w + 1].astype(f32)
    l_gain = lat_pack[:, lat_w + 2].reshape(-1, rows_w)[:, :rows_l].reshape(KV).astype(f32)
    wo = lax.all_gather(w_output, EVERY, axis=0, tiled=True)
    reachable = ancestry(parents[0], segs)
    depth = jnp.sum(reachable, axis=1) - 1.0
    reach = reachable.astype(jnp.int32).reshape(segs * segs)
    half_width = ROPE // 2
    freq = 10000.0 ** (-2.0 * jnp.arange(half_width, dtype=f32) / ROPE)
    seg_angle = (depth * SEG)[:, None] * freq[None, :]
    off_angle = jnp.arange(SEG, dtype=f32)[:, None] * freq[None, :]

    def lanes(values):
        return jnp.pad(
            jnp.concatenate([values, values], axis=1), ((0, 0), (0, KEY - NOPE - ROPE))
        )

    tables = [
        lanes(jnp.cos(seg_angle)),
        lanes(jnp.sin(seg_angle)),
        lanes(jnp.cos(off_angle)),
        lanes(jnp.sin(off_angle)),
    ]
    seg_cos = lax.dynamic_slice_in_dim(tables[0], rank, 1, 0)[:, :half_width]
    seg_sin = lax.dynamic_slice_in_dim(tables[1], rank, 1, 0)[:, :half_width]
    off_cos = tables[2][:, :half_width]
    off_sin = tables[3][:, :half_width]
    own_cos = seg_cos * off_cos - seg_sin * off_sin
    own_sin = seg_sin * off_cos + seg_cos * off_sin

    def own(values):
        return lax.dynamic_slice_in_dim(values, rank * tok_dev, tok_dev, 0)

    side, ring = ring_pairs(group)

    def across(values):
        return lax.ppermute(values, "expert", side)

    def onward(values):
        return lax.ppermute(values, "expert", ring)

    x_all, g0 = tie(x_all, grad_out)
    g1 = onward(g0)
    h1, q_att, k_att, v_att, latent, ckv = project(
        x_all, packed, lat_pack, we, a_gain[None], l_gain[None], tables, mine
    )
    def behind(values, s, far):
        at = 2 * lax.rem(rank // 2 - s + half, half) + lax.rem(rank + far, 2)
        return lax.dynamic_index_in_dim(values, at, 0, keepdims=False)

    def line_swap(values, m):
        own_bit = lax.rem(lax.axis_index("dp") // (1 << m), 2)
        at = spread.bit_length() - 2 - m
        keep = lax.dynamic_index_in_dim(values, own_bit, at, False)
        send = lax.dynamic_index_in_dim(values, 1 - own_bit, at, False)
        swap = [(d, d ^ (1 << m)) for d in range(spread)]
        return keep, lax.ppermute(send, "dp", swap)

    def both_halves(keep, other):
        return (keep.astype(f32) + other.astype(f32)).astype(bf16)

    gate_of = jnp.concatenate(
        [
            lax.dynamic_slice(
                gate_of,
                (2 * lax.rem(rank // 2 - s + half, half) + rank % 2, rank + k - 2 * k * (rank % 2), 0),
                (1, 1, tok_dev),
            )[0]
            for s in range(half)
            for k in range(2)
        ],
        axis=0,
    )
    routed = gate_of > 0.0
    upto = (
        jnp.arange(tok_dev, dtype=jnp.int32)[:, None]
        <= jnp.arange(tok_dev, dtype=jnp.int32)[None, :]
    )
    place = matmul(routed.astype(bf16), upto.astype(bf16)).astype(jnp.int32) - 1
    chosen = (
        place[:, None, :] == jnp.arange(slots, dtype=jnp.int32)[None, :, None]
    ) & routed[:, None, :]
    pick_all = chosen.astype(bf16).reshape(half, 2 * slots, tok_dev)
    gates_all = jnp.sum(jnp.where(chosen, gate_of[:, None, :], 0.0), axis=2).reshape(
        half, 2 * slots, 1
    )

    def take(s, rows, weights=None):
        picked = matmul(pick_all[s], rows)
        if weights is not None:
            picked = picked * weights
        return picked.astype(bf16)

    q_att, g1 = tie(q_att, g1)
    g2 = onward(g1)
    attn_heads, attended, log_total = attend(reach, q_att, k_att, v_att, scale)
    attn_heads, g2 = tie(attn_heads, g2)
    attn_own = lax.all_to_all(attn_heads, "expert", split_axis=0, concat_axis=1, tiled=True)
    w0, w1, w2 = (take(s, g, gates_all[s]) for s, g in enumerate((g0, g1, g2)))
    far0, far1, far2 = (dot_last(g, sd).astype(bf16) for g in (g0, g1, g2))
    attn_own, w0, w1, w2, far0, far1, far2, g2 = tie(
        attn_own, w0, w1, w2, far0, far1, far2, g2
    )
    g3 = onward(g2)
    tokens_f = tokens.astype(f32)
    resid = tokens_f + matmul(attn_own, wo)
    second_normed, second_norm_back = jax.vjp(norm_rows, resid, f_gain)
    b0 = second_normed.astype(bf16)

    b1 = onward(b0)
    def shared(h2, grad_s_act):
        s_act, s_gating_back = jax.vjp(gating, matmul(h2, sg), matmul(h2, su))
        s_act = s_act.astype(bf16)
        gate_part, up_part = s_gating_back(grad_s_act.astype(f32))
        gate_part = gate_part.astype(bf16)
        up_part = up_part.astype(bf16)
        near = dot_last(gate_part, sg) + dot_last(up_part, su)
        return near, s_act, gate_part, up_part

    def expert(e_rows, e_grad):
        activated, e_gating_back = jax.vjp(
            gating, matmul(e_rows, expert_gate[0]), matmul(e_rows, expert_up[0])
        )
        activated = activated.astype(bf16)
        grad_e_act = dot_last(e_grad, expert_down[0]).astype(bf16)
        gate_part, up_part = e_gating_back(grad_e_act.astype(f32))
        gate_part = gate_part.astype(bf16)
        up_part = up_part.astype(bf16)
        grad_rows = (
            dot_last(gate_part, expert_gate[0]) + dot_last(up_part, expert_up[0])
        ).astype(bf16)
        return grad_rows, activated, gate_part, up_part

    def join(mine, arrived):
        return jnp.concatenate([mine[:slots], arrived], axis=0)

    def spread_back(s, near, mine, arrived, *more):
        total = near + dot_first(pick_all[s], join(mine, arrived))
        for other in more:
            total = total + other.astype(f32)
        return total

    e0 = take(0, b0)
    e0_in = across(e0[slots:])
    w0_in, w1_in = (across(w[slots:]) for w in (w0, w1))
    n0_near, *s0 = shared(b0, far0)
    n0_near, b1, e0_in, w0_in, w1_in = tie(n0_near, b1, e0_in, w0_in, w1_in)
    b2 = onward(b1)
    w2_in = across(w2[slots:])
    e1 = take(1, b1)
    e1_in = across(e1[slots:])
    r0, w0 = join(e0, e0_in), join(w0, w0_in)
    n0, *k0 = expert(r0, w0)
    n0, b1, e1_in, w2_in = tie(n0, b1, e1_in, w2_in)
    n0_in = across(n0[slots:])
    n1_near, *s1 = shared(b1, far1)
    n1_near, b2, e1_in, n0_in, w2_in, g3 = tie(n1_near, b2, e1_in, n0_in, w2_in, g3)
    w3 = take(3, g3, gates_all[3])
    w3_in = across(w3[slots:])
    b3 = onward(b2)
    e2 = take(2, b2)
    e2_in = across(e2[slots:])
    r1, w1 = join(e1, e1_in), join(w1, w1_in)
    n1, *k1 = expert(r1, w1)
    n1, b2, e2_in, w3_in = tie(n1, b2, e2_in, w3_in)
    n1_in = across(n1[slots:])
    n2_near, *s2 = shared(b2, far2)
    n2_near, b3, e2_in, n1_in, w3_in = tie(n2_near, b3, e2_in, n1_in, w3_in)
    ring1 = onward(spread_back(1, n1_near, n1, n1_in).astype(bf16))
    e3 = take(3, b3)
    e3_in = across(e3[slots:])
    r2, w2 = join(e2, e2_in), join(w2, w2_in)
    n2, *k2 = expert(r2, w2)
    n2, b3, e3_in = tie(n2, b3, e3_in)
    n2_in = across(n2[slots:])
    n3_near, *s3 = shared(b3, dot_last(g3, sd).astype(bf16))
    n3_near, e3_in, n2_in, ring1 = tie(n3_near, e3_in, n2_in, ring1)
    ring2 = onward(spread_back(2, n2_near, n2, n2_in, ring1).astype(bf16))
    r3, w3 = join(e3, e3_in), join(w3, w3_in)
    n3, *k3 = expert(r3, w3)
    n3, ring2 = tie(n3, ring2)
    n3_in = across(n3[slots:])
    s_act, s_gate_part, s_up_part = (
        jnp.concatenate(pieces, axis=0) for pieces in zip(s0, s1, s2, s3)
    )
    b_all = jnp.concatenate([b0, b1, b2, b3], axis=0)
    g_all = jnp.concatenate([g0, g1, g2, g3], axis=0)
    grad_s_cols = dot_first(b_all, jnp.concatenate([s_gate_part, s_up_part], axis=1)).astype(bf16)
    grad_s_cols, n3_in = tie(grad_s_cols, n3_in)
    ring3 = onward(spread_back(3, n3_near, n3, n3_in, ring2).astype(bf16))
    e_rows = jnp.concatenate([r0, r1, r2, r3], axis=0)
    e_grad = jnp.concatenate([w0, w1, w2, w3], axis=0)
    activated, gate_part, up_part = (
        jnp.concatenate(pieces, axis=0) for pieces in zip(k0, k1, k2, k3)
    )
    grad_e_gate = dot_first(e_rows, gate_part).astype(bf16)
    grad_e_up = dot_first(e_rows, up_part).astype(bf16)
    e_result = matmul(activated, expert_down[0]).astype(bf16).reshape(half, 2 * slots, width)
    grad_s_down = dot_first(s_act, g_all).astype(bf16)
    grad_e_gate, grad_e_up, ring3, activated, s_act, e_result, grad_s_down = tie(
        grad_e_gate, grad_e_up, ring3, activated, s_act, e_result, grad_s_down
    )
    grad_second = spread_back(0, n0_near, n0, n0_in, ring3)
    o_in = across(e_result[:, slots:])
    grad_e_down = dot_first(activated, e_grad).astype(bf16)

    def out_term(s, *more):
        weighed = (join(e_result[s], o_in[s]).astype(f32) * gates_all[s]).astype(bf16)
        total = matmul(s_act[s * tok_dev : (s + 1) * tok_dev], sd) + dot_first(
            pick_all[s], weighed
        )
        for other in more:
            total = total + other.astype(f32)
        return total

    grad_e_gate = lax.psum_scatter(grad_e_gate, "dp", scatter_dimension=0, tiled=True)
    grad_e_up = lax.psum_scatter(grad_e_up, "dp", scatter_dimension=0, tiled=True)
    grad_e_down_all, grad_s_down = grad_e_down, grad_s_down[:ff_own]

    def sum_columns(grads):
        return lax.psum_scatter(grads, "dp", scatter_dimension=0, tiled=True)

    grad_s_cols = sum_columns(grad_s_cols)

    def ff_restore(cut):
        both = cut[:, :, :ff_own].astype(f32).reshape(half, 2, rows_w, spread, 2 * ff_cut)
        return (both[:, 0] + both[:, 1]).transpose(1, 2, 0, 3).reshape(rows_w, -1)

    grad_f = grad_out.astype(f32)
    grad_resid_norm, grad_f_gain = second_norm_back(grad_second)
    grad_resid = grad_f + grad_resid_norm
    grad_attn_out = grad_resid.astype(bf16)
    grad_w_out = dot_first(attn_own, grad_attn_out).astype(bf16)
    grad_attended = dot_last(grad_attn_out, wo).astype(bf16)
    grad_heads = lax.all_to_all(grad_attended, "expert", split_axis=1, concat_axis=0, tiled=True)
    grad_heads, grad_w_out, grad_s_cols, grad_e_down, grad_s_down = tie(
        grad_heads,
        grad_w_out,
        grad_s_cols,
        grad_e_down_all,
        grad_s_down,
    )
    s_keep, s_other = line_swap(
        grad_s_down.reshape((2,) * (spread.bit_length() - 1) + (2, ff_cut, width)), 0
    )
    grad_s_cut = lax.all_to_all(
        grad_s_cols.reshape(group, rows_w, -1), "expert", split_axis=0, concat_axis=0, tiled=True
    )
    grad_w_out = lax.psum_scatter(grad_w_out, "dp", scatter_dimension=0, tiled=True)
    grad_q_lin, grad_kv, lat_part = attend_back(
        reach, q_att, k_att, v_att, grad_heads, attended, log_total, we, tables, scale
    )
    lat_part, grad_q_lin, o_in, grad_e_down, s_other = tie(
        lat_part, grad_q_lin, o_in, grad_e_down, s_other
    )
    ring1 = onward(out_term(1).astype(bf16))
    grad_s_down = both_halves(s_keep, s_other)
    for m in range(1, spread.bit_length() - 1):
        s_keep, s_other = line_swap(grad_s_down, m)
        if m < spread.bit_length() - 2:
            grad_s_down = both_halves(s_keep, s_other)
    (grad_lat_sum,) = reduce_rows([lat_part.reshape(group, tok_dev, -1)], 5, 2)
    grad_lat_sum, grad_q_lin, ring1, s_other, grad_w_out, grad_e_down = tie(
        grad_lat_sum, grad_q_lin, ring1, s_other, grad_w_out, grad_e_down
    )
    grad_s_down = both_halves(s_keep, s_other)
    own_side = rank % 2
    s_keep = lax.dynamic_index_in_dim(grad_s_down, own_side, 0, False)
    s_other = across(lax.dynamic_index_in_dim(grad_s_down, 1 - own_side, 0, False))
    ring2 = onward(out_term(2, ring1).astype(bf16))
    first_part = dot_last(grad_q_lin, wq).astype(bf16).reshape(group, tok_dev, width)
    steps = list(range(1, half)) + [0]
    w_blocks = grad_w_out.reshape(group, rows_w, width)
    w_in = across(jnp.stack([behind(w_blocks, s, 1) for s in steps]))

    def ring_term(blocks, arrived, k, *more):
        total = behind(blocks, steps[k], 0).astype(f32) + arrived[k].astype(f32)
        for other in more:
            total = total + other.astype(f32)
        return total

    def latent_parts(latent_in, gain_vec):
        return (
            norm_rows(latent_in[:, :KV], gain_vec),
            rotate(latent_in[:, KV : KV + ROPE], own_cos, own_sin),
        )

    unused, latent_back = jax.vjp(latent_parts, own(latent), l_gain)
    grad_latent, grad_l_gain = latent_back(
        (grad_lat_sum[:, :KV], grad_lat_sum[:, KV : KV + ROPE])
    )
    grad_latent = grad_latent.astype(bf16)
    grad_w_lat = dot_first(own(h1), grad_latent)[:, : KV + ROPE]
    grad_gains = jnp.stack(
        [
            grad_f_gain,
            jnp.pad(grad_l_gain.reshape(-1, rows_l), ((0, 0), (0, rows_w - rows_l))).reshape(width),
        ],
        axis=1,
    )
    lat_grads_in = jnp.concatenate(
        [grad_w_lat, jnp.pad(grad_gains, ((0, 0), (0, ROPE - 2)))], axis=1
    ).astype(bf16)
    first_part, lat_grads, w_in, grad_q_lin = tie(first_part, lat_grads_in, w_in, grad_q_lin)
    lat_grads = lax.psum_scatter(lat_grads, "dp", scatter_dimension=0, tiled=True)
    w_ring = onward(ring_term(w_blocks, w_in, 0).astype(bf16))
    grad_a_cols = jnp.concatenate(
        [dot_first(h1, grad_q_lin), dot_first(ckv, grad_kv).reshape(width, e_fold)], axis=1
    ).astype(bf16)
    first_part, grad_a_cols, w_ring = tie(first_part, grad_a_cols, w_ring)
    grad_a_cols = lax.psum_scatter(grad_a_cols, "dp", scatter_dimension=0, tiled=True)
    w_ring = onward(ring_term(w_blocks, w_in, 1, w_ring).astype(bf16))
    grad_e_down = lax.psum_scatter(grad_e_down, "dp", scatter_dimension=1, tiled=True)
    (first_sum,) = reduce_rows([first_part], 6, 4)
    (
        first_sum,
        lat_grads,
        ring2,
        w_ring,
        s_keep,
        s_other,
        grad_a_cols,
        grad_s_cut,
        grad_e_gate,
        grad_e_up,
    ) = tie(
        first_sum,
        lat_grads,
        ring2,
        w_ring,
        s_keep,
        s_other,
        grad_a_cols,
        grad_s_cut,
        grad_e_gate,
        grad_e_up,
    )
    w_ring = onward(ring_term(w_blocks, w_in, 2, w_ring).astype(bf16))
    lat_blocks = lat_grads.reshape(group, rows_w, -1)
    lat_in = across(jnp.stack([behind(lat_blocks, s, 1) for s in steps]))
    ring3 = onward(out_term(3, ring2).astype(bf16))
    grad_first = first_sum + dot_last(grad_latent[:, :lat_w], wl)
    unused, first_norm_back = jax.vjp(lambda v: norm_rows(v, a_gain), tokens_f)
    (grad_tokens_norm,) = first_norm_back(grad_first)
    grad_tokens = grad_resid + grad_tokens_norm
    grad_tokens, lat_in, w_ring = tie(grad_tokens, lat_in, w_ring)
    grad_w_out = ring_term(w_blocks, w_in, 3, w_ring)
    lat_ring = onward(ring_term(lat_blocks, lat_in, 0).astype(bf16))
    grad_s_gate = ff_restore(grad_s_cut[:, :, :ff_pad])
    grad_s_gate, grad_s_cut, lat_ring = tie(grad_s_gate, grad_s_cut, lat_ring)
    lat_ring = onward(ring_term(lat_blocks, lat_in, 1, lat_ring).astype(bf16))
    grad_s_up = ff_restore(grad_s_cut[:, :, ff_pad:])
    grad_s_up, lat_ring, ring3 = tie(grad_s_up, lat_ring, ring3)
    block_out = (resid + out_term(0, ring3)).astype(bf16)
    lat_ring = onward(ring_term(lat_blocks, lat_in, 2, lat_ring).astype(bf16))
    lat_grads = ring_term(lat_blocks, lat_in, 3, lat_ring)
    grad_s_down = s_keep.astype(f32) + s_other.astype(f32)
    grad_w_lat = lat_grads[:, :lat_w]
    grad_f_gain = lat_grads[:, lat_w]
    grad_l_gain = lat_grads[:rows_l, lat_w + 1]
    grad_a_cols = lax.all_to_all(
        grad_a_cols.reshape(group, rows_w, -1), "expert", split_axis=0, concat_axis=0, tiled=True
    )
    grad_w_q = (
        grad_a_cols[:, :, :q_own]
        .reshape(group, rows_w, mine, KEY)[..., : NOPE + ROPE]
        .transpose(1, 0, 2, 3)
        .reshape(rows_w, -1)
        .astype(f32)
    )
    grad_w_exp = (
        grad_a_cols[:, :, q_own:]
        .reshape(group, rows_l, e_own)
        .transpose(1, 0, 2)
        .reshape(rows_l, -1)
        .astype(f32)
    )
    grad_a_gain = (
        jnp.sum(grad_w_q * w_query.astype(f32), axis=1)
        + jnp.sum(grad_w_lat * w_latent.astype(f32), axis=1)
    ) / attn_gain.astype(f32)

    return (
        block_out,
        grad_tokens,
        grad_a_gain,
        grad_w_q,
        grad_w_lat,
        grad_l_gain,
        grad_w_exp,
        grad_w_out,
        grad_f_gain,
        grad_s_gate,
        grad_s_up,
        grad_s_down,
        grad_e_gate.astype(f32)[None],
        grad_e_up.astype(f32)[None],
        grad_e_down.astype(f32)[None],
    )


def solution(mesh):
    placed = (
        P(EVERY, None),
        P(EVERY, None),
        P(EVERY, None),
        P(EVERY, None),
        P("dp", None),
        P(EVERY),
        P(EVERY, None),
        P(EVERY, None),
        P(EVERY),
        P(EVERY, None),
        P(EVERY, None),
        P(EVERY),
        P(EVERY, None),
        P(EVERY, None),
        P(EVERY, None),
        P("expert", None, None),
        P("expert", None, None),
        P("expert", None, None),
    )
    return jax.shard_map(
        per_device,
        mesh=mesh,
        in_specs=placed,
        out_specs=(
            P(EVERY, None),
            P(EVERY, None),
            P(EVERY),
            P(EVERY, None),
            P(EVERY, None),
            P(EVERY),
            P(EVERY, None),
            P(EVERY, None),
            P(EVERY),
            P(EVERY, None),
            P(EVERY, None),
            P(EVERY, None),
            P("expert", "dp", None),
            P("expert", "dp", None),
            P("expert", None, "dp"),
        ),
        check_vma=False,
    )
```

```python
import functools

import jax
import jax.numpy as jnp
from jax import lax
from jax.experimental import pallas as pl
from jax.experimental.pallas import tpu as pltpu
from jax.sharding import PartitionSpec as P

HEADS = 16
NOPE = 128
ROPE = 64
KV = 512
VD = 128
SEG = 256
KEY = 256

epsilon = 1e-06
bf16 = jnp.bfloat16
f32 = jnp.float32
EVERY = ("dp", "expert")
MESH = pl.DeviceIdType.MESH
VMEM_LIMIT = 60 << 20
WIRE = pl.CostEstimate(flops=0, bytes_accessed=300_000_000, transcendentals=0)


def norm_rows(values, gain_vec):
    return (
        values * lax.rsqrt(jnp.mean(values * values, axis=-1, keepdims=True) + epsilon) * gain_vec
    )


def rotate(values, cos_table, sin_table):
    half_width = values.shape[-1] // 2
    first_half = values[..., :half_width]
    second_half = values[..., half_width:]
    return jnp.concatenate(
        [
            first_half * cos_table - second_half * sin_table,
            second_half * cos_table + first_half * sin_table,
        ],
        axis=-1,
    )


def gating(gate_part, up_part):
    return jax.nn.silu(gate_part) * up_part


def ancestry(parent_row, seg_count):
    identity = jnp.eye(seg_count, dtype=f32)
    parent_hot = (parent_row[:, None] == jnp.arange(seg_count, dtype=jnp.int32)[None, :]).astype(
        f32
    )
    reachable = identity
    for _ in range(seg_count - 1):
        reachable = jnp.maximum(identity, jnp.dot(parent_hot, reachable))
    return reachable


def matmul(left, right):
    return jnp.dot(left, right, preferred_element_type=f32)


def dot_last(left, right):
    return lax.dot_general(left, right, (((1,), (1,)), ((), ())), preferred_element_type=f32)


def dot_first(left, right):
    return lax.dot_general(left, right, (((0,), (0,)), ((), ())), preferred_element_type=f32)


def greet(rank, last):
    barrier = pltpu.get_barrier_semaphore()
    a = rank // 2

    def hail(other):
        pl.semaphore_signal(barrier, inc=1, device_id={"expert": other}, device_id_type=MESH)

    hail(rank + 1 - 2 * (rank % 2))

    @pl.when(a < last)
    def _():
        hail(rank + 2)

    @pl.when(a > 0)
    def _():
        hail(rank - 2)

    pl.semaphore_wait(barrier, 1 + (a + last - 1) // last + (2 * last - 1 - a) // last)


class Chain:
    def __init__(self, chunks, x_ref, o_ref, sx, rx, su, ru, sd, rd):
        self.chunks, self.x, self.o = chunks, x_ref, o_ref
        self.sems = (sx, rx, su, ru, sd, rd)
        self.rank = lax.axis_index("expert")
        self.last = o_ref.shape[0] // 2 - 1
        self.a = self.rank // 2
        self.side = self.rank + 1 - 2 * (self.rank % 2)
        self.rows = x_ref.shape[0] // chunks

    def piece(self, ref, c):
        return ref.at[pl.ds(c * self.rows, self.rows)]

    def to(self, src, block, c, send, recv, target):
        return pltpu.make_async_remote_copy(
            src_ref=src,
            dst_ref=self.piece(self.o.at[block], c),
            send_sem=send,
            recv_sem=recv,
            device_id={"expert": target},
            device_id_type=MESH,
        )

    def start(self):
        sx, rx, su, ru, sd, rd = self.sems
        rank, a, last, to = self.rank, self.a, self.last, self.to
        for c in range(self.chunks):
            own = self.piece(self.x, c)
            to(own, rank, c, sx.at[0, c], rx.at[0, c], self.side).start()

            @pl.when(a < last)
            def _():
                to(own, rank, c, su.at[0, c], ru.at[0, c], rank + 2).start()

            @pl.when(a > 0)
            def _():
                to(own, rank, c, sd.at[0, c], rd.at[0, c], rank - 2).start()

    def step(self, s):
        sx, rx, su, ru, sd, rd = self.sems
        rank, a, last, to = self.rank, self.a, self.last, self.to
        for c in range(self.chunks):

            @pl.when(a >= s)
            def _():
                block = rank - 2 * s
                src = self.piece(self.o.at[block], c)
                to(src, block, c, su.at[s - 1, c], ru.at[s - 1, c], rank + 2).wait_recv()
                to(src, block, c, sx.at[s, c], rx.at[s, c], self.side).start()

                @pl.when(a < last)
                def _():
                    to(src, block, c, su.at[s, c], ru.at[s, c], rank + 2).start()

            @pl.when(a + s <= last)
            def _():
                block = rank + 2 * s
                src = self.piece(self.o.at[block], c)
                to(src, block, c, sd.at[s - 1, c], rd.at[s - 1, c], rank - 2).wait_recv()
                to(src, block, c, sx.at[last + s, c], rx.at[last + s, c], self.side).start()

                @pl.when(a > 0)
                def _():
                    to(src, block, c, sd.at[s, c], rd.at[s, c], rank - 2).start()

    def finish(self):
        sx, rx, su, ru, sd, rd = self.sems
        rank, a, last, to, side = self.rank, self.a, self.last, self.to, self.side
        for c in range(self.chunks):
            own = self.piece(self.x, c)
            to(own, side, c, sx.at[0, c], rx.at[0, c], side).wait()

            @pl.when(a < last)
            def _():
                to(own, rank, c, su.at[0, c], ru.at[0, c], rank + 2).wait_send()

            @pl.when(a > 0)
            def _():
                to(own, rank, c, sd.at[0, c], rd.at[0, c], rank - 2).wait_send()

        for s in range(1, last + 1):
            for c in range(self.chunks):

                @pl.when(a >= s)
                def _():
                    block = rank - 2 * s
                    src = self.piece(self.o.at[block], c)
                    to(src, side - 2 * s, c, sx.at[s, c], rx.at[s, c], side).wait()

                    @pl.when(a < last)
                    def _():
                        to(src, block, c, su.at[s, c], ru.at[s, c], rank + 2).wait_send()

                @pl.when(a + s <= last)
                def _():
                    block = rank + 2 * s
                    src = self.piece(self.o.at[block], c)
                    to(src, side + 2 * s, c, sx.at[last + s, c], rx.at[last + s, c], side).wait()

                    @pl.when(a > 0)
                    def _():
                        to(src, block, c, sd.at[s, c], rd.at[s, c], rank - 2).wait_send()


def chain_sems(count, chunks):
    half = count // 2
    dma = pltpu.SemaphoreType.DMA
    return [dma((2 * half, chunks))] * 2 + [dma((half, chunks))] * 4


class Share:
    def __init__(self, ref, send_out, recv_out, send_pass, recv_pass):
        self.ref = ref
        self.sems = (send_out, recv_out, send_pass, recv_pass)
        self.line = lax.axis_index("dp")
        self.count = ref.shape[0] // 2

    def out(self, k):
        peer = 2 * lax.rem(self.line // 2 + k, self.count) + self.line % 2
        return pltpu.make_async_remote_copy(
            src_ref=self.ref.at[self.line],
            dst_ref=self.ref.at[self.line],
            send_sem=self.sems[0].at[k],
            recv_sem=self.sems[1].at[k],
            device_id={"dp": peer},
            device_id_type=MESH,
        )

    def hand(self, k):
        slab = 2 * lax.rem(self.line // 2 + self.count - k, self.count) + self.line % 2
        return pltpu.make_async_remote_copy(
            src_ref=self.ref.at[slab],
            dst_ref=self.ref.at[slab],
            send_sem=self.sems[2].at[k],
            recv_sem=self.sems[3].at[k],
            device_id={"dp": self.line + 1 - 2 * (self.line % 2)},
            device_id_type=MESH,
        )

    def start(self):
        for k in range(1, self.count):
            self.out(k).start()
        self.hand(0).start()

    def middle(self):
        for k in range(1, self.count):
            self.out(k).wait_recv()
            self.hand(k).start()

    def finish(self):
        for k in range(1, self.count):
            self.out(k).wait_send()
        for k in range(self.count):
            self.hand(k).wait()


def prologue_kernel(
    chunks,
    x_ref,
    w_ref,
    d_ref,
    t_ref,
    o_ref,
    pk_ref,
    do_ref,
    to_ref,
    wa_s,
    wa_r,
    ta_s,
    ta_r,
    da_s,
    da_r,
    *sems,
):
    group, spread = o_ref.shape[0], pk_ref.shape[0]
    packs, downs = Share(pk_ref, *sems[:4]), Share(do_ref, *sems[4:8])
    chain = Chain(chunks, x_ref, o_ref, *sems[8:])
    rank, line = chain.rank, packs.line
    mine = rank % 2
    barrier = pltpu.get_barrier_semaphore()
    for k in range(1, group):
        pl.semaphore_signal(
            barrier,
            inc=1,
            device_id={"expert": lax.rem(rank + k, group)},
            device_id_type=MESH,
        )
    for k in range(1, packs.count):
        peer = 2 * lax.rem(line // 2 + k, packs.count) + line % 2
        pl.semaphore_signal(barrier, inc=1, device_id={"dp": peer}, device_id_type=MESH)
    pl.semaphore_signal(
        barrier, inc=1, device_id={"dp": line + 1 - 2 * (line % 2)}, device_id_type=MESH
    )
    pl.semaphore_wait(barrier, group - 1 + packs.count)

    def far(src, dst, send, recv, peer):
        return pltpu.make_async_remote_copy(
            src_ref=src,
            dst_ref=dst,
            send_sem=send,
            recv_sem=recv,
            device_id={"expert": peer},
            device_id_type=MESH,
        )

    def cut(k):
        peer = lax.rem(rank + k, group)
        return far(w_ref.at[peer], pk_ref.at[line, rank], wa_s.at[k - 1], wa_r.at[k - 1], peer)

    def gates(k):
        peer = lax.rem(rank + k, group)
        return far(t_ref, to_ref.at[rank], ta_s.at[k - 1], ta_r.at[k - 1], peer)

    def down():
        return far(d_ref, do_ref.at[line, mine], da_s.at[0], da_r.at[0], chain.side)

    down().start()
    for k in range(1, group):
        cut(k).start()
        gates(k).start()
    chain.start()
    pk_ref[line, rank] = w_ref[rank]
    do_ref[line, mine] = d_ref[...]
    to_ref[rank] = t_ref[...]
    o_ref[rank] = x_ref[...]
    down().wait_recv()
    downs.start()
    for k in range(1, group):
        cut(k).wait_recv()
    packs.start()
    for s in range(1, chain.last):
        chain.step(s)
    downs.middle()
    packs.middle()
    chain.step(chain.last)
    chain.finish()
    down().wait_send()
    for k in range(1, group):
        cut(k).wait_send()
        gates(k).wait()
    downs.finish()
    packs.finish()


def prologue(x, cuts, down, gates, spread, call_id, chunks=2):
    group = cuts.shape[0]
    dma = pltpu.SemaphoreType.DMA
    vmem = pl.BlockSpec(memory_space=pltpu.VMEM)
    return pl.pallas_call(
        functools.partial(prologue_kernel, chunks),
        out_shape=[
            jax.ShapeDtypeStruct((group,) + x.shape, x.dtype),
            jax.ShapeDtypeStruct((spread,) + cuts.shape, cuts.dtype),
            jax.ShapeDtypeStruct((spread, 2) + down.shape, down.dtype),
            jax.ShapeDtypeStruct((group,) + gates.shape, gates.dtype),
        ],
        in_specs=[vmem] * 4,
        out_specs=[vmem] * 4,
        scratch_shapes=[dma((group - 1,))] * 4
        + [dma((1,))] * 2
        + [dma((spread // 2,))] * 8
        + chain_sems(group, chunks),
        compiler_params=pltpu.CompilerParams(
            collective_id=call_id, has_side_effects=True, vmem_limit_bytes=VMEM_LIMIT
        ),
        cost_estimate=WIRE,
        name="prologue",
    )(x, cuts, down, gates)


def ring_pairs(group):
    half = group // 2
    side = [(r, r + 1 - 2 * (r % 2)) for r in range(group)]
    onward = [(2 * a + b, 2 * ((a + 1) % half) + b) for a in range(half) for b in range(2)]
    return side, onward


def tie(*values):
    return lax.optimization_barrier(values)


def reduce_kernel(parts, *refs):
    n = len(parts)
    p_refs, o_refs = refs[:n], refs[n : 2 * n]
    bufs = [refs[2 * n + 4 * k : 2 * n + 4 * k + 4] for k in range(n)]
    acc, sxs, rxs, sus, rus, sds, rds = refs[6 * n :]
    rank = lax.axis_index("expert")
    last = p_refs[0].shape[0] // 2 - 1
    a = rank // 2
    b = rank % 2
    greet(rank, last)
    h = a // 2
    order = [3 - 3 * h, 2 - h, 4 * h + 1 - a, a]
    pieces = []
    for k, chunks in enumerate(parts):
        rows = p_refs[k].shape[1] // chunks
        pieces += [(k, c * rows, rows) for c in range(chunks)]

    def copy(src, dst, send, recv, target):
        return pltpu.make_async_remote_copy(
            src_ref=src,
            dst_ref=dst,
            send_sem=send,
            recv_sem=recv,
            device_id={"expert": target},
            device_id_type=MESH,
        )

    for t in order:
        for c, (k, at, rows) in enumerate(pieces):
            src = p_refs[k].at[2 * t + 1 - b, pl.ds(at, rows)]
            dst = bufs[k][0].at[t, pl.ds(at, rows)]
            copy(src, dst, sxs.at[t, c], rxs.at[t, c], rank + 1 - 2 * b).start()

    def moves(t, c, k, at, rows):
        cut = pl.ds(at, rows)
        rx, st, ru, rd = (buf.at[t, cut] for buf in bufs[k])
        src = p_refs[k].at[2 * t + 1 - b, cut]
        across = copy(src, rx, sxs.at[t, c], rxs.at[t, c], rank + 1 - 2 * b)
        upward = copy(st, ru, sus.at[t, c], rus.at[t, c], rank + 2)
        downward = copy(st, rd, sds.at[t, c], rds.at[t, c], rank - 2)
        return rx, st, ru, rd, across, upward, downward

    for t in order:
        for c, (k, at, rows) in enumerate(pieces):
            rx, st, ru, rd, across, upward, downward = moves(t, c, k, at, rows)
            width = p_refs[k].shape[2]
            total = acc.at[pl.ds(0, rows), pl.ds(0, width)]
            across.wait_recv()
            total[...] = p_refs[k][2 * t + b, pl.ds(at, rows)].astype(f32) + rx[...].astype(f32)

            @pl.when((t >= a) & (a > 0))
            def _():
                upward.wait_recv()
                total[...] += ru[...].astype(f32)

            @pl.when((t <= a) & (a < last))
            def _():
                downward.wait_recv()
                total[...] += rd[...].astype(f32)

            @pl.when(t == a)
            def _():
                o_refs[k][pl.ds(at, rows)] = total[...]

            @pl.when(t > a)
            def _():
                st[...] = total[...].astype(bf16)
                upward.start()

            @pl.when(t < a)
            def _():
                st[...] = total[...].astype(bf16)
                downward.start()

    for t in order:
        for c, (k, at, rows) in enumerate(pieces):
            rx, st, ru, rd, across, upward, downward = moves(t, c, k, at, rows)
            across.wait_send()

            @pl.when(t > a)
            def _():
                upward.wait_send()

            @pl.when(t < a)
            def _():
                downward.wait_send()


def reduce_rows(operands, call_id, most):
    half = operands[0].shape[0] // 2
    parts = [
        max(c for c in range(1, most + 1) if p.shape[1] % (16 * c) == 0 and p.shape[1] // c >= 16)
        if p.shape[1] > 64
        else 1
        for p in operands
    ]
    high = max(p.shape[1] // c for p, c in zip(operands, parts))
    wide = max(p.shape[2] for p in operands)
    sem = pltpu.SemaphoreType.DMA((half, sum(parts)))
    vmem = pl.BlockSpec(memory_space=pltpu.VMEM)
    bufs = [
        pltpu.VMEM((half,) + p.shape[1:], p.dtype) for p in operands for _ in range(4)
    ]
    return pl.pallas_call(
        functools.partial(reduce_kernel, parts),
        out_shape=[jax.ShapeDtypeStruct(p.shape[1:], f32) for p in operands],
        in_specs=[vmem] * len(operands),
        out_specs=[vmem] * len(operands),
        scratch_shapes=bufs + [pltpu.VMEM((high, wide), f32)] + [sem] * 6,
        compiler_params=pltpu.CompilerParams(
            collective_id=call_id, has_side_effects=True, vmem_limit_bytes=VMEM_LIMIT
        ),
        cost_estimate=pl.CostEstimate(
            flops=0, bytes_accessed=36 * sum(p.size for p in operands) * 2, transcendentals=0
        ),
        name="reduce_rows",
    )(*operands)


def swap_halves(values):
    lane = lax.broadcasted_iota(jnp.int32, values.shape, 1)
    half = ROPE // 2
    return jnp.where(lane < half, pltpu.roll(values, KEY - NOPE - half, 1), pltpu.roll(values, half, 1))


def turns(seg_cos, seg_sin, off_cos, off_sin):
    lane = lax.broadcasted_iota(jnp.int32, off_cos.shape, 1)
    sine = seg_sin * off_cos + seg_cos * off_sin
    return seg_cos * off_cos - seg_sin * off_sin, jnp.where(lane < ROPE // 2, -sine, sine)


def project_kernel(
    heads,
    x_ref,
    wq_ref,
    wl_ref,
    we_ref,
    ag_ref,
    lg_ref,
    sc_ref,
    ss_ref,
    oc_ref,
    os_ref,
    h1_ref,
    q_ref,
    k_ref,
    v_ref,
    lat_ref,
    ckv_ref,
):
    i = pl.program_id(0)
    x = x_ref[...].astype(f32)
    power = jnp.mean(x * x, axis=-1, keepdims=True)
    h1 = (x * lax.rsqrt(power + epsilon) * ag_ref[...]).astype(bf16)
    h1_ref[...] = h1
    cosine, sine = turns(sc_ref[pl.ds(i, 1)], ss_ref[pl.ds(i, 1)], oc_ref[...], os_ref[...])

    def turn(values):
        return (values * cosine + swap_halves(values) * sine).astype(bf16)

    query = matmul(h1, wq_ref[...])
    for h in range(heads):
        at = h * KEY
        q_ref[:, at : at + NOPE] = query[:, at : at + NOPE].astype(bf16)
        q_ref[:, at + NOPE : at + KEY] = turn(query[:, at + NOPE : at + KEY])
    latent = matmul(h1, wl_ref[...])
    lat_ref[...] = latent
    low = latent[:, :KV]
    power = jnp.mean(low * low, axis=-1, keepdims=True)
    ckv = (low * lax.rsqrt(power + epsilon) * lg_ref[...]).astype(bf16)
    ckv_ref[...] = ckv
    krope = turn(latent[:, KV:])
    kv = matmul(ckv, we_ref[...]).astype(bf16)
    for h in range(heads):
        at = h * KEY
        k_ref[:, at : at + NOPE] = kv[:, at : at + NOPE]
        k_ref[:, at + NOPE : at + KEY] = krope
        v_ref[:, h * VD : (h + 1) * VD] = kv[:, at + NOPE : at + KEY]


def project(x, packed, lat_pack, we, a_gain, l_gain, tables, heads):
    tree, width = x.shape
    segs = tree // SEG
    lat_width = lat_pack.shape[1]
    fixed = lambda arr: pl.BlockSpec(arr.shape, lambda i: (0, 0))
    part = lambda cols: pl.BlockSpec((SEG, cols), lambda i: (i, 0))
    return pl.pallas_call(
        functools.partial(project_kernel, heads),
        grid=(segs,),
        in_specs=[
            part(width),
            pl.BlockSpec((width, heads * KEY), lambda i: (0, 0)),
            fixed(lat_pack),
            fixed(we),
            fixed(a_gain),
            fixed(l_gain),
        ]
        + [fixed(table) for table in tables],
        out_specs=[
            part(width),
            part(heads * KEY),
            part(heads * KEY),
            part(heads * VD),
            part(lat_width),
            part(KV),
        ],
        out_shape=[
            jax.ShapeDtypeStruct((tree, width), bf16),
            jax.ShapeDtypeStruct((tree, heads * KEY), bf16),
            jax.ShapeDtypeStruct((tree, heads * KEY), bf16),
            jax.ShapeDtypeStruct((tree, heads * VD), bf16),
            jax.ShapeDtypeStruct((tree, lat_width), f32),
            jax.ShapeDtypeStruct((tree, KV), bf16),
        ],
        compiler_params=pltpu.CompilerParams(vmem_limit_bytes=VMEM_LIMIT),
        cost_estimate=pl.CostEstimate(flops=0, bytes_accessed=60_000_000, transcendentals=0),
        name="project",
    )(x, packed, lat_pack, we, a_gain, l_gain, *tables)


def triangle():
    keys = lax.broadcasted_iota(jnp.int32, (SEG, SEG), 0)
    queries = lax.broadcasted_iota(jnp.int32, (SEG, SEG), 1)
    return keys <= queries


def attend_kernel(
    heads, segs, scale, reach_ref, q_ref, k_ref, v_ref, out_ref, full_ref, log_ref, m_s, l_s, acc_s
):
    i = pl.program_id(0)
    diag = triangle()

    def score(h, j):
        keys = k_ref[pl.ds(j * SEG, SEG), h * KEY : (h + 1) * KEY]
        return dot_last(keys, q_ref[:, h * KEY : (h + 1) * KEY]) * scale

    def weigh(h, j, weights):
        vals = v_ref[pl.ds(j * SEG, SEG), h * VD : (h + 1) * VD]
        return dot_first(vals, weights.astype(bf16))

    for h in range(heads):
        s = jnp.where(diag, score(h, i), -1e30)
        top = jnp.max(s, axis=0, keepdims=True)
        w = jnp.where(diag, jnp.exp(s - top), 0.0)
        m_s[h : h + 1] = top
        l_s[h : h + 1] = jnp.sum(w, axis=0, keepdims=True)
        acc_s[h] = weigh(h, i, w)

    def step(j, carry):
        @pl.when(reach_ref[i * segs + j] > 0)
        def _():
            for h in range(heads):
                s = score(h, j)
                old = m_s[h : h + 1]
                top = jnp.maximum(old, jnp.max(s, axis=0, keepdims=True))
                w = jnp.exp(s - top)
                fade = jnp.exp(old - top)
                m_s[h : h + 1] = top
                l_s[h : h + 1] = l_s[h : h + 1] * fade + jnp.sum(w, axis=0, keepdims=True)
                acc_s[h] = acc_s[h] * fade + weigh(h, j, w)

        return carry

    lax.fori_loop(0, i, step, 0)
    for h in range(heads):
        total = l_s[h : h + 1]
        rows = (acc_s[h] * (1.0 / total)).T
        full_ref[:, h * VD : (h + 1) * VD] = rows
        out_ref[:, h * VD : (h + 1) * VD] = rows.astype(bf16)
        log_ref[h : h + 1] = m_s[h : h + 1] + jnp.log(total)


def attend(reach, q, k, v, scale):
    tree = q.shape[0]
    segs = tree // SEG
    heads = q.shape[1] // KEY
    whole = lambda width: pl.BlockSpec((tree, width), lambda i, r: (0, 0))
    part = lambda width: pl.BlockSpec((SEG, width), lambda i, r: (i, 0))
    return pl.pallas_call(
        functools.partial(attend_kernel, heads, segs, scale),
        grid_spec=pltpu.PrefetchScalarGridSpec(
            num_scalar_prefetch=1,
            grid=(segs,),
            in_specs=[part(heads * KEY), whole(heads * KEY), whole(heads * VD)],
            out_specs=[
                part(heads * VD),
                part(heads * VD),
                pl.BlockSpec((heads, SEG), lambda i, r: (0, i)),
            ],
            scratch_shapes=[
                pltpu.VMEM((heads, SEG), f32),
                pltpu.VMEM((heads, SEG), f32),
                pltpu.VMEM((heads, VD, SEG), f32),
            ],
        ),
        out_shape=[
            jax.ShapeDtypeStruct((tree, heads * VD), bf16),
            jax.ShapeDtypeStruct((tree, heads * VD), f32),
            jax.ShapeDtypeStruct((heads, tree), f32),
        ],
        compiler_params=pltpu.CompilerParams(vmem_limit_bytes=VMEM_LIMIT),
        cost_estimate=pl.CostEstimate(flops=0, bytes_accessed=70_000_000, transcendentals=0),
        name="attend",
    )(reach, q, k, v)


def attend_back_kernel(
    heads,
    segs,
    scale,
    reach_ref,
    q_ref,
    k_ref,
    v_ref,
    g_ref,
    att_ref,
    log_ref,
    we_ref,
    sc_ref,
    ss_ref,
    oc_ref,
    os_ref,
    gq_ref,
    dkv_ref,
    lat_ref,
    dq_s,
    dk_s,
    dv_s,
    delta_s,
):
    j = pl.program_id(0)
    diag = triangle()

    @pl.when(j == 0)
    def _():
        def prepare(i, carry):
            rows = pl.ds(i * SEG, SEG)
            for h in range(heads):
                vcols = slice(h * VD, (h + 1) * VD)
                both = g_ref[rows, vcols].astype(f32) * att_ref[rows, vcols]
                delta_s[h : h + 1, rows] = jnp.sum(both.T, axis=0, keepdims=True)
            dq_s[rows] = jnp.zeros((SEG, heads * KEY), f32)
            return carry

        lax.fori_loop(0, segs, prepare, 0)

    dk_s[...] = jnp.zeros_like(dk_s)
    dv_s[...] = jnp.zeros_like(dv_s)

    def block(i, masked):
        rows = pl.ds(i * SEG, SEG)
        for h in range(heads):
            kcols = slice(h * KEY, (h + 1) * KEY)
            vcols = slice(h * VD, (h + 1) * VD)
            q = q_ref[rows, kcols]
            k = k_ref[:, kcols]
            g = g_ref[rows, vcols]
            s = dot_last(k, q) * scale
            w = jnp.exp(s - log_ref[h : h + 1, rows])
            if masked:
                w = jnp.where(diag, w, 0.0)
            dw = dot_last(v_ref[:, vcols], g)
            ds = (w * (dw - delta_s[h : h + 1, rows])).astype(bf16)
            dv_s[h] += matmul(w.astype(bf16), g)
            dk_s[h] += matmul(ds, q)
            dq_s[rows, kcols] += dot_first(ds, k)

    block(j, True)

    def step(i, carry):
        @pl.when(reach_ref[i * segs + j] > 0)
        def _():
            block(i, False)

        return carry

    lax.fori_loop(j + 1, segs, step, 0)
    rope = jnp.zeros((SEG, KEY - NOPE), f32)
    for h in range(heads):
        dkv_ref[:, h * KEY : h * KEY + NOPE] = (dk_s[h, :, :NOPE] * scale).astype(bf16)
        dkv_ref[:, h * KEY + NOPE : (h + 1) * KEY] = dv_s[h].astype(bf16)
        rope = rope + dk_s[h, :, NOPE:]
    lat_ref[:, :KV] = dot_last(dkv_ref[...], we_ref[...]).astype(bf16)
    lat_ref[:, KV:] = (rope * scale).astype(bf16)

    @pl.when(j == segs - 1)
    def _():
        def finish(i, carry):
            rows = pl.ds(i * SEG, SEG)
            cosine, sine = turns(
                sc_ref[pl.ds(i, 1)], ss_ref[pl.ds(i, 1)], oc_ref[...], os_ref[...]
            )
            for h in range(heads):
                at = h * KEY
                gq_ref[rows, at : at + NOPE] = (dq_s[rows, at : at + NOPE] * scale).astype(bf16)
                turned = dq_s[rows, at + NOPE : at + KEY] * scale
                gq_ref[rows, at + NOPE : at + KEY] = (
                    turned * cosine - swap_halves(turned) * sine
                ).astype(bf16)
            return carry

        lax.fori_loop(0, segs, finish, 0)


def attend_back(reach, q, k, v, g, attended, log_total, we, tables, scale):
    tree = q.shape[0]
    segs = tree // SEG
    heads = q.shape[1] // KEY
    whole = lambda width: pl.BlockSpec((tree, width), lambda j, r: (0, 0))
    part = lambda width: pl.BlockSpec((SEG, width), lambda j, r: (j, 0))
    fixed = lambda arr: pl.BlockSpec(arr.shape, lambda j, r: (0, 0))
    lat_width = KV + KEY - NOPE
    return pl.pallas_call(
        functools.partial(attend_back_kernel, heads, segs, scale),
        grid_spec=pltpu.PrefetchScalarGridSpec(
            num_scalar_prefetch=1,
            grid=(segs,),
            in_specs=[
                whole(heads * KEY),
                part(heads * KEY),
                part(heads * VD),
                whole(heads * VD),
                whole(heads * VD),
                fixed(log_total),
                fixed(we),
            ]
            + [fixed(table) for table in tables],
            out_specs=[whole(heads * KEY), part(heads * KEY), part(lat_width)],
            scratch_shapes=[
                pltpu.VMEM((tree, heads * KEY), f32),
                pltpu.VMEM((heads, SEG, KEY), f32),
                pltpu.VMEM((heads, SEG, VD), f32),
                pltpu.VMEM((heads, tree), f32),
            ],
        ),
        out_shape=[
            jax.ShapeDtypeStruct((tree, heads * KEY), bf16),
            jax.ShapeDtypeStruct((tree, heads * KEY), bf16),
            jax.ShapeDtypeStruct((tree, lat_width), bf16),
        ],
        compiler_params=pltpu.CompilerParams(vmem_limit_bytes=VMEM_LIMIT),
        cost_estimate=pl.CostEstimate(flops=0, bytes_accessed=90_000_000, transcendentals=0),
        name="attend_back",
    )(reach, q, k, v, g, attended, log_total, we, *tables)


def per_device(
    tokens,
    grad_out,
    routes,
    gate_values,
    parents,
    attn_gain,
    w_query,
    w_latent,
    latent_gain,
    w_expand,
    w_output,
    ffn_gain,
    shared_gate,
    shared_up,
    shared_down,
    expert_gate,
    expert_up,
    expert_down,
):
    group = lax.axis_size("expert")
    spread = lax.axis_size("dp")
    rank = lax.axis_index("expert")
    tok_dev, width = tokens.shape
    tree = tok_dev * group
    segs = parents.shape[1]
    per_token = routes.shape[1]
    capacity = tok_dev * per_token * 9 // (8 * group)
    slots = -(-capacity // 16) * 16
    scale = (NOPE + ROPE) ** (-0.5)
    mine = HEADS // group
    rows_w = w_query.shape[0]
    rows_l = w_expand.shape[0]
    ff_cut = shared_down.shape[0]
    half = group // 2
    ff_own = 2 * ff_cut * spread
    ff_pad = -(-ff_own // 128) * 128
    q_own = mine * KEY
    e_own = mine * (NOPE + VD)
    e_fold = rows_l * e_own // rows_w

    wq_cut = jnp.pad(
        w_query.reshape(rows_w, group, mine, NOPE + ROPE),
        ((0, 0), (0, 0), (0, 0), (0, KEY - NOPE - ROPE)),
    ).reshape(rows_w, group, q_own)

    def ff_columns(weight):
        cut = weight.reshape(rows_w, spread, half, 2 * ff_cut).transpose(2, 0, 1, 3)
        cut = jnp.pad(
            cut.reshape(half, 1, rows_w, ff_own),
            ((0, 0), (0, 0), (0, 0), (0, ff_pad - ff_own)),
        )
        return jnp.broadcast_to(cut, (half, 2, rows_w, ff_pad)).reshape(group, rows_w, ff_pad)

    we_cut = (
        w_expand.reshape(rows_l, group, e_own).transpose(1, 0, 2).reshape(group, rows_w, e_fold)
    )
    packed = jnp.concatenate(
        [
            wq_cut.transpose(1, 0, 2),
            we_cut,
            ff_columns(shared_gate),
            ff_columns(shared_up),
        ],
        axis=2,
    )
    expert_ids = jnp.arange(group, dtype=jnp.int32)
    gate_of = jnp.sum(
        jnp.where(routes[:, :, None] == expert_ids[None, None, :], gate_values[:, :, None], 0.0),
        axis=1,
    ).T
    x_all, packed, sd, gate_of = prologue(tokens, packed, shared_down, gate_of, spread, 0)
    x_all, parents, gate_of = lax.optimization_barrier(
        (x_all.reshape(tree, width), parents, gate_of)
    )
    packed = packed.reshape(width, -1)
    wq = packed[:, :q_own]
    we = packed[:, q_own : q_own + e_fold].reshape(KV, e_own)
    sg = packed[:, q_own + e_fold : q_own + e_fold + ff_pad]
    su = packed[:, q_own + e_fold + ff_pad :]
    sd = jnp.pad(sd.reshape(ff_own, width), ((0, ff_pad - ff_own), (0, 0)))

    lat_w = KV + ROPE
    gains = jnp.stack(
        [attn_gain, ffn_gain, jnp.pad(latent_gain, (0, rows_w - rows_l))], axis=1
    )
    gains = jnp.pad(gains, ((0, 0), (0, ROPE - 3)))
    lat_pack = lax.all_gather(
        jnp.concatenate([w_latent, gains], axis=1), EVERY, axis=0, tiled=True
    )
    wl = lat_pack[:, :lat_w]
    a_gain = lat_pack[:, lat_w].astype(f32)
    f_gain = lat_pack[:, lat_w + 1].astype(f32)
    l_gain = lat_pack[:, lat_w + 2].reshape(-1, rows_w)[:, :rows_l].reshape(KV).astype(f32)
    wo = lax.all_gather(w_output, EVERY, axis=0, tiled=True)
    reachable = ancestry(parents[0], segs)
    depth = jnp.sum(reachable, axis=1) - 1.0
    reach = reachable.astype(jnp.int32).reshape(segs * segs)
    half_width = ROPE // 2
    freq = 10000.0 ** (-2.0 * jnp.arange(half_width, dtype=f32) / ROPE)
    seg_angle = (depth * SEG)[:, None] * freq[None, :]
    off_angle = jnp.arange(SEG, dtype=f32)[:, None] * freq[None, :]

    def lanes(values):
        return jnp.pad(
            jnp.concatenate([values, values], axis=1), ((0, 0), (0, KEY - NOPE - ROPE))
        )

    tables = [
        lanes(jnp.cos(seg_angle)),
        lanes(jnp.sin(seg_angle)),
        lanes(jnp.cos(off_angle)),
        lanes(jnp.sin(off_angle)),
    ]
    seg_cos = lax.dynamic_slice_in_dim(tables[0], rank, 1, 0)[:, :half_width]
    seg_sin = lax.dynamic_slice_in_dim(tables[1], rank, 1, 0)[:, :half_width]
    off_cos = tables[2][:, :half_width]
    off_sin = tables[3][:, :half_width]
    own_cos = seg_cos * off_cos - seg_sin * off_sin
    own_sin = seg_sin * off_cos + seg_cos * off_sin

    def own(values):
        return lax.dynamic_slice_in_dim(values, rank * tok_dev, tok_dev, 0)

    side, ring = ring_pairs(group)

    def across(values):
        return lax.ppermute(values, "expert", side)

    def onward(values):
        return lax.ppermute(values, "expert", ring)

    x_all, g0 = tie(x_all, grad_out)
    g1 = onward(g0)
    h1, q_att, k_att, v_att, latent, ckv = project(
        x_all, packed, lat_pack, we, a_gain[None], l_gain[None], tables, mine
    )
    def behind(values, s, far):
        at = 2 * lax.rem(rank // 2 - s + half, half) + lax.rem(rank + far, 2)
        return lax.dynamic_index_in_dim(values, at, 0, keepdims=False)

    def line_swap(values, m):
        own_bit = lax.rem(lax.axis_index("dp") // (1 << m), 2)
        at = spread.bit_length() - 2 - m
        keep = lax.dynamic_index_in_dim(values, own_bit, at, False)
        send = lax.dynamic_index_in_dim(values, 1 - own_bit, at, False)
        swap = [(d, d ^ (1 << m)) for d in range(spread)]
        return keep, lax.ppermute(send, "dp", swap)

    def both_halves(keep, other):
        return (keep.astype(f32) + other.astype(f32)).astype(bf16)

    gate_of = jnp.concatenate(
        [
            lax.dynamic_slice(
                gate_of,
                (2 * lax.rem(rank // 2 - s + half, half) + rank % 2, rank + k - 2 * k * (rank % 2), 0),
                (1, 1, tok_dev),
            )[0]
            for s in range(half)
            for k in range(2)
        ],
        axis=0,
    )
    routed = gate_of > 0.0
    upto = (
        jnp.arange(tok_dev, dtype=jnp.int32)[:, None]
        <= jnp.arange(tok_dev, dtype=jnp.int32)[None, :]
    )
    place = matmul(routed.astype(bf16), upto.astype(bf16)).astype(jnp.int32) - 1
    chosen = (
        place[:, None, :] == jnp.arange(slots, dtype=jnp.int32)[None, :, None]
    ) & routed[:, None, :]
    pick_all = chosen.astype(bf16).reshape(half, 2 * slots, tok_dev)
    gates_all = jnp.sum(jnp.where(chosen, gate_of[:, None, :], 0.0), axis=2).reshape(
        half, 2 * slots, 1
    )

    def take(s, rows, weights=None):
        picked = matmul(pick_all[s], rows)
        if weights is not None:
            picked = picked * weights
        return picked.astype(bf16)

    q_att, g1 = tie(q_att, g1)
    g2 = onward(g1)
    attn_heads, attended, log_total = attend(reach, q_att, k_att, v_att, scale)
    attn_heads, g2 = tie(attn_heads, g2)
    attn_own = lax.all_to_all(attn_heads, "expert", split_axis=0, concat_axis=1, tiled=True)
    w0, w1, w2 = (take(s, g, gates_all[s]) for s, g in enumerate((g0, g1, g2)))
    far0, far1, far2 = (dot_last(g, sd).astype(bf16) for g in (g0, g1, g2))
    attn_own, w0, w1, w2, far0, far1, far2 = tie(attn_own, w0, w1, w2, far0, far1, far2)
    tokens_f = tokens.astype(f32)
    resid = tokens_f + matmul(attn_own, wo)
    second_normed, second_norm_back = jax.vjp(norm_rows, resid, f_gain)
    b0 = second_normed.astype(bf16)

    b1 = onward(b0)
    def shared(h2, grad_s_act):
        s_act, s_gating_back = jax.vjp(gating, matmul(h2, sg), matmul(h2, su))
        s_act = s_act.astype(bf16)
        gate_part, up_part = s_gating_back(grad_s_act.astype(f32))
        gate_part = gate_part.astype(bf16)
        up_part = up_part.astype(bf16)
        near = dot_last(gate_part, sg) + dot_last(up_part, su)
        return near, s_act, gate_part, up_part

    def expert(e_rows, e_grad):
        activated, e_gating_back = jax.vjp(
            gating, matmul(e_rows, expert_gate[0]), matmul(e_rows, expert_up[0])
        )
        activated = activated.astype(bf16)
        grad_e_act = dot_last(e_grad, expert_down[0]).astype(bf16)
        gate_part, up_part = e_gating_back(grad_e_act.astype(f32))
        gate_part = gate_part.astype(bf16)
        up_part = up_part.astype(bf16)
        grad_rows = (
            dot_last(gate_part, expert_gate[0]) + dot_last(up_part, expert_up[0])
        ).astype(bf16)
        return grad_rows, activated, gate_part, up_part

    def join(mine, arrived):
        return jnp.concatenate([mine[:slots], arrived], axis=0)

    def spread_back(s, near, mine, arrived, *more):
        total = near + dot_first(pick_all[s], join(mine, arrived))
        for other in more:
            total = total + other.astype(f32)
        return total

    e0 = take(0, b0)
    e0_in = across(e0[slots:])
    w0_in, w1_in = (across(w[slots:]) for w in (w0, w1))
    n0_near, *s0 = shared(b0, far0)
    n0_near, b1, e0_in, w0_in, w1_in, g2_last = tie(n0_near, b1, e0_in, w0_in, w1_in, g2)
    b2, g3 = onward(b1), onward(g2_last)
    w2_in = across(w2[slots:])
    e1 = take(1, b1)
    e1_in = across(e1[slots:])
    r0, w0 = join(e0, e0_in), join(w0, w0_in)
    n0, *k0 = expert(r0, w0)
    n0, b1, e1_in, w2_in = tie(n0, b1, e1_in, w2_in)
    n0_in = across(n0[slots:])
    n1_near, *s1 = shared(b1, far1)
    n1_near, b2, e1_in, n0_in, w2_in, g3 = tie(n1_near, b2, e1_in, n0_in, w2_in, g3)
    w3 = take(3, g3, gates_all[3])
    w3_in = across(w3[slots:])
    b3 = onward(b2)
    e2 = take(2, b2)
    e2_in = across(e2[slots:])
    r1, w1 = join(e1, e1_in), join(w1, w1_in)
    n1, *k1 = expert(r1, w1)
    n1, b2, e2_in, w3_in = tie(n1, b2, e2_in, w3_in)
    n1_in = across(n1[slots:])
    n2_near, *s2 = shared(b2, far2)
    n2_near, b3, e2_in, n1_in, w3_in = tie(n2_near, b3, e2_in, n1_in, w3_in)
    ring1 = onward(spread_back(1, n1_near, n1, n1_in).astype(bf16))
    e3 = take(3, b3)
    e3_in = across(e3[slots:])
    r2, w2 = join(e2, e2_in), join(w2, w2_in)
    n2, *k2 = expert(r2, w2)
    n2, b3, e3_in = tie(n2, b3, e3_in)
    n2_in = across(n2[slots:])
    n3_near, *s3 = shared(b3, dot_last(g3, sd).astype(bf16))
    n3_near, e3_in, n2_in, ring1 = tie(n3_near, e3_in, n2_in, ring1)
    ring2 = onward(spread_back(2, n2_near, n2, n2_in, ring1).astype(bf16))
    r3, w3 = join(e3, e3_in), join(w3, w3_in)
    n3, *k3 = expert(r3, w3)
    n3, ring2 = tie(n3, ring2)
    n3_in = across(n3[slots:])
    s_act, s_gate_part, s_up_part = (
        jnp.concatenate(pieces, axis=0) for pieces in zip(s0, s1, s2, s3)
    )
    b_all = jnp.concatenate([b0, b1, b2, b3], axis=0)
    g_all = jnp.concatenate([g0, g1, g2, g3], axis=0)
    grad_s_cols = dot_first(b_all, jnp.concatenate([s_gate_part, s_up_part], axis=1)).astype(bf16)
    grad_s_cols, n3_in = tie(grad_s_cols, n3_in)
    ring3 = onward(spread_back(3, n3_near, n3, n3_in, ring2).astype(bf16))
    e_rows = jnp.concatenate([r0, r1, r2, r3], axis=0)
    e_grad = jnp.concatenate([w0, w1, w2, w3], axis=0)
    activated, gate_part, up_part = (
        jnp.concatenate(pieces, axis=0) for pieces in zip(k0, k1, k2, k3)
    )
    grad_e_gate = dot_first(e_rows, gate_part).astype(bf16)
    grad_e_up = dot_first(e_rows, up_part).astype(bf16)
    e_result = matmul(activated, expert_down[0]).astype(bf16).reshape(half, 2 * slots, width)
    grad_s_down = dot_first(s_act, g_all).astype(bf16)
    grad_e_gate, grad_e_up, ring3, activated, s_act, e_result, grad_s_down = tie(
        grad_e_gate, grad_e_up, ring3, activated, s_act, e_result, grad_s_down
    )
    grad_second = spread_back(0, n0_near, n0, n0_in, ring3)
    o_in = across(e_result[:, slots:])
    grad_e_down = dot_first(activated, e_grad).astype(bf16)

    def out_term(s, *more):
        weighed = (join(e_result[s], o_in[s]).astype(f32) * gates_all[s]).astype(bf16)
        total = matmul(s_act[s * tok_dev : (s + 1) * tok_dev], sd) + dot_first(
            pick_all[s], weighed
        )
        for other in more:
            total = total + other.astype(f32)
        return total

    grad_e_gate = lax.psum_scatter(grad_e_gate, "dp", scatter_dimension=0, tiled=True)
    grad_e_down_all, grad_s_down = grad_e_down, grad_s_down[:ff_own]

    def sum_columns(grads):
        return lax.psum_scatter(grads, "dp", scatter_dimension=0, tiled=True)

    grad_s_cols = sum_columns(grad_s_cols)

    def ff_restore(cut):
        both = cut[:, :, :ff_own].astype(f32).reshape(half, 2, rows_w, spread, 2 * ff_cut)
        return (both[:, 0] + both[:, 1]).transpose(1, 2, 0, 3).reshape(rows_w, -1)

    grad_f = grad_out.astype(f32)
    grad_resid_norm, grad_f_gain = second_norm_back(grad_second)
    grad_resid = grad_f + grad_resid_norm
    grad_attn_out = grad_resid.astype(bf16)
    grad_w_out = dot_first(attn_own, grad_attn_out).astype(bf16)
    grad_attended = dot_last(grad_attn_out, wo).astype(bf16)
    grad_heads = lax.all_to_all(grad_attended, "expert", split_axis=1, concat_axis=0, tiled=True)
    grad_heads, grad_w_out, grad_s_cols, grad_e_down, grad_s_down = tie(
        grad_heads,
        grad_w_out,
        grad_s_cols,
        grad_e_down_all,
        grad_s_down,
    )
    s_keep, s_other = line_swap(
        grad_s_down.reshape((2,) * (spread.bit_length() - 1) + (2, ff_cut, width)), 0
    )
    grad_s_cut = lax.all_to_all(
        grad_s_cols.reshape(group, rows_w, -1), "expert", split_axis=0, concat_axis=0, tiled=True
    )
    grad_w_out = lax.psum_scatter(grad_w_out, "dp", scatter_dimension=0, tiled=True)
    grad_q_lin, grad_kv, lat_part = attend_back(
        reach, q_att, k_att, v_att, grad_heads, attended, log_total, we, tables, scale
    )
    lat_part, grad_q_lin, o_in, grad_e_down, s_other = tie(
        lat_part, grad_q_lin, o_in, grad_e_down, s_other
    )
    ring1 = onward(out_term(1).astype(bf16))
    grad_s_down = both_halves(s_keep, s_other)
    for m in range(1, spread.bit_length() - 1):
        s_keep, s_other = line_swap(grad_s_down, m)
        if m < spread.bit_length() - 2:
            grad_s_down = both_halves(s_keep, s_other)
    (grad_lat_sum,) = reduce_rows([lat_part.reshape(group, tok_dev, -1)], 5, 2)
    grad_lat_sum, grad_q_lin, ring1, s_other, grad_w_out, grad_e_down, grad_e_up = tie(
        grad_lat_sum, grad_q_lin, ring1, s_other, grad_w_out, grad_e_down, grad_e_up
    )
    grad_s_down = both_halves(s_keep, s_other)
    own_side = rank % 2
    s_keep = lax.dynamic_index_in_dim(grad_s_down, own_side, 0, False)
    s_other = across(lax.dynamic_index_in_dim(grad_s_down, 1 - own_side, 0, False))
    ring2 = onward(out_term(2, ring1).astype(bf16))
    first_part = dot_last(grad_q_lin, wq).astype(bf16).reshape(group, tok_dev, width)
    steps = list(range(1, half)) + [0]
    w_blocks = grad_w_out.reshape(group, rows_w, width)
    w_in = across(jnp.stack([behind(w_blocks, s, 1) for s in steps]))

    def ring_term(blocks, arrived, k, *more):
        total = behind(blocks, steps[k], 0).astype(f32) + arrived[k].astype(f32)
        for other in more:
            total = total + other.astype(f32)
        return total

    def latent_parts(latent_in, gain_vec):
        return (
            norm_rows(latent_in[:, :KV], gain_vec),
            rotate(latent_in[:, KV : KV + ROPE], own_cos, own_sin),
        )

    unused, latent_back = jax.vjp(latent_parts, own(latent), l_gain)
    grad_latent, grad_l_gain = latent_back(
        (grad_lat_sum[:, :KV], grad_lat_sum[:, KV : KV + ROPE])
    )
    grad_latent = grad_latent.astype(bf16)
    grad_w_lat = dot_first(own(h1), grad_latent)[:, : KV + ROPE]
    grad_gains = jnp.stack(
        [
            grad_f_gain,
            jnp.pad(grad_l_gain.reshape(-1, rows_l), ((0, 0), (0, rows_w - rows_l))).reshape(width),
        ],
        axis=1,
    )
    lat_grads_in = jnp.concatenate(
        [grad_w_lat, jnp.pad(grad_gains, ((0, 0), (0, ROPE - 2)))], axis=1
    ).astype(bf16)
    first_part, lat_grads, w_in, grad_q_lin = tie(first_part, lat_grads_in, w_in, grad_q_lin)
    lat_grads = lax.psum_scatter(lat_grads, "dp", scatter_dimension=0, tiled=True)
    w_ring = onward(ring_term(w_blocks, w_in, 0).astype(bf16))
    grad_a_cols = jnp.concatenate(
        [dot_first(h1, grad_q_lin), dot_first(ckv, grad_kv).reshape(width, e_fold)], axis=1
    ).astype(bf16)
    first_part, grad_a_cols, w_ring = tie(first_part, grad_a_cols, w_ring)
    grad_a_cols = lax.psum_scatter(grad_a_cols, "dp", scatter_dimension=0, tiled=True)
    w_ring = onward(ring_term(w_blocks, w_in, 1, w_ring).astype(bf16))
    grad_e_up = lax.psum_scatter(grad_e_up, "dp", scatter_dimension=0, tiled=True)
    grad_e_down = lax.psum_scatter(grad_e_down, "dp", scatter_dimension=1, tiled=True)
    (first_sum,) = reduce_rows([first_part], 6, 4)
    (
        first_sum,
        lat_grads,
        ring2,
        w_ring,
        s_keep,
        s_other,
        grad_a_cols,
        grad_s_cut,
        grad_e_gate,
    ) = tie(
        first_sum,
        lat_grads,
        ring2,
        w_ring,
        s_keep,
        s_other,
        grad_a_cols,
        grad_s_cut,
        grad_e_gate,
    )
    w_ring = onward(ring_term(w_blocks, w_in, 2, w_ring).astype(bf16))
    lat_blocks = lat_grads.reshape(group, rows_w, -1)
    lat_in = across(jnp.stack([behind(lat_blocks, s, 1) for s in steps]))
    ring3 = onward(out_term(3, ring2).astype(bf16))
    grad_first = first_sum + dot_last(grad_latent[:, :lat_w], wl)
    unused, first_norm_back = jax.vjp(lambda v: norm_rows(v, a_gain), tokens_f)
    (grad_tokens_norm,) = first_norm_back(grad_first)
    grad_tokens = grad_resid + grad_tokens_norm
    grad_tokens, lat_in, w_ring = tie(grad_tokens, lat_in, w_ring)
    grad_w_out = ring_term(w_blocks, w_in, 3, w_ring)
    lat_ring = onward(ring_term(lat_blocks, lat_in, 0).astype(bf16))
    grad_s_gate = ff_restore(grad_s_cut[:, :, :ff_pad])
    grad_s_gate, grad_s_cut, lat_ring = tie(grad_s_gate, grad_s_cut, lat_ring)
    lat_ring = onward(ring_term(lat_blocks, lat_in, 1, lat_ring).astype(bf16))
    grad_s_up = ff_restore(grad_s_cut[:, :, ff_pad:])
    grad_s_up, lat_ring, ring3 = tie(grad_s_up, lat_ring, ring3)
    block_out = (resid + out_term(0, ring3)).astype(bf16)
    lat_ring = onward(ring_term(lat_blocks, lat_in, 2, lat_ring).astype(bf16))
    lat_grads = ring_term(lat_blocks, lat_in, 3, lat_ring)
    grad_s_down = s_keep.astype(f32) + s_other.astype(f32)
    grad_w_lat = lat_grads[:, :lat_w]
    grad_f_gain = lat_grads[:, lat_w]
    grad_l_gain = lat_grads[:rows_l, lat_w + 1]
    grad_a_cols = lax.all_to_all(
        grad_a_cols.reshape(group, rows_w, -1), "expert", split_axis=0, concat_axis=0, tiled=True
    )
    grad_w_q = (
        grad_a_cols[:, :, :q_own]
        .reshape(group, rows_w, mine, KEY)[..., : NOPE + ROPE]
        .transpose(1, 0, 2, 3)
        .reshape(rows_w, -1)
        .astype(f32)
    )
    grad_w_exp = (
        grad_a_cols[:, :, q_own:]
        .reshape(group, rows_l, e_own)
        .transpose(1, 0, 2)
        .reshape(rows_l, -1)
        .astype(f32)
    )
    grad_a_gain = (
        jnp.sum(grad_w_q * w_query.astype(f32), axis=1)
        + jnp.sum(grad_w_lat * w_latent.astype(f32), axis=1)
    ) / attn_gain.astype(f32)

    return (
        block_out,
        grad_tokens,
        grad_a_gain,
        grad_w_q,
        grad_w_lat,
        grad_l_gain,
        grad_w_exp,
        grad_w_out,
        grad_f_gain,
        grad_s_gate,
        grad_s_up,
        grad_s_down,
        grad_e_gate.astype(f32)[None],
        grad_e_up.astype(f32)[None],
        grad_e_down.astype(f32)[None],
    )


def solution(mesh):
    placed = (
        P(EVERY, None),
        P(EVERY, None),
        P(EVERY, None),
        P(EVERY, None),
        P("dp", None),
        P(EVERY),
        P(EVERY, None),
        P(EVERY, None),
        P(EVERY),
        P(EVERY, None),
        P(EVERY, None),
        P(EVERY),
        P(EVERY, None),
        P(EVERY, None),
        P(EVERY, None),
        P("expert", None, None),
        P("expert", None, None),
        P("expert", None, None),
    )
    return jax.shard_map(
        per_device,
        mesh=mesh,
        in_specs=placed,
        out_specs=(
            P(EVERY, None),
            P(EVERY, None),
            P(EVERY),
            P(EVERY, None),
            P(EVERY, None),
            P(EVERY),
            P(EVERY, None),
            P(EVERY, None),
            P(EVERY),
            P(EVERY, None),
            P(EVERY, None),
            P(EVERY, None),
            P("expert", "dp", None),
            P("expert", "dp", None),
            P("expert", None, "dp"),
        ),
        check_vma=False,
    )
```
